32 devices in a mesh: slab: 16 (over z, x, core), cross: 2 (over y).
Axes of the slice: x: 2, y: 2, z: 4, core: 2. Of those that a mesh axis runs over, the one named last changes fastest.
Arguments:
- sim_field: float32 [4, 1536, 4096], P(None, 'slab', 'cross'), may hold values from -6 to 6
- brick_edges: int32 [16, 2], P('slab'), may hold values from 0 to 1025, as said below
- cell_width: float32 [1024], P('slab'), may hold values from 0.5 to 2
Outputs:
- tile_detail: float32 [4, 960, 4096], P(None, 'slab', 'cross')
- tree_detail: float32 [4, 64, 4096], P(None, 'slab', 'cross')
- coarse_final: float32 [4, 5, 4096], P(None, None, 'cross')
The draws below stay inside these ranges and needn't reach their ends.
Inputs may be any that keep to these rules, and one draw needn't show every extreme that they name: Brick 0 starts at node 0; for s >= 1, brick_edges[s, 0] - 64 s lies between 1 and 16; each brick ends where the next starts and the last ends at 1025; some brick starts exactly 16 after its tile and another exactly 1 after.
All inputs are finite; a program needn't handle non-finite values.
Results may differ from the reference program's by a relative error of at most 0.00022.
Values sent between devices are 32-bit elements; how exact they have to be, the bound alone decides.
No kernel may reach another device: no remote copies, remote signals or barrier semaphores. Data moves between devices by JAX's collectives and lax.ppermute only.
A program may use at most 128 MiB of HBM per device.

```python
import math
import jax
import jax.numpy as jnp
from jax import lax

SPEC = 4
TILE = 64
HALO = 16
LEVELS = 4
CAPZ = 96
COARSE = 5
DETAILS = 60
NZ = 1024
TOTAL_LINES = 4096
LINE_BLOCK = 1024
N_SLAB = 16
N_CROSS = 2


def draw_brick_edges(key, part):
    first_key = jax.random.fold_in(key, 11)
    second_key = jax.random.fold_in(key, 23)
    third_key = jax.random.fold_in(key, 37)
    shifts = jax.random.randint(first_key, (N_SLAB + 1,), 1, HALO + 1, dtype=jnp.int32)
    high_place = jax.random.randint(second_key, (), 1, N_SLAB, dtype=jnp.int32)
    offset_step = jax.random.randint(third_key, (), 1, N_SLAB - 1, dtype=jnp.int32)
    low_place = 1 + (high_place - 1 + offset_step) % (N_SLAB - 1)
    shifts = shifts.at[0].set(0).at[high_place].set(HALO).at[low_place].set(1)
    starts = TILE * jnp.arange(N_SLAB + 1, dtype=jnp.int32) + shifts
    starts = starts.at[N_SLAB].set(TILE * N_SLAB + 1)
    return jnp.stack([starts[:-1], starts[1:]], axis=1).astype(jnp.int32)


def level_of(own_key, dims, pieces, least, high):
    def one(axis_at, shards_of):
        steps = jax.random.uniform(jax.random.fold_in(jax.random.fold_in(own_key, 6), axis_at), (shards_of,), jnp.float32, least / len(pieces), high / len(pieces))
        return jnp.repeat(jnp.exp(steps), dims[axis_at] // shards_of).reshape((-1,) + (1,) * (len(dims) - axis_at - 1))

    factor_of = one(*pieces[0])
    for cut in pieces[1:]:
        factor_of = factor_of * one(*cut)
    return factor_of


def scatter_about(rng, dims, spread, most, shards=(), held_as=jnp.bfloat16):
    drawn = spread * jax.random.normal(rng, dims, jnp.float32)
    if shards:
        drawn = drawn * level_of(rng, dims, shards, -0.22, 0.18)
    return jnp.clip(drawn, -most, most).astype(held_as)


def setup_inputs(seed: int = 0) -> dict:
    streams_of = jax.random.split(jax.random.key(seed), 4)
    return {
        "sim_field": scatter_about(streams_of[0], (SPEC, N_SLAB * CAPZ, TOTAL_LINES), 1.0, 6.0, ((1, 16), (2, 2)), jnp.float32),
        "brick_edges": draw_brick_edges(jax.random.fold_in(streams_of[3], 71), 0),
        "cell_width": jnp.clip(jnp.exp(math.log(2.0) - 1.3862944 * jax.random.uniform(streams_of[2], (NZ,), jnp.float32) ** level_of(streams_of[2], (NZ,), ((0, 16),), -0.2, 0.2)), 0.5, 2.0),
    }


def one_level(values, widths):
    left_width = widths[0::2]
    right_width = widths[1::2]
    coarse_width = left_width + right_width
    even_nodes = values[:, 0::2, :]
    odd_nodes = values[:, 1::2, :]
    details = odd_nodes - (right_width[:, None] * even_nodes[:, :-1, :] + left_width[:, None] * even_nodes[:, 1:, :]) / coarse_width[:, None]
    weight_after = left_width / 6.0 + right_width / 3.0
    before = right_width / 6.0 + left_width / 3.0
    zero_row = jnp.zeros_like(details[:, :1, :])
    load_vec = jnp.concatenate([weight_after[:, None] * details, zero_row], axis=1) + jnp.concatenate([zero_row, before[:, None] * details], axis=1)
    zero_width = jnp.zeros_like(coarse_width[:1])
    padded_width = jnp.concatenate([zero_width, coarse_width, zero_width])
    main_diag = (padded_width[:-1] + padded_width[1:]) / 3.0
    lower_diag = padded_width[:-1] / 6.0
    upper_diag = padded_width[1:] / 6.0
    identity = jnp.eye(main_diag.shape[0], dtype=values.dtype)
    inverse = lax.linalg.tridiagonal_solve(lower_diag, main_diag, upper_diag, identity)
    correction = jnp.einsum('kj,sjl->skl', inverse, load_vec, precision=lax.Precision.HIGHEST)
    return (even_nodes + correction, details, coarse_width)

def merge_sets(lower_values, lower_widths, upper_values, upper_widths):
    shared = 0.5 * (lower_values[:, -1:, :] + upper_values[:, :1, :])
    values = jnp.concatenate([lower_values[:, :-1, :], shared, upper_values[:, 1:, :]], axis=1)
    widths = jnp.concatenate([lower_widths, upper_widths])
    return one_level(values, widths)

def tree_all(all_values, all_widths):
    set_count = all_values.shape[0]
    tree_depth = set_count.bit_length() - 1
    stored = jnp.zeros((set_count, all_values.shape[1], all_values.shape[2] - 1, all_values.shape[3]), all_values.dtype)
    current_values = all_values
    current_widths = all_widths
    details = None
    for level_index in range(tree_depth):
        new_values, details, new_widths = jax.vmap(merge_sets)(current_values[0::2], current_widths[0::2], current_values[1::2], current_widths[1::2])
        stride_len = 2 ** level_index
        places = jnp.arange(current_values.shape[0] // 2, dtype=jnp.int32) * 2 * stride_len + stride_len
        stored = stored.at[places].set(details)
        current_values = new_values
        current_widths = new_widths
    stored = stored.at[0].set(details[0])
    return (stored, current_values[0])

def reference(sim_field, brick_edges, cell_width):
    relaid = sim_field.reshape(SPEC, N_SLAB * CAPZ, N_CROSS, N_CROSS, LINE_BLOCK)
    relaid = relaid.transpose(0, 1, 3, 2, 4).reshape(SPEC, N_SLAB * CAPZ, TOTAL_LINES)
    starts = brick_edges[:, 0]
    node_ids = jnp.arange(NZ + 1, dtype=jnp.int32)
    owner_ids = jnp.sum((node_ids[:, None] >= starts[None, :]).astype(jnp.int32), axis=1) - 1
    row_ids = (owner_ids * CAPZ + node_ids - starts[owner_ids]).astype(jnp.int32)
    line_field = jnp.take(relaid, row_ids, axis=1)
    tile_widths = cell_width.reshape(N_SLAB, TILE)

    def tile_work(tile_index):
        values = lax.dynamic_slice_in_dim(line_field, tile_index * TILE, TILE + 1, 1)
        widths = lax.dynamic_index_in_dim(tile_widths, tile_index, 0, keepdims=False)
        collected = []
        for level_index in range(LEVELS):
            values, details, widths = one_level(values, widths)
            collected.append(details)
        return (jnp.concatenate(collected, axis=1), values, widths)
    details_all, coarse_values, coarse_widths = lax.map(tile_work, jnp.arange(N_SLAB, dtype=jnp.int32))
    tile_detail = details_all.transpose(1, 0, 2, 3).reshape(SPEC, N_SLAB * DETAILS, TOTAL_LINES)
    stored, final_values = tree_all(coarse_values, coarse_widths)
    tree_detail = stored.transpose(1, 0, 2, 3).reshape(SPEC, N_SLAB * (COARSE - 1), TOTAL_LINES)
    return (tile_detail, tree_detail, final_values)
```

```python
import functools

import jax
import jax.numpy as jnp
from jax import lax
from jax.experimental import pallas as pl
from jax.experimental.pallas import tpu as pltpu
from jax.sharding import PartitionSpec as P

TILE = 64
HALO = 16
LEVELS = 4
COARSE = 5
DETAILS = TILE - COARSE + 1
LANES = 128
SUB = 8
F32 = jnp.float32
HIGHEST = lax.Precision.HIGHEST


def call(kernel, out_shape, **kw):
    params = pltpu.CompilerParams(vmem_limit_bytes=kw.pop("vmem", 24 << 20))
    return pl.pallas_call(kernel, out_shape=out_shape, compiler_params=params, **kw)


def vmem_spec():
    return pl.BlockSpec(memory_space=pltpu.VMEM)


def smem_spec():
    return pl.BlockSpec(memory_space=pltpu.SMEM)


def tail_kernel(edges, field, out, buf, sems):
    species = out.shape[0]
    low = TILE // 2
    copies = []
    for sp in range(species):
        copy = pltpu.make_async_copy(
            field.at[sp, pl.ds(low, TILE - HALO), :], buf.at[sp, pl.ds(0, TILE - HALO), :], sems.at[sp]
        )
        copy.start()
        copies.append(copy)
    start = edges[0, 1] - edges[0, 0] - HALO - low
    rest = start & (SUB - 1)
    whole = start - rest
    for sp in range(species):
        copies[sp].wait()
        rows = buf[sp, pl.ds(pl.multiple_of(whole, SUB), HALO + SUB), :]
        out[sp] = pltpu.roll(rows, (HALO + SUB - rest) % (HALO + SUB), 0)[:HALO]


def brick_tail(edges, field):
    species, _, lines = field.shape
    return call(
        tail_kernel,
        jax.ShapeDtypeStruct((species, HALO, lines), F32),
        in_specs=[smem_spec(), pl.BlockSpec(memory_space=pl.ANY)],
        out_specs=vmem_spec(),
        scratch_shapes=[
            pltpu.VMEM((species, TILE - HALO + SUB, lines), F32),
            pltpu.SemaphoreType.DMA((species,)),
        ],
    )(edges, field)


PAD = 32


def matrix_kernel(edges, widths, out, coarse_width, nodes, cell, low, main, up, load):
    slab = lax.axis_index("slab")
    shift = edges[0, 0] - slab * TILE
    rows = nodes.shape[0]
    node = lax.broadcasted_iota(jnp.int32, (rows, LANES), 0)
    column = lax.broadcasted_iota(jnp.int32, (rows, LANES), 1)
    held = column - HALO + shift
    held = jnp.where((slab == 0) & (column < HALO), column + TILE, held)
    nodes[...] = ((held == node) & (node <= TILE)).astype(F32)
    cell[...] = jnp.zeros_like(cell)
    cell[:TILE] = widths[...]
    for ref in (low, up, load):
        ref[...] = jnp.zeros_like(ref)
    main[...] = jnp.ones_like(main)
    out[...] = jnp.zeros_like(out)
    placed = 0
    pairs = TILE // 2
    for _ in range(LEVELS):
        size = -(-(pairs + 1) // SUB) * SUB
        here = pl.ds(PAD, size)
        inside = lax.broadcasted_iota(jnp.int32, (size, LANES), 0) < pairs
        left = cell[pl.ds(0, size, stride=2)]
        right = cell[pl.ds(1, size, stride=2)]
        total = left + right
        safe = jnp.where(inside, total, 1.0)
        even = nodes[pl.ds(0, size, stride=2)]
        odd = nodes[pl.ds(1, size, stride=2)]
        after = nodes[pl.ds(2, size, stride=2)]
        detail = jnp.where(inside, odd - (right * even + left * after) / safe, 0.0)
        out[placed : placed + pairs] = detail[:pairs]
        placed += pairs
        load[here] = (right / 6.0 + left / 3.0) * detail
        load[pl.ds(PAD - 1, 1)] = jnp.zeros((1, LANES), F32)
        grown = (left / 6.0 + right / 3.0) * detail + load[pl.ds(PAD - 1, size)]
        up[here] = total
        before = up[pl.ds(PAD - 1, size)]
        node_at = lax.broadcasted_iota(jnp.int32, (size, LANES), 0)
        diag = jnp.where(node_at <= pairs, (before + total) / 3.0, 1.0)
        lower = jnp.where(node_at <= pairs, before / 6.0, 0.0)
        upper = total / 6.0
        step = 1
        while step <= pairs:
            low[here] = lower
            up[here] = upper
            main[here] = diag
            load[here] = grown
            back = pl.ds(PAD - step, size)
            fore = pl.ds(PAD + step, size)
            alpha = -lower / main[back]
            gamma = -upper / main[fore]
            diag = diag + alpha * up[back] + gamma * low[fore]
            grown = grown + alpha * load[back] + gamma * load[fore]
            lower = alpha * low[back]
            upper = gamma * up[fore]
            step *= 2
        coarse = even + grown / diag
        coarse = jnp.where(node_at <= pairs, coarse, 0.0)
        nodes[...] = jnp.zeros_like(nodes)
        nodes[:size] = coarse
        cell[...] = jnp.zeros_like(cell)
        cell[:size] = total
        pairs //= 2
    out[pl.ds(TILE, SUB)] = nodes[:SUB]
    coarse_width[...] = cell[:SUB]


def tile_matrix(edges, cell_width):
    widths = jnp.broadcast_to(cell_width[:, None], (TILE, LANES))
    scratch = pltpu.VMEM((PAD + 40 + PAD, LANES), F32)
    return call(
        matrix_kernel,
        (
            jax.ShapeDtypeStruct((TILE + SUB, LANES), F32),
            jax.ShapeDtypeStruct((SUB, LANES), F32),
        ),
        in_specs=[smem_spec(), vmem_spec()],
        out_specs=(vmem_spec(), vmem_spec()),
        scratch_shapes=[pltpu.VMEM((88, LANES), F32), pltpu.VMEM((88, LANES), F32)] + [scratch] * 4,
    )(edges, widths)


def coarse_kernel(matrix, coarse_width, halo, field, sets, extra, turned):
    sp = pl.program_id(0)
    slab = lax.axis_index("slab")
    lines = halo.shape[2]
    dense = sets.shape[1]
    per = (lines // 2) // LANES
    node_rows = pl.num_programs(0) * per
    row = jnp.where(slab == 0, field[0, TILE : TILE + HALO], halo[0])
    extra[0] = row
    weights = matrix[pl.ds(TILE, SUB)]
    result = jnp.dot(weights[:, :HALO], row, precision=HIGHEST, preferred_element_type=F32)
    result += jnp.dot(weights[:, HALO : HALO + TILE], field[0, :TILE], precision=HIGHEST, preferred_element_type=F32)
    for t in range(lines // LANES):
        turned[t * SUB : (t + 1) * SUB] = result[:, t * LANES : (t + 1) * LANES]
    for half in range(2):
        for k in range(COARSE):
            at = pl.multiple_of(k * node_rows + sp * per, SUB)
            sets[half, pl.ds(at, per)] = turned[pl.ds(half * per * SUB + k, per, stride=SUB)]

    @pl.when(sp == 0)
    def _():
        for half in range(2):
            sets[half, dense - SUB :] = coarse_width[...]


def coarse_sets(matrix, coarse_width, halo, field):
    species, _, lines = field.shape
    node_rows = species * (lines // 2) // LANES
    dense = COARSE * node_rows + SUB
    rows = TILE + HALO
    return call(
        coarse_kernel,
        (
            jax.ShapeDtypeStruct((2, dense, LANES), F32),
            jax.ShapeDtypeStruct((species, HALO, lines), F32),
        ),
        grid=(species,),
        in_specs=[
            pl.BlockSpec((TILE + SUB, LANES), lambda i: (0, 0)),
            pl.BlockSpec((SUB, LANES), lambda i: (0, 0)),
            pl.BlockSpec((1, HALO, lines), lambda i: (i, 0, 0)),
            pl.BlockSpec((1, rows, lines), lambda i: (i, 0, 0)),
        ],
        out_specs=(
            pl.BlockSpec((2, dense, LANES), lambda i: (0, 0, 0)),
            pl.BlockSpec((1, HALO, lines), lambda i: (i, 0, 0)),
        ),
        scratch_shapes=[pltpu.VMEM((lines // LANES * SUB, LANES), F32)],
    )(matrix, coarse_width, halo, field)


def detail_kernel(place, matrix, extra, brick, *rest):
    out = rest[-1]
    weights = matrix[:TILE]
    result = jnp.dot(weights[:, :HALO], extra[0], precision=HIGHEST, preferred_element_type=F32)
    result += jnp.dot(weights[:, HALO : HALO + TILE], brick[0], precision=HIGHEST, preferred_element_type=F32)
    out[0] = result[:DETAILS]


def details(place, matrix, extra, brick, width, lines, onto=None):
    species = extra.shape[0]

    def at(own):
        return lambda i, place: (i, 0, place[0] if own else 0)

    specs = [
        pl.BlockSpec((TILE + SUB, LANES), lambda i, place: (0, 0)),
        pl.BlockSpec((1, HALO, width), at(extra.shape[2] != width)),
        pl.BlockSpec((1, TILE, width), at(brick.shape[2] != width)),
    ]
    operands = [place, matrix, extra, brick]
    alias = {}
    if onto is not None:
        specs.append(pl.BlockSpec(memory_space=pl.ANY))
        operands.append(onto)
        alias = {4: 0}
    return call(
        detail_kernel,
        jax.ShapeDtypeStruct((species, DETAILS, lines), F32),
        grid_spec=pltpu.PrefetchScalarGridSpec(
            num_scalar_prefetch=1,
            grid=(species,),
            in_specs=specs,
            out_specs=pl.BlockSpec((1, DETAILS, width), at(True)),
        ),
        input_output_aliases=alias,
    )(*operands)


def read_set(ref, node_rows):
    values = [ref[k * node_rows : (k + 1) * node_rows] for k in range(COARSE)]
    widths = [ref[COARSE * node_rows + i : COARSE * node_rows + i + 1] for i in range(COARSE - 1)]
    return values, widths


def merged(lower, upper):
    lower_values, lower_widths = lower
    upper_values, upper_widths = upper
    shared = 0.5 * (lower_values[-1] + upper_values[0])
    values = lower_values[:-1] + [shared] + upper_values[1:]
    widths = lower_widths + upper_widths
    left, right = widths[0::2], widths[1::2]
    pairs = len(left)
    total = [a + b for a, b in zip(left, right)]
    detail = []
    for i in range(pairs):
        inverse = 1.0 / total[i]
        detail.append(
            values[2 * i + 1] - ((right[i] * inverse) * values[2 * i] + (left[i] * inverse) * values[2 * i + 2])
        )
    loads = []
    for k in range(pairs + 1):
        term = None
        if k < pairs:
            term = (left[k] / 6.0 + right[k] / 3.0) * detail[k]
        if k > 0:
            other = (right[k - 1] / 6.0 + left[k - 1] / 3.0) * detail[k - 1]
            term = other if term is None else term + other
        loads.append(term)
    ratio, solved = [], []
    for k in range(pairs + 1):
        diag = (total[k - 1] if k else 0.0) + (total[k] if k < pairs else 0.0)
        diag = diag / 3.0
        if k:
            off = total[k - 1] / 6.0
            pivot = 1.0 / (diag - off * ratio[-1])
            solved.append((loads[k] - off * solved[-1]) * pivot)
        else:
            pivot = 1.0 / diag
            solved.append(loads[k] * pivot)
        if k < pairs:
            ratio.append(total[k] / 6.0 * pivot)
    for k in range(pairs - 1, -1, -1):
        solved[k] = solved[k] - ratio[k] * solved[k + 1]
    coarse = [values[2 * k] + solved[k] for k in range(pairs + 1)]
    return coarse, detail, total


def merge_kernel(level, depth, own, other, *refs):
    slab = lax.axis_index("slab")
    node_rows = (own.shape[-2] - SUB) // COARSE
    upper_side = (slab >> level) & 1 == 1
    mine, theirs = own, other
    if level == 0:
        mine = own.at[slab & 1]
    mine, theirs = read_set(mine, node_rows), read_set(theirs, node_rows)

    def pick(first, second):
        return [jnp.where(upper_side, a, b) for a, b in zip(first, second)]

    lower = (pick(theirs[0], mine[0]), pick(theirs[1], mine[1]))
    upper = (pick(mine[0], theirs[0]), pick(mine[1], theirs[1]))
    coarse, detail, widths = merged(lower, upper)
    last = level == depth - 1
    core = slab & 1
    if level == 0:
        out, odd_out = refs
        for i in range(COARSE - 1):
            odd_out[i * node_rows : (i + 1) * node_rows] = detail[i]
    else:
        kept = refs[0] if level > 1 else None
        chip = slab & ~1
        keep = ((chip >> level) & 1 == 1) & (chip & ((1 << level) - 1) == 0)
        if last:
            keep = keep | (chip == 0)
        even = []
        for i in range(COARSE - 1):
            old = kept[i * node_rows : (i + 1) * node_rows] if kept is not None else jnp.zeros_like(detail[i])
            even.append(jnp.where(keep, detail[i], old))
        if not last:
            out, even_out = refs[-2:]
            for i in range(COARSE - 1):
                even_out[i * node_rows : (i + 1) * node_rows] = even[i]
        else:
            odd_in = refs[1] if level > 1 else refs[0]
            here, away = refs[-2:]
            for k in range(COARSE):
                here[k * node_rows : (k + 1) * node_rows] = coarse[k]
                away[k * node_rows : (k + 1) * node_rows] = coarse[k]
            for i in range(COARSE - 1):
                odd = odd_in[i * node_rows : (i + 1) * node_rows]
                at = (COARSE + i) * node_rows
                here[at : at + node_rows] = jnp.where(core == 0, even[i], odd)
                away[at : at + node_rows] = jnp.where(core == 0, odd, even[i])
            return
    for k in range(COARSE):
        out[k * node_rows : (k + 1) * node_rows] = coarse[k]
    for i in range(COARSE - 1):
        out[COARSE * node_rows + i : COARSE * node_rows + i + 1] = widths[i]
    rest = COARSE * node_rows + COARSE - 1
    out[rest : rest + SUB - COARSE + 1] = jnp.zeros((SUB - COARSE + 1, LANES), F32)


def merge(level, depth, own, other, *kept):
    dense = own.shape[-2]
    node_rows = (dense - SUB) // COARSE
    stored = jax.ShapeDtypeStruct(((COARSE - 1) * node_rows, LANES), F32)
    if level == depth - 1:
        ended = jax.ShapeDtypeStruct(((2 * COARSE - 1) * node_rows, LANES), F32)
        shapes = (ended, ended)
    else:
        shapes = (jax.ShapeDtypeStruct((dense, LANES), F32), stored)
    operands = (own, other) + kept
    return call(
        functools.partial(merge_kernel, level, depth),
        shapes,
        in_specs=[vmem_spec()] * len(operands),
        out_specs=(vmem_spec(), vmem_spec()),
    )(*operands)


def finish_kernel(own, other, tree, final, turned):
    cross = lax.axis_index("cross")
    species, _, lines = tree.shape
    width = lines // 2
    per = width // LANES
    node_rows = species * per
    for block, ref in ((cross, own), (1 - cross, other)):
        for sp in range(species):
            for k in range(2 * COARSE - 1):
                at = k * node_rows + sp * per
                slot = k if k < COARSE else k - COARSE + SUB
                turned[pl.ds(slot, per, stride=2 * SUB)] = ref[at : at + per]
            for t in range(per):
                lanes = pl.ds(pl.multiple_of(block * width + t * LANES, LANES), LANES)
                final[sp, :, lanes] = turned[pl.ds(t * 2 * SUB, COARSE)]
                tree[sp, :, lanes] = turned[pl.ds(t * 2 * SUB + SUB, COARSE - 1)]


def finish(own, other, species, lines):
    return call(
        finish_kernel,
        (
            jax.ShapeDtypeStruct((species, COARSE - 1, lines), F32),
            jax.ShapeDtypeStruct((species, COARSE, lines), F32),
        ),
        in_specs=[vmem_spec(), vmem_spec()],
        out_specs=(vmem_spec(), vmem_spec()),
        scratch_shapes=[pltpu.VMEM((lines // 2 // LANES * 2 * SUB, LANES), F32)],
    )(own, other)


def from_partner(block, axis, step):
    count = lax.axis_size(axis)
    return lax.ppermute(block, axis, [(i, i ^ step) for i in range(count)])


def shifted(block, axis):
    count = lax.axis_size(axis)
    return lax.ppermute(block, axis, [(i, i + 1) for i in range(count - 1)])


def exchanged(block, axis):
    species, rows, lines = block.shape
    count = lax.axis_size(axis)
    parts = block.reshape(species, rows, count, lines // count)
    return lax.all_to_all(parts, axis, split_axis=2, concat_axis=2, tiled=True).reshape(block.shape)


def on_device(sim_field, brick_edges, cell_width):
    species, _, lines = sim_field.shape
    cross_count = lax.axis_size("cross")
    slab = lax.axis_index("slab")
    cross = lax.axis_index("cross")
    depth = lax.axis_size("slab").bit_length() - 1
    width = lines // cross_count
    swapped = cross_count == 2

    halo = shifted(brick_tail(brick_edges, sim_field), "slab")
    if swapped:
        away = lax.dynamic_slice(sim_field, (0, 0, (1 - cross) * width), (species, TILE, width))
        brick_in = from_partner(away, "cross", 1)
    matrix, coarse_width = tile_matrix(brick_edges, cell_width)
    sets, extra = coarse_sets(matrix, coarse_width, halo, sim_field)
    if swapped:
        extra_away = lax.dynamic_slice(extra, (0, 0, (1 - cross) * width), (species, HALO, width))
        extra_in = from_partner(extra_away, "cross", 1)
        here, there = cross.astype(jnp.int32).reshape(1), (1 - cross).astype(jnp.int32).reshape(1)

    current = sets
    sent = lax.dynamic_index_in_dim(sets, 1 - slab % 2, 0, keepdims=False)
    kept = ()
    odd = None
    for level in range(depth):
        other = from_partner(sent, "slab", 1 << level)
        if level == depth - 1:
            kept = kept + (odd,)
        current, stored = merge(level, depth, current, other, *kept)
        sent = current
        if level == 0:
            odd = stored
        else:
            kept = (stored,)
    here_set, away_set = current, stored
    partner_set = from_partner(away_set, "slab", 1)

    if swapped:
        core = slab % 2
        mine = jnp.where(core == cross, here_set, partner_set)
        theirs = jnp.where(core == cross, partner_set, here_set)
        arrived = from_partner(theirs, "cross", 1)
        tree_detail, coarse_final = finish(mine, arrived, species, lines)
        tile_detail = details(here, matrix, extra, sim_field, width, lines)
        tile_detail = details(there, matrix, extra_in, brick_in, width, lines, tile_detail)
    else:
        first = jnp.where(slab % 2 == 0, here_set, partner_set)
        second = jnp.where(slab % 2 == 0, partner_set, here_set)
        ended = jnp.stack([first, second]).reshape(2, 2 * COARSE - 1, species, lines // 2)
        ended = ended.transpose(2, 1, 0, 3).reshape(species, 2 * COARSE - 1, lines)
        ended = exchanged(ended, "cross")
        coarse_final, tree_detail = ended[:, :COARSE], ended[:, COARSE:]
        rows = exchanged(jnp.concatenate([extra, sim_field[:, :TILE]], axis=1), "cross")
        start = jnp.zeros((1,), jnp.int32)
        tile_detail = details(start, matrix, rows[:, :HALO], rows[:, HALO:], lines, lines)
    return (tile_detail, tree_detail, coarse_final)


def solution(mesh):
    placed = (P(None, "slab", "cross"), P("slab", None), P("slab"))
    return jax.shard_map(
        on_device,
        mesh=mesh,
        in_specs=placed,
        out_specs=(P(None, "slab", "cross"), P(None, "slab", "cross"), P(None, None, "cross")),
        check_vma=False,
    )
```

```python
import functools

import jax
import jax.numpy as jnp
from jax import lax
from jax.experimental import pallas as pl
from jax.experimental.pallas import tpu as pltpu
from jax.sharding import PartitionSpec as P

TILE = 64
HALO = 16
LEVELS = 4
COARSE = 5
DETAILS = TILE - COARSE + 1
LANES = 128
SUB = 8
HELD = TILE + HALO
FIRST = 48
SECOND = TILE - FIRST
F32 = jnp.float32
BF16 = jnp.bfloat16
HIGHEST = lax.Precision.HIGHEST


def call(kernel, out_shape, *, vmem=8 << 20, cost=None, **kw):
    params = pltpu.CompilerParams(vmem_limit_bytes=vmem)
    if cost is not None:
        kw["cost_estimate"] = pl.CostEstimate(flops=cost, bytes_accessed=cost // 100, transcendentals=0)
    return pl.pallas_call(kernel, out_shape=out_shape, compiler_params=params, **kw)


VMEM_SPEC = pl.BlockSpec(memory_space=pltpu.VMEM)
SMEM_SPEC = pl.BlockSpec(memory_space=pltpu.SMEM)
HBM_SPEC = pl.BlockSpec(memory_space=pltpu.HBM)


def leave_kernel(edges, field, tail, *away):
    species, _, lines = tail.shape
    start = edges[0, 1] - edges[0, 0] - HALO
    rest = start & (SUB - 1)
    whole = pl.multiple_of(start - rest, SUB)
    for sp in range(species):
        rows = field[sp, pl.ds(whole, HALO + SUB), :]
        tail[sp] = pltpu.roll(rows, (HALO + SUB - rest) % (HALO + SUB), 0)[:HALO]
    for out in away:
        width = out.shape[2]
        other = pl.multiple_of((1 - lax.axis_index("cross")) * width, LANES)
        for sp in range(species):
            out[sp] = field[sp, :FIRST, pl.ds(other, width)]


def leaving(edges, field, width):
    species, _, lines = field.shape
    shapes = [jax.ShapeDtypeStruct((species, HALO, lines), F32)]
    if width < lines:
        shapes.append(jax.ShapeDtypeStruct((species, FIRST, width), F32))
    return call(
        leave_kernel,
        tuple(shapes),
        in_specs=[SMEM_SPEC, VMEM_SPEC],
        out_specs=(VMEM_SPEC,) * len(shapes),
    )(edges, field)


PAD = 32


def matrix_kernel(edges, widths, factors, coarse, coarse_width, nodes, cell, low, main, up, load, stored):
    slab = lax.axis_index("slab")
    shift = edges[0, 0] - slab * TILE
    rows, lanes = nodes.shape[1], nodes.shape[0] * LANES
    node = lax.broadcasted_iota(jnp.int32, (rows, lanes), 0)
    lane = lax.broadcasted_iota(jnp.int32, (rows, lanes), 1)
    column = lane % HELD
    later = column - FIRST
    held = jnp.where(column < FIRST, column + shift, jnp.where(later < shift, later, column))
    plain = lane - 2 * LANES
    from_halo = jnp.where((slab == 0) & (plain < HALO), plain + TILE, plain - HALO + shift)
    grouped = (lane < 3 * HELD) & (column <= TILE)
    held = jnp.where(lane < 2 * LANES, jnp.where(grouped, held, -1), jnp.where(plain < HELD, from_halo, -1))
    chosen = ((held == node) & (node <= TILE)).astype(F32)
    for j in range(lanes // LANES):
        nodes[j] = chosen[:, j * LANES : (j + 1) * LANES]
    cell[...] = jnp.zeros_like(cell)
    cell[:TILE] = widths[...]
    for ref in (low, up, load):
        ref[...] = jnp.zeros_like(ref)
    main[...] = jnp.ones_like(main)
    stored[...] = jnp.zeros_like(stored)
    wide = lambda x: jnp.concatenate([x] * (lanes // LANES), axis=1)
    placed = 0
    pairs = TILE // 2
    for _ in range(LEVELS):
        size = -(-(pairs + 1) // SUB) * SUB
        here = pl.ds(PAD, size)
        inside = lax.broadcasted_iota(jnp.int32, (size, LANES), 0) < pairs
        left = cell[pl.ds(0, size, stride=2)]
        right = cell[pl.ds(1, size, stride=2)]
        total = left + right
        safe = jnp.where(inside, total, 1.0)
        even, odd, after = [
            jnp.concatenate([nodes[j, pl.ds(i, size, stride=2)] for j in range(lanes // LANES)], axis=1)
            for i in range(3)
        ]
        inverse = 1.0 / safe
        detail = odd - (wide(right * inverse) * even + wide(left * inverse) * after)
        detail = jnp.where(wide(inside), detail, 0.0)
        stored[placed : placed + pairs] = detail[:pairs]
        placed += pairs
        load[here] = wide(right / 6.0 + left / 3.0) * detail
        load[pl.ds(PAD - 1, 1)] = jnp.zeros((1, lanes), F32)
        grown = wide(left / 6.0 + right / 3.0) * detail + load[pl.ds(PAD - 1, size)]
        up[here] = total
        before = up[pl.ds(PAD - 1, size)]
        held_rows = lax.broadcasted_iota(jnp.int32, (size, LANES), 0) <= pairs
        diag = jnp.where(held_rows, (before + total) / 3.0, 1.0)
        lower = jnp.where(held_rows, before / 6.0, 0.0)
        upper = total / 6.0
        step = 1
        while step <= pairs:
            low[here] = lower
            up[here] = upper
            main[here] = 1.0 / diag
            load[here] = grown
            back = pl.ds(PAD - step, size)
            fore = pl.ds(PAD + step, size)
            alpha = -lower * main[back]
            gamma = -upper * main[fore]
            diag = diag + alpha * up[back] + gamma * low[fore]
            grown = grown + wide(alpha) * load[back] + wide(gamma) * load[fore]
            lower = alpha * low[back]
            upper = gamma * up[fore]
            step *= 2
        result = even + grown * wide(1.0 / diag)
        result = jnp.where(wide(held_rows), result, 0.0)
        nodes[...] = jnp.zeros_like(nodes)
        for j in range(lanes // LANES):
            nodes[j, :size] = result[:, j * LANES : (j + 1) * LANES]
        cell[...] = jnp.zeros_like(cell)
        cell[:size] = total
        pairs //= 2
    coarse[...] = nodes[2, :SUB]
    coarse_width[...] = cell[:SUB]
    matrix = stored[:, : 2 * LANES]
    lane = lax.broadcasted_iota(jnp.int32, matrix.shape, 1)
    for i in range(3):
        term = matrix.astype(BF16)
        matrix = matrix - term.astype(F32)
        factors[i * TILE : (i + 1) * TILE] = jnp.where(lane < (3 - i) * HELD, term.astype(F32), 0.0).astype(BF16)


def tile_matrix(edges, cell_width):
    widths = jnp.broadcast_to(cell_width[:, None], (TILE, LANES))
    narrow = pltpu.VMEM((PAD + 40 + PAD, LANES), F32)
    broad = pltpu.VMEM((PAD + 40 + PAD, 3 * LANES), F32)
    return call(
        matrix_kernel,
        (
            jax.ShapeDtypeStruct((3 * TILE, 2 * LANES), BF16),
            jax.ShapeDtypeStruct((SUB, LANES), F32),
            jax.ShapeDtypeStruct((SUB, LANES), F32),
        ),
        in_specs=[SMEM_SPEC, VMEM_SPEC],
        out_specs=(VMEM_SPEC,) * 3,
        scratch_shapes=[
            pltpu.VMEM((3, 88, LANES), F32),
            pltpu.VMEM((88, LANES), F32),
            narrow,
            narrow,
            narrow,
            broad,
            pltpu.VMEM((TILE, 3 * LANES), F32),
        ],
    )(edges, widths)


def to_dense(result, turned, sets, sp, species):
    blocks = result.shape[1] // LANES
    per = blocks // 2
    for t in range(blocks):
        turned[t * SUB : (t + 1) * SUB] = result[:, t * LANES : (t + 1) * LANES]
    for half in range(2):
        for k in range(COARSE):
            at = ((half * COARSE + k) * species + sp) * per
            sets[pl.ds(at if isinstance(sp, int) else pl.multiple_of(at, per), per)] = turned[
                pl.ds(half * per * SUB + k, per, stride=SUB)
            ]


def brick_kernel(weights, coarse_width, field, sets, turned):
    sp = pl.program_id(0)
    slab = lax.axis_index("slab")
    own = weights[...]
    result = jnp.dot(own[:, HALO:HELD], field[0, :TILE], precision=HIGHEST, preferred_element_type=F32)
    row = jnp.where(slab == 0, field[0, TILE:HELD], 0.0)
    result += jnp.dot(own[:, :HALO], row, precision=HIGHEST, preferred_element_type=F32)
    to_dense(result, turned, sets, sp, pl.num_programs(0))

    @pl.when(sp == 0)
    def _():
        sets[sets.shape[0] - SUB :] = coarse_width[...]


def brick_part(weights, coarse_width, field):
    species, _, lines = field.shape
    dense = COARSE * species * lines // LANES + SUB
    return call(
        brick_kernel,
        jax.ShapeDtypeStruct((dense, LANES), F32),
        grid=(species,),
        in_specs=[
            pl.BlockSpec((SUB, LANES), lambda i: (0, 0)),
            pl.BlockSpec((SUB, LANES), lambda i: (0, 0)),
            pl.BlockSpec((1, HELD, lines), lambda i: (i, 0, 0)),
        ],
        out_specs=pl.BlockSpec((dense, LANES), lambda i: (0, 0)),
        scratch_shapes=[pltpu.VMEM((lines // LANES * SUB, LANES), F32)],
    )(weights, coarse_width, field)


def halo_kernel(weights, halo, part, own_half, other_half, turned, fresh):
    species = halo.shape[0]
    slab = lax.axis_index("slab")
    own = weights[:, :HALO]
    for sp in range(species):
        result = jnp.dot(own, halo[sp], precision=HIGHEST, preferred_element_type=F32)
        to_dense(result, turned, fresh, sp, species)
    rows = fresh.shape[0] // 2
    for ref, half in ((own_half, slab & 1), (other_half, 1 - (slab & 1))):
        here = pl.ds(pl.multiple_of(half * rows, SUB), rows)
        ref[:rows] = part[here] + jnp.where(slab == 0, 0.0, fresh[here])
        ref[rows:] = part[2 * rows :]


def coarse_sets(weights, halo, part):
    lines = halo.shape[2]
    rows = part.shape[0] - SUB
    half = jax.ShapeDtypeStruct((rows // 2 + SUB, LANES), F32)
    return call(
        halo_kernel,
        (half, half),
        in_specs=[VMEM_SPEC] * 3,
        out_specs=(VMEM_SPEC,) * 2,
        scratch_shapes=[
            pltpu.VMEM((lines // LANES * SUB, LANES), F32),
            pltpu.VMEM((rows, LANES), F32),
        ],
    )(weights, halo, part)


def later_nodes(shift, halo, brick):
    rows = jnp.concatenate([halo, brick], axis=0)
    count = rows.shape[0]
    return pltpu.roll(rows, (count - HALO + shift) % count, 0)


BRICK_END = TILE + SUB


def rest_kernel(edges, halo, field, out):
    species = halo.shape[0]
    shift = edges[0, 0] - lax.axis_index("slab") * TILE
    width = out.shape[1]
    other = pl.ds(pl.multiple_of((1 - lax.axis_index("cross")) * width, LANES), width)
    last = species * SECOND
    out[last:] = jnp.zeros((out.shape[0] - last, width), F32)
    for sp in range(species):
        rows = later_nodes(shift, halo[sp, :, other], field[sp, FIRST:BRICK_END, other])
        out[sp * SECOND : (sp + 1) * SECOND] = rows[:SECOND]
        out[last + sp : last + sp + 1] = rows[SECOND : SECOND + 1]


def rest_away(edges, halo, field, width):
    species = halo.shape[0]
    rows = species * SECOND + -(-species // SUB) * SUB
    return call(
        rest_kernel,
        jax.ShapeDtypeStruct((rows, width), F32),
        in_specs=[SMEM_SPEC, VMEM_SPEC, VMEM_SPEC],
        out_specs=VMEM_SPEC,
        cost=400_000_000,
    )(edges, halo, field)


def detail_kernel(local, place, factors, first, second, *rest):
    out, wide = rest[-2:]
    species = out.shape[1]
    width = out.shape[2]
    weights = factors[:, : 3 * HELD]
    for sp in range(species):
        if local:
            more = later_nodes(place[1], first[sp], second[sp, FIRST:BRICK_END])
            pieces = [second[sp, :FIRST], more[: SECOND + HALO]]
        else:
            last = species * SECOND
            end = pltpu.roll(second[last : last + SUB], (SUB - sp) % SUB, 0)
            pieces = [first[sp], second[sp * SECOND : (sp + 1) * SECOND], end, end]
        left = jnp.concatenate(pieces, axis=0)
        terms = []
        for _ in range(3):
            terms.append(left.astype(BF16))
            left = left - terms[-1].astype(F32)
        stack = jnp.concatenate(terms, axis=0)
        result = jnp.dot(weights, stack, preferred_element_type=F32)
        result = result[:TILE] + result[TILE : 2 * TILE] + result[2 * TILE :]
        for t in range(width // LANES):
            wide[t, pl.ds(sp, TILE, stride=species)] = result[:, t * LANES : (t + 1) * LANES]
    for t in range(width // LANES):
        for k in range(DETAILS):
            out[k, :, t * LANES : (t + 1) * LANES] = wide[t, k * species : (k + 1) * species]


def details(local, place, factors, first, second, width, species, lines, onto=None):
    chunk = min(width, 512)
    steps = width // chunk

    def at(own, i, place):
        return place[0] * steps + i if own else i

    whole = first.shape[2] == lines
    if local:
        specs = [
            pl.BlockSpec((species, HALO, chunk), lambda i, place: (0, 0, at(whole, i, place))),
            pl.BlockSpec((species, HELD, chunk), lambda i, place: (0, 0, at(whole, i, place))),
        ]
    else:
        specs = [
            pl.BlockSpec((species, FIRST, chunk), lambda i, place: (0, 0, i)),
            pl.BlockSpec((second.shape[0], chunk), lambda i, place: (0, i)),
        ]
    specs = [pl.BlockSpec((3 * TILE, 2 * LANES), lambda i, place: (0, 0))] + specs
    operands = [place, factors, first, second]
    alias = {}
    if onto is not None:
        specs.append(HBM_SPEC)
        operands.append(onto)
        alias = {4: 0}
    return call(
        functools.partial(detail_kernel, local),
        jax.ShapeDtypeStruct((DETAILS, species, lines), F32),
        grid_spec=pltpu.PrefetchScalarGridSpec(
            num_scalar_prefetch=1,
            grid=(steps,),
            in_specs=specs,
            out_specs=pl.BlockSpec((DETAILS, species, chunk), lambda i, place: (0, 0, at(True, i, place))),
            scratch_shapes=[pltpu.VMEM((chunk // LANES, TILE * species, LANES), F32)],
        ),
        input_output_aliases=alias,
        cost=2_000_000_000,
    )(*operands)


def merged(lower, upper):
    lower_values, lower_widths = lower
    upper_values, upper_widths = upper
    shared = 0.5 * (lower_values[-1] + upper_values[0])
    values = lower_values[:-1] + [shared] + upper_values[1:]
    widths = lower_widths + upper_widths
    left, right = widths[0::2], widths[1::2]
    pairs = len(left)
    total = [a + b for a, b in zip(left, right)]
    detail = []
    for i in range(pairs):
        inverse = 1.0 / total[i]
        detail.append(
            values[2 * i + 1] - ((right[i] * inverse) * values[2 * i] + (left[i] * inverse) * values[2 * i + 2])
        )
    loads = []
    for k in range(pairs + 1):
        term = None
        if k < pairs:
            term = (left[k] / 6.0 + right[k] / 3.0) * detail[k]
        if k > 0:
            other = (right[k - 1] / 6.0 + left[k - 1] / 3.0) * detail[k - 1]
            term = other if term is None else term + other
        loads.append(term)
    ratio, solved = [], []
    for k in range(pairs + 1):
        diag = (total[k - 1] if k else 0.0) + (total[k] if k < pairs else 0.0)
        diag = diag / 3.0
        if k:
            off = total[k - 1] / 6.0
            pivot = 1.0 / (diag - off * ratio[-1])
            solved.append((loads[k] - off * solved[-1]) * pivot)
        else:
            pivot = 1.0 / diag
            solved.append(loads[k] * pivot)
        if k < pairs:
            ratio.append(total[k] / 6.0 * pivot)
    for k in range(pairs - 1, -1, -1):
        solved[k] = solved[k] - ratio[k] * solved[k + 1]
    coarse = [values[2 * k] + solved[k] for k in range(pairs + 1)]
    return coarse, detail, total


def values_at(ref, first, rows):
    return [ref[pl.ds(first + k * rows, rows)] for k in range(COARSE)]


def widths_at(ref, first):
    return [ref[pl.ds(first + i, 1)] for i in range(COARSE - 1)]


def put(ref, first, rows, values):
    for k, value in enumerate(values):
        ref[pl.ds(first + k * rows, rows)] = value


def put_widths(ref, first, widths):
    put(ref, first, 1, widths)
    ref[first + COARSE - 1 : first + SUB] = jnp.zeros((SUB - COARSE + 1, LANES), F32)


def in_order(upper_side, mine, theirs):
    def pick(first, second):
        return [jnp.where(upper_side, a, b) for a, b in zip(first, second)]

    lower = (pick(theirs[0], mine[0]), pick(theirs[1], mine[1]))
    upper = (pick(mine[0], theirs[0]), pick(mine[1], theirs[1]))
    return merged(lower, upper)


def merge_kernel(level, depth, rows, swapped, *refs):
    slab = lax.axis_index("slab")
    core = slab & 1
    chip = slab & ~1
    upper_side = (slab >> level) & 1 == 1
    last = level == depth - 1
    set_rows = COARSE * rows + SUB
    detail_rows = (COARSE - 1) * rows
    own, other = refs[0], refs[1]
    outs = refs[-2:]

    def state(ref):
        values = values_at(ref, 0, rows) + widths_at(ref, COARSE * rows)
        if level > 0:
            values += [ref[pl.ds(set_rows + i * rows, rows)] for i in range(COARSE - 1)]
        if level > 1:
            values += [ref[pl.ds(set_rows + detail_rows + i * rows, rows)] for i in range(COARSE - 1)]
        return values

    held = state(own)
    if swapped and last:
        home = core == lax.axis_index("cross")
        held = [jnp.where(home, a, b) for a, b in zip(held, state(refs[2]))]
    mine = (held[:COARSE], held[COARSE : 2 * COARSE - 1])
    odd = held[2 * COARSE - 1 : 3 * COARSE - 2]
    even = held[3 * COARSE - 2 :]
    theirs = (values_at(other, 0, rows), widths_at(other, COARSE * rows))

    def pick(first, second):
        return [jnp.where(upper_side, a, b) for a, b in zip(first, second)]

    lower = (pick(theirs[0], mine[0]), pick(theirs[1], mine[1]))
    upper = (pick(mine[0], theirs[0]), pick(mine[1], theirs[1]))
    coarse, detail, widths = merged(lower, upper)
    if level == 0:
        odd = detail
    else:
        keep = ((chip >> level) & 1 == 1) & (chip & ((1 << level) - 1) == 0)
        if last:
            keep = keep | (chip == 0)
        even = even if level > 1 else [0.0] * (COARSE - 1)
        even = [jnp.where(keep, a, b) for a, b in zip(detail, even)]
    if last:
        here, away = outs
        put(here, 0, rows, coarse)
        put(away, 0, rows, coarse)
        put(here, COARSE * rows, rows, [jnp.where(core == 0, a, b) for a, b in zip(even, odd)])
        put(away, COARSE * rows, rows, [jnp.where(core == 0, b, a) for a, b in zip(even, odd)])
        return
    send, carried = outs
    for ref in (send, carried):
        put(ref, 0, rows, coarse)
        put_widths(ref, COARSE * rows, widths)
    put(carried, set_rows, rows, odd)
    if level > 0:
        put(carried, set_rows + detail_rows, rows, even)


def merge(level, depth, rows, swapped, *operands):
    set_rows = COARSE * rows + SUB
    detail_rows = (COARSE - 1) * rows
    if level == depth - 1:
        sizes = ((2 * COARSE - 1) * rows,) * 2
    else:
        sizes = (set_rows, set_rows + min(level + 1, 2) * detail_rows)
    return call(
        functools.partial(merge_kernel, level, depth, rows, swapped),
        tuple(jax.ShapeDtypeStruct((size, LANES), F32) for size in sizes),
        in_specs=[VMEM_SPEC] * len(operands),
        out_specs=(VMEM_SPEC,) * 2,
    )(*operands)


def finish_kernel(own, other, tree, final, turned):
    core = lax.axis_index("slab") & 1
    species, _, lines = tree.shape
    width = lines // 2
    per = width // LANES
    group = COARSE - 1
    for block, ref in ((core, own), (1 - core, other)):

        def lanes(t):
            return pl.ds(pl.multiple_of(block * width + t * LANES, LANES), LANES)

        for k in range(COARSE):
            for sp in range(species):
                turned[pl.ds(sp, per, stride=species)] = ref[(k * species + sp) * per : (k * species + sp + 1) * per]
            for t in range(per):
                final[k, :, lanes(t)] = turned[t * species : (t + 1) * species]
        for sp in range(species):
            for i in range(group):
                at = ((COARSE + i) * species + sp) * per
                turned[pl.ds(i, per, stride=group)] = ref[at : at + per]
            for t in range(per):
                tree[sp, :, lanes(t)] = turned[t * group : (t + 1) * group]


def finish(own, other, species, lines):
    return call(
        finish_kernel,
        (
            jax.ShapeDtypeStruct((species, COARSE - 1, lines), F32),
            jax.ShapeDtypeStruct((COARSE, species, lines), F32),
        ),
        in_specs=[VMEM_SPEC] * 2,
        out_specs=(VMEM_SPEC,) * 2,
        scratch_shapes=[pltpu.VMEM((lines // 2 // LANES * SUB, LANES), F32)],
    )(own, other)


def from_partner(block, axis, step):
    count = lax.axis_size(axis)
    return lax.ppermute(block, axis, [(i, i ^ step) for i in range(count)])


def shifted(block, axis):
    count = lax.axis_size(axis)
    return lax.ppermute(block, axis, [(i, i + 1) for i in range(count - 1)])


def exchanged(block, axis):
    species, rows, lines = block.shape
    count = lax.axis_size(axis)
    parts = block.reshape(species, rows, count, lines // count)
    return lax.all_to_all(parts, axis, split_axis=2, concat_axis=2, tiled=True).reshape(block.shape)


def last_routes(slabs):
    partner, own = [], []
    for s in range(slabs):
        for c in range(2):
            home = (s & 1) == c
            target = (s, c) if home else (s ^ 1, 1 - c)
            partner.append((s * 2 + c, (target[0] ^ (slabs // 2)) * 2 + target[1]))
            if not home:
                own.append((s * 2 + c, target[0] * 2 + target[1]))
    return partner, own


def on_device(sim_field, brick_edges, cell_width):
    species, _, lines = sim_field.shape
    cross_count = lax.axis_size("cross")
    slabs = lax.axis_size("slab")
    cross = lax.axis_index("cross")
    core = lax.axis_index("slab") % 2
    depth = slabs.bit_length() - 1
    width = lines // cross_count
    rows = species * (lines // 2) // LANES
    swapped = cross_count == 2
    both = ("slab", "cross")

    if swapped:
        tail, first_away = leaving(brick_edges, sim_field, width)
        first_in = from_partner(first_away, "cross", 1)
    else:
        (tail,) = leaving(brick_edges, sim_field, lines)
    halo = shifted(tail, "slab")
    factors, weights, coarse_width = tile_matrix(brick_edges, cell_width)
    part = brick_part(weights, coarse_width, sim_field)
    halo, part, factors = lax.optimization_barrier((halo, part, factors))
    own_half, other_half = coarse_sets(weights, halo, part)
    shift = brick_edges[0, 0] - lax.axis_index("slab") * TILE
    if swapped:
        rest_in = from_partner(rest_away(brick_edges, halo, sim_field, width), "cross", 1)

    send, carried = other_half, own_half
    for level in range(depth):
        if swapped and level == depth - 1:
            partner_route, own_route = last_routes(slabs)
            send, carried, rest_in = lax.optimization_barrier((send, carried, rest_in))
            operands = (carried, lax.ppermute(send, both, partner_route), lax.ppermute(carried, both, own_route))
        else:
            operands = (carried, from_partner(send, "slab", 1 << level))
        send, carried = merge(level, depth, rows, swapped, *operands)
    here_set, away_set = send, carried
    partner_set = from_partner(away_set, "slab", 1)

    if swapped:
        tree_detail, coarse_final = finish(here_set, partner_set, species, lines)
        coarse_final = coarse_final.transpose(1, 0, 2)
        here, there = jnp.stack([cross, shift]), jnp.stack([1 - cross, shift])
        tile_detail = details(True, here, factors, halo, sim_field, width, species, lines)
        tile_detail = details(False, there, factors, first_in, rest_in, width, species, lines, tile_detail)
    else:
        first = jnp.where(core == 0, here_set, partner_set)
        second = jnp.where(core == 0, partner_set, here_set)
        ended = jnp.stack([first, second]).reshape(2, 2 * COARSE - 1, species, lines // 2)
        ended = ended.transpose(2, 1, 0, 3).reshape(species, 2 * COARSE - 1, lines)
        ended = exchanged(ended, "cross")
        coarse_final, tree_detail = ended[:, :COARSE], ended[:, COARSE:]
        moved = exchanged(jnp.concatenate([halo, sim_field[:, :HELD]], axis=1), "cross")
        place = jnp.stack([jnp.zeros_like(shift), shift])
        tile_detail = details(True, place, factors, moved[:, :HALO], moved[:, HALO:], lines, species, lines)
    return (tile_detail.transpose(1, 0, 2), tree_detail, coarse_final)


def solution(mesh):
    placed = (P(None, "slab", "cross"), P("slab", None), P("slab"))
    return jax.shard_map(
        on_device,
        mesh=mesh,
        in_specs=placed,
        out_specs=(P(None, "slab", "cross"), P(None, "slab", "cross"), P(None, None, "cross")),
        check_vma=False,
    )
```

```python
import functools

import jax
import jax.numpy as jnp
from jax import lax
from jax.experimental import pallas as pl
from jax.experimental.pallas import tpu as pltpu
from jax.sharding import PartitionSpec as P

TILE = 64
HALO = 16
LEVELS = 4
COARSE = 5
DETAILS = TILE - COARSE + 1
LANES = 128
SUB = 8
HELD = TILE + HALO
FIRST = 48
SECOND = TILE - FIRST
F32 = jnp.float32
BF16 = jnp.bfloat16
HIGHEST = lax.Precision.HIGHEST


def call(kernel, out_shape, *, vmem=8 << 20, cost=None, **kw):
    params = pltpu.CompilerParams(vmem_limit_bytes=vmem)
    if cost is not None:
        kw["cost_estimate"] = pl.CostEstimate(flops=cost, bytes_accessed=cost // 100, transcendentals=0)
    return pl.pallas_call(kernel, out_shape=out_shape, compiler_params=params, **kw)


VMEM_SPEC = pl.BlockSpec(memory_space=pltpu.VMEM)
SMEM_SPEC = pl.BlockSpec(memory_space=pltpu.SMEM)
HBM_SPEC = pl.BlockSpec(memory_space=pltpu.HBM)


def leave_kernel(edges, field, tail, *refs):
    species, _, lines = tail.shape
    buf, sems = refs[-2:]
    away = refs[0] if len(refs) > 2 else None
    copies = []
    if away is not None:
        width = away.shape[2]
        other = pl.ds(pl.multiple_of((1 - lax.axis_index("cross")) * width, LANES), width)
    start = edges[0, 1] - edges[0, 0] - HALO
    rest = start & (SUB - 1)
    whole = pl.multiple_of(start - rest, SUB)
    window = []
    for sp in range(species):
        window.append(pltpu.make_async_copy(field.at[sp, pl.ds(whole, HALO + SUB), :], buf.at[sp], sems.at[0, sp]))
        window[-1].start()
    for sp in range(species if away is not None else 0):
        copies.append(pltpu.make_async_copy(field.at[sp, pl.ds(0, FIRST), other], away.at[sp], sems.at[1, sp]))
        copies[-1].start()
    for sp in range(species):
        window[sp].wait()
        tail[sp] = pltpu.roll(buf[sp], (HALO + SUB - rest) % (HALO + SUB), 0)[:HALO]
    for copy in copies:
        copy.wait()


def leaving(edges, field, width):
    species, _, lines = field.shape
    shapes = [jax.ShapeDtypeStruct((species, HALO, lines), F32)]
    if width < lines:
        shapes.append(jax.ShapeDtypeStruct((species, FIRST, width), F32))
    return call(
        leave_kernel,
        tuple(shapes),
        in_specs=[SMEM_SPEC, HBM_SPEC],
        out_specs=(VMEM_SPEC,) * len(shapes),
        scratch_shapes=[pltpu.VMEM((species, HALO + SUB, lines), F32), pltpu.SemaphoreType.DMA((2, species))],
        vmem=62 << 20,
    )(edges, field)


PAD = 32


def matrix_kernel(edges, widths, factors, coarse, coarse_width, nodes, cell, low, main, up, load, stored):
    slab = lax.axis_index("slab")
    shift = edges[0, 0] - slab * TILE
    rows, lanes = nodes.shape[1], nodes.shape[0] * LANES
    node = lax.broadcasted_iota(jnp.int32, (rows, lanes), 0)
    lane = lax.broadcasted_iota(jnp.int32, (rows, lanes), 1)
    column = lane % HELD
    later = column - FIRST
    held = jnp.where(column < FIRST, column + shift, jnp.where(later < shift, later, column))
    plain = lane - 2 * LANES
    from_halo = jnp.where((slab == 0) & (plain < HALO), plain + TILE, plain - HALO + shift)
    grouped = (lane < 3 * HELD) & (column <= TILE)
    held = jnp.where(lane < 2 * LANES, jnp.where(grouped, held, -1), jnp.where(plain < HELD, from_halo, -1))
    chosen = ((held == node) & (node <= TILE)).astype(F32)
    for j in range(lanes // LANES):
        nodes[j] = chosen[:, j * LANES : (j + 1) * LANES]
    cell[...] = jnp.zeros_like(cell)
    cell[:TILE] = widths[...]
    for ref in (low, up, load):
        ref[...] = jnp.zeros_like(ref)
    main[...] = jnp.ones_like(main)
    stored[...] = jnp.zeros_like(stored)
    wide = lambda x: jnp.concatenate([x] * (lanes // LANES), axis=1)
    placed = 0
    pairs = TILE // 2
    for _ in range(LEVELS):
        size = -(-(pairs + 1) // SUB) * SUB
        here = pl.ds(PAD, size)
        inside = lax.broadcasted_iota(jnp.int32, (size, LANES), 0) < pairs
        left = cell[pl.ds(0, size, stride=2)]
        right = cell[pl.ds(1, size, stride=2)]
        total = left + right
        safe = jnp.where(inside, total, 1.0)
        even, odd, after = [
            jnp.concatenate([nodes[j, pl.ds(i, size, stride=2)] for j in range(lanes // LANES)], axis=1)
            for i in range(3)
        ]
        inverse = 1.0 / safe
        detail = odd - (wide(right * inverse) * even + wide(left * inverse) * after)
        detail = jnp.where(wide(inside), detail, 0.0)
        stored[placed : placed + pairs] = detail[:pairs]
        placed += pairs
        load[here] = wide(right / 6.0 + left / 3.0) * detail
        load[pl.ds(PAD - 1, 1)] = jnp.zeros((1, lanes), F32)
        grown = wide(left / 6.0 + right / 3.0) * detail + load[pl.ds(PAD - 1, size)]
        up[here] = total
        before = up[pl.ds(PAD - 1, size)]
        held_rows = lax.broadcasted_iota(jnp.int32, (size, LANES), 0) <= pairs
        diag = jnp.where(held_rows, (before + total) / 3.0, 1.0)
        lower = jnp.where(held_rows, before / 6.0, 0.0)
        upper = total / 6.0
        step = 1
        while step <= pairs:
            low[here] = lower
            up[here] = upper
            main[here] = 1.0 / diag
            load[here] = grown
            back = pl.ds(PAD - step, size)
            fore = pl.ds(PAD + step, size)
            alpha = -lower * main[back]
            gamma = -upper * main[fore]
            diag = diag + alpha * up[back] + gamma * low[fore]
            grown = grown + wide(alpha) * load[back] + wide(gamma) * load[fore]
            lower = alpha * low[back]
            upper = gamma * up[fore]
            step *= 2
        result = even + grown * wide(1.0 / diag)
        result = jnp.where(wide(held_rows), result, 0.0)
        nodes[...] = jnp.zeros_like(nodes)
        for j in range(lanes // LANES):
            nodes[j, :size] = result[:, j * LANES : (j + 1) * LANES]
        cell[...] = jnp.zeros_like(cell)
        cell[:size] = total
        pairs //= 2
    coarse[...] = nodes[2, :SUB]
    coarse_width[...] = cell[:SUB]
    matrix = stored[:, : 2 * LANES]
    lane = lax.broadcasted_iota(jnp.int32, matrix.shape, 1)
    for i in range(3):
        term = matrix.astype(BF16)
        matrix = matrix - term.astype(F32)
        factors[i * TILE : (i + 1) * TILE] = jnp.where(lane < (3 - i) * HELD, term.astype(F32), 0.0).astype(BF16)


def tile_matrix(edges, cell_width):
    widths = jnp.broadcast_to(cell_width[:, None], (TILE, LANES))
    narrow = pltpu.VMEM((PAD + 40 + PAD, LANES), F32)
    broad = pltpu.VMEM((PAD + 40 + PAD, 3 * LANES), F32)
    return call(
        matrix_kernel,
        (
            jax.ShapeDtypeStruct((3 * TILE, 2 * LANES), BF16),
            jax.ShapeDtypeStruct((SUB, LANES), F32),
            jax.ShapeDtypeStruct((SUB, LANES), F32),
        ),
        in_specs=[SMEM_SPEC, VMEM_SPEC],
        out_specs=(VMEM_SPEC,) * 3,
        scratch_shapes=[
            pltpu.VMEM((3, 88, LANES), F32),
            pltpu.VMEM((88, LANES), F32),
            narrow,
            narrow,
            narrow,
            broad,
            pltpu.VMEM((TILE, 3 * LANES), F32),
        ],
    )(edges, widths)


def to_dense(result, turned, sets, sp, species):
    blocks = result.shape[1] // LANES
    per = blocks // 2
    for t in range(blocks):
        turned[t * SUB : (t + 1) * SUB] = result[:, t * LANES : (t + 1) * LANES]
    for half in range(2):
        for k in range(COARSE):
            at = ((half * COARSE + k) * species + sp) * per
            sets[pl.ds(at if isinstance(sp, int) else pl.multiple_of(at, per), per)] = turned[
                pl.ds(half * per * SUB + k, per, stride=SUB)
            ]


def brick_kernel(weights, coarse_width, field, sets, turned):
    sp = pl.program_id(0)
    slab = lax.axis_index("slab")
    own = weights[...]
    result = jnp.dot(own[:, HALO:HELD], field[0, :TILE], precision=HIGHEST, preferred_element_type=F32)
    row = jnp.where(slab == 0, field[0, TILE:HELD], 0.0)
    result += jnp.dot(own[:, :HALO], row, precision=HIGHEST, preferred_element_type=F32)
    to_dense(result, turned, sets, sp, pl.num_programs(0))

    @pl.when(sp == 0)
    def _():
        sets[sets.shape[0] - SUB :] = coarse_width[...]


def brick_part(weights, coarse_width, field):
    species, _, lines = field.shape
    dense = COARSE * species * lines // LANES + SUB
    return call(
        brick_kernel,
        jax.ShapeDtypeStruct((dense, LANES), F32),
        grid=(species,),
        in_specs=[
            pl.BlockSpec((SUB, LANES), lambda i: (0, 0)),
            pl.BlockSpec((SUB, LANES), lambda i: (0, 0)),
            pl.BlockSpec((1, HELD, lines), lambda i: (i, 0, 0)),
        ],
        out_specs=pl.BlockSpec((dense, LANES), lambda i: (0, 0)),
        scratch_shapes=[pltpu.VMEM((lines // LANES * SUB, LANES), F32)],
    )(weights, coarse_width, field)


def halo_kernel(weights, halo, part, own_half, other_half, turned, fresh):
    species = halo.shape[0]
    slab = lax.axis_index("slab")
    own = weights[:, :HALO]
    for sp in range(species):
        result = jnp.dot(own, halo[sp], precision=HIGHEST, preferred_element_type=F32)
        to_dense(result, turned, fresh, sp, species)
    rows = fresh.shape[0] // 2
    for ref, half in ((own_half, slab & 1), (other_half, 1 - (slab & 1))):
        here = pl.ds(pl.multiple_of(half * rows, SUB), rows)
        ref[:rows] = part[here] + jnp.where(slab == 0, 0.0, fresh[here])
        ref[rows:] = part[2 * rows :]


def coarse_sets(weights, halo, part):
    lines = halo.shape[2]
    rows = part.shape[0] - SUB
    half = jax.ShapeDtypeStruct((rows // 2 + SUB, LANES), F32)
    return call(
        halo_kernel,
        (half, half),
        in_specs=[VMEM_SPEC] * 3,
        out_specs=(VMEM_SPEC,) * 2,
        scratch_shapes=[
            pltpu.VMEM((lines // LANES * SUB, LANES), F32),
            pltpu.VMEM((rows, LANES), F32),
        ],
    )(weights, halo, part)


def later_nodes(shift, halo, brick):
    rows = jnp.concatenate([halo, brick], axis=0)
    count = rows.shape[0]
    return pltpu.roll(rows, (count - HALO + shift) % count, 0)


BRICK_END = TILE + SUB


def rest_kernel(edges, halo, field, out):
    species = halo.shape[0]
    shift = edges[0, 0] - lax.axis_index("slab") * TILE
    width = out.shape[1]
    other = pl.ds(pl.multiple_of((1 - lax.axis_index("cross")) * width, LANES), width)
    last = species * SECOND
    out[last:] = jnp.zeros((out.shape[0] - last, width), F32)
    for sp in range(species):
        rows = later_nodes(shift, halo[sp, :, other], field[sp, FIRST:BRICK_END, other])
        out[sp * SECOND : (sp + 1) * SECOND] = rows[:SECOND]
        out[last + sp : last + sp + 1] = rows[SECOND : SECOND + 1]


def rest_away(edges, halo, field, width):
    species = halo.shape[0]
    rows = species * SECOND + -(-species // SUB) * SUB
    return call(
        rest_kernel,
        jax.ShapeDtypeStruct((rows, width), F32),
        in_specs=[SMEM_SPEC, VMEM_SPEC, VMEM_SPEC],
        out_specs=VMEM_SPEC,
        cost=400_000_000,
    )(edges, halo, field)


def detail_kernel(local, edges, factors, first, second, *rest):
    out, wide = rest[-2:]
    species = out.shape[1]
    width = out.shape[2]
    weights = factors[:, : 3 * HELD]
    shift = edges[0, 0] - lax.axis_index("slab") * TILE
    for sp in range(species):
        if local:
            more = later_nodes(shift, first[sp], second[sp, FIRST:BRICK_END])
            pieces = [second[sp, :FIRST], more[: SECOND + HALO]]
        else:
            last = species * SECOND
            end = pltpu.roll(second[last : last + SUB], (SUB - sp) % SUB, 0)
            pieces = [first[sp], second[sp * SECOND : (sp + 1) * SECOND], end, end]
        left = jnp.concatenate(pieces, axis=0)
        terms = []
        for _ in range(3):
            terms.append(left.astype(BF16))
            left = left - terms[-1].astype(F32)
        stack = jnp.concatenate(terms, axis=0)
        result = jnp.dot(weights, stack, preferred_element_type=F32)
        result = result[:TILE] + result[TILE : 2 * TILE] + result[2 * TILE :]
        for t in range(width // LANES):
            wide[t, pl.ds(sp, TILE, stride=species)] = result[:, t * LANES : (t + 1) * LANES]
    for t in range(width // LANES):
        for k in range(DETAILS):
            out[k, :, t * LANES : (t + 1) * LANES] = wide[t, k * species : (k + 1) * species]


def details(local, edges, factors, first, second, width, species, lines, onto=None):
    chunk = min(width, 512)
    steps = width // chunk

    def here(i):
        return i if width == lines else lax.axis_index("cross") * steps + i

    def there(i):
        return (1 - lax.axis_index("cross")) * steps + i

    if local:
        specs = [
            pl.BlockSpec((species, HALO, chunk), lambda i: (0, 0, here(i))),
            pl.BlockSpec((species, HELD, chunk), lambda i: (0, 0, here(i))),
        ]
    else:
        specs = [
            pl.BlockSpec((species, FIRST, chunk), lambda i: (0, 0, i)),
            pl.BlockSpec((second.shape[0], chunk), lambda i: (0, i)),
        ]
    specs = [SMEM_SPEC, pl.BlockSpec((3 * TILE, 2 * LANES), lambda i: (0, 0))] + specs
    operands = [edges, factors, first, second]
    alias = {}
    if onto is not None:
        specs.append(HBM_SPEC)
        operands.append(onto)
        alias = {4: 0}
    return call(
        functools.partial(detail_kernel, local),
        jax.ShapeDtypeStruct((DETAILS, species, lines), F32),
        grid=(steps,),
        in_specs=specs,
        out_specs=pl.BlockSpec((DETAILS, species, chunk), lambda i: (0, 0, here(i) if local else there(i))),
        scratch_shapes=[pltpu.VMEM((chunk // LANES, TILE * species, LANES), F32)],
        input_output_aliases=alias,
        cost=2_000_000_000,
    )(*operands)


def merged(lower, upper):
    lower_values, lower_widths = lower
    upper_values, upper_widths = upper
    shared = 0.5 * (lower_values[-1] + upper_values[0])
    values = lower_values[:-1] + [shared] + upper_values[1:]
    widths = lower_widths + upper_widths
    left, right = widths[0::2], widths[1::2]
    pairs = len(left)
    total = [a + b for a, b in zip(left, right)]
    detail = []
    for i in range(pairs):
        inverse = 1.0 / total[i]
        detail.append(
            values[2 * i + 1] - ((right[i] * inverse) * values[2 * i] + (left[i] * inverse) * values[2 * i + 2])
        )
    loads = []
    for k in range(pairs + 1):
        term = None
        if k < pairs:
            term = (left[k] / 6.0 + right[k] / 3.0) * detail[k]
        if k > 0:
            other = (right[k - 1] / 6.0 + left[k - 1] / 3.0) * detail[k - 1]
            term = other if term is None else term + other
        loads.append(term)
    ratio, solved = [], []
    for k in range(pairs + 1):
        diag = (total[k - 1] if k else 0.0) + (total[k] if k < pairs else 0.0)
        diag = diag / 3.0
        if k:
            off = total[k - 1] / 6.0
            pivot = 1.0 / (diag - off * ratio[-1])
            solved.append((loads[k] - off * solved[-1]) * pivot)
        else:
            pivot = 1.0 / diag
            solved.append(loads[k] * pivot)
        if k < pairs:
            ratio.append(total[k] / 6.0 * pivot)
    for k in range(pairs - 1, -1, -1):
        solved[k] = solved[k] - ratio[k] * solved[k + 1]
    coarse = [values[2 * k] + solved[k] for k in range(pairs + 1)]
    return coarse, detail, total


def values_at(ref, first, rows):
    return [ref[pl.ds(first + k * rows, rows)] for k in range(COARSE)]


def widths_at(ref, first):
    return [ref[pl.ds(first + i, 1)] for i in range(COARSE - 1)]


def put(ref, first, rows, values):
    for k, value in enumerate(values):
        ref[pl.ds(first + k * rows, rows)] = value


def put_widths(ref, first, widths):
    put(ref, first, 1, widths)
    ref[first + COARSE - 1 : first + SUB] = jnp.zeros((SUB - COARSE + 1, LANES), F32)


def in_order(upper_side, mine, theirs):
    def pick(first, second):
        return [jnp.where(upper_side, a, b) for a, b in zip(first, second)]

    lower = (pick(theirs[0], mine[0]), pick(theirs[1], mine[1]))
    upper = (pick(mine[0], theirs[0]), pick(mine[1], theirs[1]))
    return merged(lower, upper)


def merge_kernel(level, depth, rows, swapped, *refs):
    slab = lax.axis_index("slab")
    core = slab & 1
    chip = slab & ~1
    upper_side = (slab >> level) & 1 == 1
    last = level == depth - 1
    set_rows = COARSE * rows + SUB
    detail_rows = (COARSE - 1) * rows
    own, other = refs[0], refs[1]
    outs = refs[-2:]

    def state(ref):
        values = values_at(ref, 0, rows) + widths_at(ref, COARSE * rows)
        if level > 0:
            values += [ref[pl.ds(set_rows + i * rows, rows)] for i in range(COARSE - 1)]
        if level > 1:
            values += [ref[pl.ds(set_rows + detail_rows + i * rows, rows)] for i in range(COARSE - 1)]
        return values

    held = state(own)
    if swapped and last:
        home = core == lax.axis_index("cross")
        held = [jnp.where(home, a, b) for a, b in zip(held, state(refs[2]))]
    mine = (held[:COARSE], held[COARSE : 2 * COARSE - 1])
    odd = held[2 * COARSE - 1 : 3 * COARSE - 2]
    even = held[3 * COARSE - 2 :]
    theirs = (values_at(other, 0, rows), widths_at(other, COARSE * rows))

    def pick(first, second):
        return [jnp.where(upper_side, a, b) for a, b in zip(first, second)]

    lower = (pick(theirs[0], mine[0]), pick(theirs[1], mine[1]))
    upper = (pick(mine[0], theirs[0]), pick(mine[1], theirs[1]))
    coarse, detail, widths = merged(lower, upper)
    if level == 0:
        odd = detail
    else:
        keep = ((chip >> level) & 1 == 1) & (chip & ((1 << level) - 1) == 0)
        if last:
            keep = keep | (chip == 0)
        even = even if level > 1 else [0.0] * (COARSE - 1)
        even = [jnp.where(keep, a, b) for a, b in zip(detail, even)]
    if last:
        here, away = outs
        put(here, 0, rows, coarse)
        put(away, 0, rows, coarse)
        put(here, COARSE * rows, rows, [jnp.where(core == 0, a, b) for a, b in zip(even, odd)])
        put(away, COARSE * rows, rows, [jnp.where(core == 0, b, a) for a, b in zip(even, odd)])
        return
    send, carried = outs
    for ref in (send, carried):
        put(ref, 0, rows, coarse)
        put_widths(ref, COARSE * rows, widths)
    put(carried, set_rows, rows, odd)
    if level > 0:
        put(carried, set_rows + detail_rows, rows, even)


def merge(level, depth, rows, swapped, *operands):
    set_rows = COARSE * rows + SUB
    detail_rows = (COARSE - 1) * rows
    if level == depth - 1:
        sizes = ((2 * COARSE - 1) * rows,) * 2
    else:
        sizes = (set_rows, set_rows + min(level + 1, 2) * detail_rows)
    return call(
        functools.partial(merge_kernel, level, depth, rows, swapped),
        tuple(jax.ShapeDtypeStruct((size, LANES), F32) for size in sizes),
        in_specs=[VMEM_SPEC] * len(operands),
        out_specs=(VMEM_SPEC,) * 2,
    )(*operands)


def finish_kernel(own, other, tree, final, turned):
    core = lax.axis_index("slab") & 1
    species, _, lines = tree.shape
    width = lines // 2
    per = width // LANES
    group = COARSE - 1
    for block, ref in ((core, own), (1 - core, other)):

        def lanes(t):
            return pl.ds(pl.multiple_of(block * width + t * LANES, LANES), LANES)

        for k in range(COARSE):
            for sp in range(species):
                turned[pl.ds(sp, per, stride=species)] = ref[(k * species + sp) * per : (k * species + sp + 1) * per]
            for t in range(per):
                final[k, :, lanes(t)] = turned[t * species : (t + 1) * species]
        for sp in range(species):
            for i in range(group):
                at = ((COARSE + i) * species + sp) * per
                turned[pl.ds(i, per, stride=group)] = ref[at : at + per]
            for t in range(per):
                tree[sp, :, lanes(t)] = turned[t * group : (t + 1) * group]


def finish(own, other, species, lines):
    return call(
        finish_kernel,
        (
            jax.ShapeDtypeStruct((species, COARSE - 1, lines), F32),
            jax.ShapeDtypeStruct((COARSE, species, lines), F32),
        ),
        in_specs=[VMEM_SPEC] * 2,
        out_specs=(VMEM_SPEC,) * 2,
        scratch_shapes=[pltpu.VMEM((lines // 2 // LANES * SUB, LANES), F32)],
    )(own, other)


def from_partner(block, axis, step):
    count = lax.axis_size(axis)
    return lax.ppermute(block, axis, [(i, i ^ step) for i in range(count)])


def shifted(block, axis):
    count = lax.axis_size(axis)
    return lax.ppermute(block, axis, [(i, i + 1) for i in range(count - 1)])


def exchanged(block, axis):
    species, rows, lines = block.shape
    count = lax.axis_size(axis)
    parts = block.reshape(species, rows, count, lines // count)
    return lax.all_to_all(parts, axis, split_axis=2, concat_axis=2, tiled=True).reshape(block.shape)


def last_routes(slabs):
    partner, own = [], []
    for s in range(slabs):
        for c in range(2):
            home = (s & 1) == c
            target = (s, c) if home else (s ^ 1, 1 - c)
            partner.append((s * 2 + c, (target[0] ^ (slabs // 2)) * 2 + target[1]))
            if not home:
                own.append((s * 2 + c, target[0] * 2 + target[1]))
    return partner, own


def on_device(sim_field, brick_edges, cell_width):
    species, _, lines = sim_field.shape
    cross_count = lax.axis_size("cross")
    slabs = lax.axis_size("slab")
    depth = slabs.bit_length() - 1
    width = lines // cross_count
    rows = species * (lines // 2) // LANES
    swapped = cross_count == 2
    both = ("slab", "cross")

    field = sim_field
    tail, *away = leaving(brick_edges, field, width)
    if swapped:
        first_in = from_partner(away[0], "cross", 1)
    halo = shifted(tail, "slab")
    factors, weights, coarse_width = tile_matrix(brick_edges, cell_width)
    part = brick_part(weights, coarse_width, field)
    halo, part, factors = lax.optimization_barrier((halo, part, factors))
    own_half, other_half = coarse_sets(weights, halo, part)
    halo, other_half = lax.optimization_barrier((halo, other_half))
    if swapped:
        rest_in = from_partner(rest_away(brick_edges, halo, field, width), "cross", 1)

    send, carried = other_half, own_half
    for level in range(depth):
        if swapped and level == depth - 1:
            partner_route, own_route = last_routes(slabs)
            operands = (carried, lax.ppermute(send, both, partner_route), lax.ppermute(carried, both, own_route))
            operands, rest_in = lax.optimization_barrier((operands, rest_in))
        else:
            operands = (carried, from_partner(send, "slab", 1 << level))
        send, carried = merge(level, depth, rows, swapped, *operands)
    here_set, away_set = send, carried
    partner_set = from_partner(away_set, "slab", 1)

    if swapped:
        tree_detail, coarse_final = finish(here_set, partner_set, species, lines)
        coarse_final = coarse_final.transpose(1, 0, 2)
        tile_detail = details(True, brick_edges, factors, halo, field, width, species, lines)
        tile_detail = details(False, brick_edges, factors, first_in, rest_in, width, species, lines, tile_detail)
    else:
        core = lax.axis_index("slab") % 2
        first = jnp.where(core == 0, here_set, partner_set)
        second = jnp.where(core == 0, partner_set, here_set)
        ended = jnp.stack([first, second]).reshape(2, 2 * COARSE - 1, species, lines // 2)
        ended = ended.transpose(2, 1, 0, 3).reshape(species, 2 * COARSE - 1, lines)
        ended = exchanged(ended, "cross")
        coarse_final, tree_detail = ended[:, :COARSE], ended[:, COARSE:]
        moved = exchanged(jnp.concatenate([halo, sim_field[:, :HELD]], axis=1), "cross")
        tile_detail = details(True, brick_edges, factors, moved[:, :HALO], moved[:, HALO:], lines, species, lines)
    return (tile_detail.transpose(1, 0, 2), tree_detail, coarse_final)


def solution(mesh):
    placed = (P(None, "slab", "cross"), P("slab", None), P("slab"))
    return jax.shard_map(
        on_device,
        mesh=mesh,
        in_specs=placed,
        out_specs=(P(None, "slab", "cross"), P(None, "slab", "cross"), P(None, None, "cross")),
        check_vma=False,
    )
```

```python
import functools

import jax
import jax.numpy as jnp
from jax import lax
from jax.experimental import pallas as pl
from jax.experimental.pallas import tpu as pltpu
from jax.sharding import PartitionSpec as P

TILE = 64
HALO = 16
LEVELS = 4
COARSE = 5
DETAILS = TILE - COARSE + 1
LANES = 128
SUB = 8
HELD = TILE + HALO
FIRST = 48
SECOND = TILE - FIRST
F32 = jnp.float32
BF16 = jnp.bfloat16
HIGHEST = lax.Precision.HIGHEST


def call(kernel, out_shape, *, vmem=8 << 20, cost=None, **kw):
    params = pltpu.CompilerParams(vmem_limit_bytes=vmem)
    if cost is not None:
        kw["cost_estimate"] = pl.CostEstimate(flops=cost, bytes_accessed=cost // 100, transcendentals=0)
    return pl.pallas_call(kernel, out_shape=out_shape, compiler_params=params, **kw)


VMEM_SPEC = pl.BlockSpec(memory_space=pltpu.VMEM)
SMEM_SPEC = pl.BlockSpec(memory_space=pltpu.SMEM)
HBM_SPEC = pl.BlockSpec(memory_space=pltpu.HBM)


def leave_kernel(edges, field, tail, *aways):
    species = tail.shape[0]
    for away in aways:
        width = away.shape[2]
        other = pl.ds(pl.multiple_of((1 - lax.axis_index("cross")) * width, LANES), width)
        for sp in range(species):
            away[sp] = field[sp, :FIRST, other]
    start = edges[0, 1] - edges[0, 0] - HALO
    rest = start & (SUB - 1)
    whole = pl.multiple_of(start - rest, SUB)
    for sp in range(species):
        rows = field[sp, pl.ds(whole, HALO + SUB), :]
        tail[sp] = pltpu.roll(rows, (HALO + SUB - rest) % (HALO + SUB), 0)[:HALO]


def leaving(edges, field, width):
    species, _, lines = field.shape
    shapes = [jax.ShapeDtypeStruct((species, HALO, lines), F32)]
    if width < lines:
        shapes.append(jax.ShapeDtypeStruct((species, FIRST, width), F32))
    return call(
        leave_kernel,
        tuple(shapes),
        in_specs=[SMEM_SPEC, VMEM_SPEC],
        out_specs=(VMEM_SPEC,) * len(shapes),
    )(edges, field)


PAD = 32


def matrix_kernel(edges, widths, factors, coarse, coarse_width, nodes, cell, low, main, up, load, stored):
    slab = lax.axis_index("slab")
    shift = edges[0, 0] - slab * TILE
    rows, lanes = nodes.shape[1], nodes.shape[0] * LANES
    node = lax.broadcasted_iota(jnp.int32, (rows, lanes), 0)
    lane = lax.broadcasted_iota(jnp.int32, (rows, lanes), 1)
    column = lane % HELD
    later = column - FIRST
    held = jnp.where(column < FIRST, column + shift, jnp.where(later < shift, later, column))
    plain = lane - 2 * LANES
    from_halo = jnp.where((slab == 0) & (plain < HALO), plain + TILE, plain - HALO + shift)
    grouped = (lane < 3 * HELD) & (column <= TILE)
    held = jnp.where(lane < 2 * LANES, jnp.where(grouped, held, -1), jnp.where(plain < HELD, from_halo, -1))
    chosen = ((held == node) & (node <= TILE)).astype(F32)
    for j in range(lanes // LANES):
        nodes[j] = chosen[:, j * LANES : (j + 1) * LANES]
    cell[...] = jnp.zeros_like(cell)
    cell[:TILE] = widths[...]
    for ref in (low, up, load):
        ref[...] = jnp.zeros_like(ref)
    main[...] = jnp.ones_like(main)
    stored[...] = jnp.zeros_like(stored)
    wide = lambda x: jnp.concatenate([x] * (lanes // LANES), axis=1)
    placed = 0
    pairs = TILE // 2
    for _ in range(LEVELS):
        size = -(-(pairs + 1) // SUB) * SUB
        here = pl.ds(PAD, size)
        inside = lax.broadcasted_iota(jnp.int32, (size, LANES), 0) < pairs
        left = cell[pl.ds(0, size, stride=2)]
        right = cell[pl.ds(1, size, stride=2)]
        total = left + right
        safe = jnp.where(inside, total, 1.0)
        even, odd, after = [
            jnp.concatenate([nodes[j, pl.ds(i, size, stride=2)] for j in range(lanes // LANES)], axis=1)
            for i in range(3)
        ]
        inverse = 1.0 / safe
        detail = odd - (wide(right * inverse) * even + wide(left * inverse) * after)
        detail = jnp.where(wide(inside), detail, 0.0)
        stored[placed : placed + pairs] = detail[:pairs]
        placed += pairs
        load[here] = wide(right / 6.0 + left / 3.0) * detail
        load[pl.ds(PAD - 1, 1)] = jnp.zeros((1, lanes), F32)
        grown = wide(left / 6.0 + right / 3.0) * detail + load[pl.ds(PAD - 1, size)]
        up[here] = total
        before = up[pl.ds(PAD - 1, size)]
        held_rows = lax.broadcasted_iota(jnp.int32, (size, LANES), 0) <= pairs
        diag = jnp.where(held_rows, (before + total) / 3.0, 1.0)
        lower = jnp.where(held_rows, before / 6.0, 0.0)
        upper = total / 6.0
        step = 1
        while step <= pairs:
            low[here] = lower
            up[here] = upper
            main[here] = 1.0 / diag
            load[here] = grown
            back = pl.ds(PAD - step, size)
            fore = pl.ds(PAD + step, size)
            alpha = -lower * main[back]
            gamma = -upper * main[fore]
            diag = diag + alpha * up[back] + gamma * low[fore]
            grown = grown + wide(alpha) * load[back] + wide(gamma) * load[fore]
            lower = alpha * low[back]
            upper = gamma * up[fore]
            step *= 2
        result = even + grown * wide(1.0 / diag)
        result = jnp.where(wide(held_rows), result, 0.0)
        nodes[...] = jnp.zeros_like(nodes)
        for j in range(lanes // LANES):
            nodes[j, :size] = result[:, j * LANES : (j + 1) * LANES]
        cell[...] = jnp.zeros_like(cell)
        cell[:size] = total
        pairs //= 2
    coarse[...] = nodes[2, :SUB]
    coarse_width[...] = cell[:SUB]
    matrix = stored[:, : 2 * LANES]
    lane = lax.broadcasted_iota(jnp.int32, matrix.shape, 1)
    for i in range(3):
        term = matrix.astype(BF16)
        matrix = matrix - term.astype(F32)
        factors[i * TILE : (i + 1) * TILE] = jnp.where(lane < (3 - i) * HELD, term.astype(F32), 0.0).astype(BF16)


def tile_matrix(edges, cell_width):
    widths = jnp.broadcast_to(cell_width[:, None], (TILE, LANES))
    narrow = pltpu.VMEM((PAD + 40 + PAD, LANES), F32)
    broad = pltpu.VMEM((PAD + 40 + PAD, 3 * LANES), F32)
    return call(
        matrix_kernel,
        (
            jax.ShapeDtypeStruct((3 * TILE, 2 * LANES), BF16),
            jax.ShapeDtypeStruct((SUB, LANES), F32),
            jax.ShapeDtypeStruct((SUB, LANES), F32),
        ),
        in_specs=[SMEM_SPEC, VMEM_SPEC],
        out_specs=(VMEM_SPEC,) * 3,
        scratch_shapes=[
            pltpu.VMEM((3, 88, LANES), F32),
            pltpu.VMEM((88, LANES), F32),
            narrow,
            narrow,
            narrow,
            broad,
            pltpu.VMEM((TILE, 3 * LANES), F32),
        ],
    )(edges, widths)


def to_dense(result, turned, sets, sp, species):
    blocks = result.shape[1] // LANES
    per = blocks // 2
    for t in range(blocks):
        turned[t * SUB : (t + 1) * SUB] = result[:, t * LANES : (t + 1) * LANES]
    for half in range(2):
        for k in range(COARSE):
            at = ((half * COARSE + k) * species + sp) * per
            sets[pl.ds(at if isinstance(sp, int) else pl.multiple_of(at, per), per)] = turned[
                pl.ds(half * per * SUB + k, per, stride=SUB)
            ]


def brick_kernel(weights, coarse_width, field, sets, turned):
    sp = pl.program_id(0)
    slab = lax.axis_index("slab")
    own = weights[...]
    result = jnp.dot(own[:, HALO:HELD], field[0, :TILE], precision=HIGHEST, preferred_element_type=F32)
    row = jnp.where(slab == 0, field[0, TILE:HELD], 0.0)
    result += jnp.dot(own[:, :HALO], row, precision=HIGHEST, preferred_element_type=F32)
    to_dense(result, turned, sets, sp, pl.num_programs(0))

    @pl.when(sp == 0)
    def _():
        sets[sets.shape[0] - SUB :] = coarse_width[...]


def brick_part(weights, coarse_width, field):
    species, _, lines = field.shape
    dense = COARSE * species * lines // LANES + SUB
    return call(
        brick_kernel,
        jax.ShapeDtypeStruct((dense, LANES), F32),
        grid=(species,),
        in_specs=[
            pl.BlockSpec((SUB, LANES), lambda i: (0, 0)),
            pl.BlockSpec((SUB, LANES), lambda i: (0, 0)),
            pl.BlockSpec((1, HELD, lines), lambda i: (i, 0, 0)),
        ],
        out_specs=pl.BlockSpec((dense, LANES), lambda i: (0, 0)),
        scratch_shapes=[pltpu.VMEM((lines // LANES * SUB, LANES), F32)],
    )(weights, coarse_width, field)


def halo_kernel(weights, halo, part, own_half, other_half, turned, fresh):
    species = halo.shape[0]
    slab = lax.axis_index("slab")
    own = weights[:, :HALO]
    for sp in range(species):
        result = jnp.dot(own, halo[sp], precision=HIGHEST, preferred_element_type=F32)
        to_dense(result, turned, fresh, sp, species)
    rows = fresh.shape[0] // 2
    for ref, half in ((own_half, slab & 1), (other_half, 1 - (slab & 1))):
        here = pl.ds(pl.multiple_of(half * rows, SUB), rows)
        ref[:rows] = part[here] + jnp.where(slab == 0, 0.0, fresh[here])
        ref[rows:] = part[2 * rows :]


def coarse_sets(weights, halo, part):
    lines = halo.shape[2]
    rows = part.shape[0] - SUB
    half = jax.ShapeDtypeStruct((rows // 2 + SUB, LANES), F32)
    return call(
        halo_kernel,
        (half, half),
        in_specs=[VMEM_SPEC] * 3,
        out_specs=(VMEM_SPEC,) * 2,
        scratch_shapes=[
            pltpu.VMEM((lines // LANES * SUB, LANES), F32),
            pltpu.VMEM((rows, LANES), F32),
        ],
    )(weights, halo, part)


def later_nodes(shift, halo, brick):
    rows = jnp.concatenate([halo, brick], axis=0)
    count = rows.shape[0]
    return pltpu.roll(rows, (count - HALO + shift) % count, 0)


BRICK_END = TILE + SUB


def rest_kernel(edges, halo, field, out):
    species = halo.shape[0]
    shift = edges[0, 0] - lax.axis_index("slab") * TILE
    width = out.shape[1]
    other = pl.ds(pl.multiple_of((1 - lax.axis_index("cross")) * width, LANES), width)
    last = species * SECOND
    out[last:] = jnp.zeros((out.shape[0] - last, width), F32)
    for sp in range(species):
        rows = later_nodes(shift, halo[sp, :, other], field[sp, FIRST:BRICK_END, other])
        out[sp * SECOND : (sp + 1) * SECOND] = rows[:SECOND]
        out[last + sp : last + sp + 1] = rows[SECOND : SECOND + 1]


def rest_away(edges, halo, field, width):
    species = halo.shape[0]
    rows = species * SECOND + -(-species // SUB) * SUB
    return call(
        rest_kernel,
        jax.ShapeDtypeStruct((rows, width), F32),
        in_specs=[SMEM_SPEC, VMEM_SPEC, VMEM_SPEC],
        out_specs=VMEM_SPEC,
        cost=20_000_000,
    )(edges, halo, field)


def detail_kernel(local, edges, factors, first, second, *rest):
    out, wide = rest[-2:]
    species = out.shape[1]
    width = out.shape[2]
    weights = factors[:, : 3 * HELD]
    shift = edges[0, 0] - lax.axis_index("slab") * TILE
    for sp in range(species):
        if local:
            more = later_nodes(shift, first[sp], second[sp, FIRST:BRICK_END])
            pieces = [second[sp, :FIRST], more[: SECOND + HALO]]
        else:
            last = species * SECOND
            end = pltpu.roll(second[last : last + SUB], (SUB - sp) % SUB, 0)
            pieces = [first[sp], second[sp * SECOND : (sp + 1) * SECOND], end, end]
        left = jnp.concatenate(pieces, axis=0)
        terms = []
        for _ in range(3):
            terms.append(left.astype(BF16))
            left = left - terms[-1].astype(F32)
        stack = jnp.concatenate(terms, axis=0)
        result = jnp.dot(weights, stack, preferred_element_type=F32)
        result = result[:TILE] + result[TILE : 2 * TILE] + result[2 * TILE :]
        for t in range(width // LANES):
            wide[t, pl.ds(sp, TILE, stride=species)] = result[:, t * LANES : (t + 1) * LANES]
    for t in range(width // LANES):
        for k in range(DETAILS):
            out[k, :, t * LANES : (t + 1) * LANES] = wide[t, k * species : (k + 1) * species]


def details(local, edges, factors, first, second, width, species, lines, onto=None, part=None):
    chunk = min(width, 512)
    steps = width // chunk
    begin, count = (0, steps) if part is None else (part, 1)

    def here(i):
        i = i + begin
        return i if width == lines else lax.axis_index("cross") * steps + i

    def there(i):
        return (1 - lax.axis_index("cross")) * steps + i + begin

    if local:
        specs = [
            pl.BlockSpec((species, HALO, chunk), lambda i: (0, 0, here(i))),
            pl.BlockSpec((species, HELD, chunk), lambda i: (0, 0, here(i))),
        ]
    else:
        specs = [
            pl.BlockSpec((species, FIRST, chunk), lambda i: (0, 0, i + begin)),
            pl.BlockSpec((second.shape[0], chunk), lambda i: (0, i + begin)),
        ]
    specs = [SMEM_SPEC, pl.BlockSpec((3 * TILE, 2 * LANES), lambda i: (0, 0))] + specs
    operands = [edges, factors, first, second]
    alias = {}
    if onto is not None:
        specs.append(HBM_SPEC)
        operands.append(onto)
        alias = {4: 0}
    return call(
        functools.partial(detail_kernel, local),
        jax.ShapeDtypeStruct((DETAILS, species, lines), F32),
        grid=(count,),
        in_specs=specs,
        out_specs=pl.BlockSpec((DETAILS, species, chunk), lambda i: (0, 0, here(i) if local else there(i))),
        scratch_shapes=[pltpu.VMEM((chunk // LANES, TILE * species, LANES), F32)],
        input_output_aliases=alias,
        cost=20_000_000,
    )(*operands)


def merged(lower, upper):
    lower_values, lower_widths = lower
    upper_values, upper_widths = upper
    shared = 0.5 * (lower_values[-1] + upper_values[0])
    values = lower_values[:-1] + [shared] + upper_values[1:]
    widths = lower_widths + upper_widths
    left, right = widths[0::2], widths[1::2]
    pairs = len(left)
    total = [a + b for a, b in zip(left, right)]
    detail = []
    for i in range(pairs):
        inverse = 1.0 / total[i]
        detail.append(
            values[2 * i + 1] - ((right[i] * inverse) * values[2 * i] + (left[i] * inverse) * values[2 * i + 2])
        )
    loads = []
    for k in range(pairs + 1):
        term = None
        if k < pairs:
            term = (left[k] / 6.0 + right[k] / 3.0) * detail[k]
        if k > 0:
            other = (right[k - 1] / 6.0 + left[k - 1] / 3.0) * detail[k - 1]
            term = other if term is None else term + other
        loads.append(term)
    ratio, solved = [], []
    for k in range(pairs + 1):
        diag = (total[k - 1] if k else 0.0) + (total[k] if k < pairs else 0.0)
        diag = diag / 3.0
        if k:
            off = total[k - 1] / 6.0
            pivot = 1.0 / (diag - off * ratio[-1])
            solved.append((loads[k] - off * solved[-1]) * pivot)
        else:
            pivot = 1.0 / diag
            solved.append(loads[k] * pivot)
        if k < pairs:
            ratio.append(total[k] / 6.0 * pivot)
    for k in range(pairs - 1, -1, -1):
        solved[k] = solved[k] - ratio[k] * solved[k + 1]
    coarse = [values[2 * k] + solved[k] for k in range(pairs + 1)]
    return coarse, detail, total


def values_at(ref, first, rows):
    return [ref[pl.ds(first + k * rows, rows)] for k in range(COARSE)]


def widths_at(ref, first):
    return [ref[pl.ds(first + i, 1)] for i in range(COARSE - 1)]


def put(ref, first, rows, values):
    for k, value in enumerate(values):
        ref[pl.ds(first + k * rows, rows)] = value


def put_widths(ref, first, widths):
    put(ref, first, 1, widths)
    ref[first + COARSE - 1 : first + SUB] = jnp.zeros((SUB - COARSE + 1, LANES), F32)


def in_order(upper_side, mine, theirs):
    def pick(first, second):
        return [jnp.where(upper_side, a, b) for a, b in zip(first, second)]

    lower = (pick(theirs[0], mine[0]), pick(theirs[1], mine[1]))
    upper = (pick(mine[0], theirs[0]), pick(mine[1], theirs[1]))
    return merged(lower, upper)


def merge_kernel(level, depth, rows, swapped, *refs):
    slab = lax.axis_index("slab")
    core = slab & 1
    chip = slab & ~1
    upper_side = (slab >> level) & 1 == 1
    last = level == depth - 1
    set_rows = COARSE * rows + SUB
    detail_rows = (COARSE - 1) * rows
    own, other = refs[0], refs[1]
    outs = refs[-2:]

    def state(ref):
        values = values_at(ref, 0, rows) + widths_at(ref, COARSE * rows)
        if level > 0:
            values += [ref[pl.ds(set_rows + i * rows, rows)] for i in range(COARSE - 1)]
        if level > 1:
            values += [ref[pl.ds(set_rows + detail_rows + i * rows, rows)] for i in range(COARSE - 1)]
        return values

    held = state(own)
    if swapped and last:
        home = core == lax.axis_index("cross")
        held = [jnp.where(home, a, b) for a, b in zip(held, state(refs[2]))]
    mine = (held[:COARSE], held[COARSE : 2 * COARSE - 1])
    odd = held[2 * COARSE - 1 : 3 * COARSE - 2]
    even = held[3 * COARSE - 2 :]
    theirs = (values_at(other, 0, rows), widths_at(other, COARSE * rows))

    def pick(first, second):
        return [jnp.where(upper_side, a, b) for a, b in zip(first, second)]

    lower = (pick(theirs[0], mine[0]), pick(theirs[1], mine[1]))
    upper = (pick(mine[0], theirs[0]), pick(mine[1], theirs[1]))
    coarse, detail, widths = merged(lower, upper)
    if level == 0:
        odd = detail
    else:
        keep = ((chip >> level) & 1 == 1) & (chip & ((1 << level) - 1) == 0)
        if last:
            keep = keep | (chip == 0)
        even = even if level > 1 else [0.0] * (COARSE - 1)
        even = [jnp.where(keep, a, b) for a, b in zip(detail, even)]
    if last:
        here, away = outs
        put(here, 0, rows, coarse)
        put(away, 0, rows, coarse)
        put(here, COARSE * rows, rows, [jnp.where(core == 0, a, b) for a, b in zip(even, odd)])
        put(away, COARSE * rows, rows, [jnp.where(core == 0, b, a) for a, b in zip(even, odd)])
        return
    send, carried = outs
    for ref in (send, carried):
        put(ref, 0, rows, coarse)
        put_widths(ref, COARSE * rows, widths)
    put(carried, set_rows, rows, odd)
    if level > 0:
        put(carried, set_rows + detail_rows, rows, even)


def merge(level, depth, rows, swapped, *operands):
    set_rows = COARSE * rows + SUB
    detail_rows = (COARSE - 1) * rows
    if level == depth - 1:
        sizes = ((2 * COARSE - 1) * rows,) * 2
    else:
        sizes = (set_rows, set_rows + min(level + 1, 2) * detail_rows)
    return call(
        functools.partial(merge_kernel, level, depth, rows, swapped),
        tuple(jax.ShapeDtypeStruct((size, LANES), F32) for size in sizes),
        in_specs=[VMEM_SPEC] * len(operands),
        out_specs=(VMEM_SPEC,) * 2,
    )(*operands)


def finish_kernel(own, other, tree, final, turned):
    core = lax.axis_index("slab") & 1
    species, _, lines = tree.shape
    width = lines // 2
    per = width // LANES
    group = COARSE - 1
    for block, ref in ((core, own), (1 - core, other)):

        def lanes(t):
            return pl.ds(pl.multiple_of(block * width + t * LANES, LANES), LANES)

        for k in range(COARSE):
            for sp in range(species):
                turned[pl.ds(sp, per, stride=species)] = ref[(k * species + sp) * per : (k * species + sp + 1) * per]
            for t in range(per):
                final[k, :, lanes(t)] = turned[t * species : (t + 1) * species]
        for sp in range(species):
            for i in range(group):
                at = ((COARSE + i) * species + sp) * per
                turned[pl.ds(i, per, stride=group)] = ref[at : at + per]
            for t in range(per):
                tree[sp, :, lanes(t)] = turned[t * group : (t + 1) * group]


def finish(own, other, species, lines):
    return call(
        finish_kernel,
        (
            jax.ShapeDtypeStruct((species, COARSE - 1, lines), F32),
            jax.ShapeDtypeStruct((COARSE, species, lines), F32),
        ),
        in_specs=[VMEM_SPEC] * 2,
        out_specs=(VMEM_SPEC,) * 2,
        scratch_shapes=[pltpu.VMEM((lines // 2 // LANES * SUB, LANES), F32)],
    )(own, other)


def from_partner(block, axis, step):
    count = lax.axis_size(axis)
    return lax.ppermute(block, axis, [(i, i ^ step) for i in range(count)])


def shifted(block, axis):
    count = lax.axis_size(axis)
    return lax.ppermute(block, axis, [(i, i + 1) for i in range(count - 1)])


def exchanged(block, axis):
    species, rows, lines = block.shape
    count = lax.axis_size(axis)
    parts = block.reshape(species, rows, count, lines // count)
    return lax.all_to_all(parts, axis, split_axis=2, concat_axis=2, tiled=True).reshape(block.shape)


def last_routes(slabs):
    partner, own = [], []
    for s in range(slabs):
        for c in range(2):
            home = (s & 1) == c
            target = (s, c) if home else (s ^ 1, 1 - c)
            partner.append((s * 2 + c, (target[0] ^ (slabs // 2)) * 2 + target[1]))
            if not home:
                own.append((s * 2 + c, target[0] * 2 + target[1]))
    return partner, own


def on_device(sim_field, brick_edges, cell_width):
    species, _, lines = sim_field.shape
    cross_count = lax.axis_size("cross")
    slabs = lax.axis_size("slab")
    depth = slabs.bit_length() - 1
    width = lines // cross_count
    rows = species * (lines // 2) // LANES
    swapped = cross_count == 2
    both = ("slab", "cross")

    field = sim_field
    tail, *away = leaving(brick_edges, field, width)
    if swapped:
        first_in = from_partner(away[0], "cross", 1)
    halo = shifted(tail, "slab")
    factors, weights, coarse_width = tile_matrix(brick_edges, cell_width)
    part = brick_part(weights, coarse_width, field)
    halo, part, factors = lax.optimization_barrier((halo, part, factors))
    own_half, other_half = coarse_sets(weights, halo, part)
    halo, other_half = lax.optimization_barrier((halo, other_half))
    if swapped:
        rest_in = from_partner(rest_away(brick_edges, halo, field, width), "cross", 1)

    if swapped:
        near = details(True, brick_edges, factors, halo, field, width, species, lines)
    send, carried = other_half, own_half
    for level in range(depth):
        last = level == depth - 1
        if swapped and level == depth - 2:
            send, near = lax.optimization_barrier((send, near))
        if swapped and last:
            partner_route, own_route = last_routes(slabs)
            operands = (carried, lax.ppermute(send, both, partner_route), lax.ppermute(carried, both, own_route))
            tile_detail = details(False, brick_edges, factors, first_in, rest_in, width, species, lines, near)
            operands, tile_detail = lax.optimization_barrier((operands, tile_detail))
        else:
            operands = (carried, from_partner(send, "slab", 1 << level))
        send, carried = merge(level, depth, rows, swapped, *operands)
    here_set, away_set = send, carried
    partner_set = from_partner(away_set, "slab", 1)

    if swapped:
        tree_detail, coarse_final = finish(here_set, partner_set, species, lines)
        coarse_final = coarse_final.transpose(1, 0, 2)
    else:
        core = lax.axis_index("slab") % 2
        first = jnp.where(core == 0, here_set, partner_set)
        second = jnp.where(core == 0, partner_set, here_set)
        ended = jnp.stack([first, second]).reshape(2, 2 * COARSE - 1, species, lines // 2)
        ended = ended.transpose(2, 1, 0, 3).reshape(species, 2 * COARSE - 1, lines)
        ended = exchanged(ended, "cross")
        coarse_final, tree_detail = ended[:, :COARSE], ended[:, COARSE:]
        moved = exchanged(jnp.concatenate([halo, sim_field[:, :HELD]], axis=1), "cross")
        tile_detail = details(True, brick_edges, factors, moved[:, :HALO], moved[:, HALO:], lines, species, lines)
    return (tile_detail.transpose(1, 0, 2), tree_detail, coarse_final)


def solution(mesh):
    placed = (P(None, "slab", "cross"), P("slab", None), P("slab"))
    return jax.shard_map(
        on_device,
        mesh=mesh,
        in_specs=placed,
        out_specs=(P(None, "slab", "cross"), P(None, "slab", "cross"), P(None, None, "cross")),
        check_vma=False,
    )
```

```python
import functools

import jax
import jax.numpy as jnp
from jax import lax
from jax.experimental import pallas as pl
from jax.experimental.pallas import tpu as pltpu
from jax.sharding import PartitionSpec as P

TILE = 64
HALO = 16
LEVELS = 4
COARSE = 5
DETAILS = TILE - COARSE + 1
LANES = 128
SUB = 8
HELD = TILE + HALO
FIRST = 48
SECOND = TILE - FIRST
F32 = jnp.float32
BF16 = jnp.bfloat16
HIGHEST = lax.Precision.HIGHEST


def call(kernel, out_shape, *, vmem=8 << 20, cost=None, **kw):
    params = pltpu.CompilerParams(vmem_limit_bytes=vmem)
    if cost is not None:
        kw["cost_estimate"] = pl.CostEstimate(flops=cost, bytes_accessed=cost // 100, transcendentals=0)
    return pl.pallas_call(kernel, out_shape=out_shape, compiler_params=params, **kw)


VMEM_SPEC = pl.BlockSpec(memory_space=pltpu.VMEM)
SMEM_SPEC = pl.BlockSpec(memory_space=pltpu.SMEM)
HBM_SPEC = pl.BlockSpec(memory_space=pltpu.HBM)


LOW = TILE // 2


def tail_kernel(edges, rows, tail):
    start = edges[0, 1] - edges[0, 0] - HALO - LOW
    rest = start & (SUB - 1)
    whole = pl.multiple_of(start - rest, SUB)
    for sp in range(tail.shape[0]):
        window = rows[sp, pl.ds(whole, HALO + SUB), :]
        tail[sp] = pltpu.roll(window, (HALO + SUB - rest) % (HALO + SUB), 0)[:HALO]


def brick_tail(edges, field):
    species, _, lines = field.shape
    return call(
        tail_kernel,
        jax.ShapeDtypeStruct((species, HALO, lines), F32),
        in_specs=[SMEM_SPEC, VMEM_SPEC],
        out_specs=VMEM_SPEC,
    )(edges, field[:, LOW : LOW + TILE])


def first_kernel(field, away):
    species, _, width = away.shape
    other = pl.ds(pl.multiple_of((1 - lax.axis_index("cross")) * width, LANES), width)
    for sp in range(species):
        away[sp] = field[sp, :FIRST, other]


def first_rows(field, width):
    return call(
        first_kernel,
        jax.ShapeDtypeStruct((field.shape[0], FIRST, width), F32),
        in_specs=[VMEM_SPEC],
        out_specs=VMEM_SPEC,
    )(field)


PAD = 32


def matrix_kernel(edges, widths, factors, coarse, coarse_width, nodes, cell, low, main, up, load, stored):
    slab = lax.axis_index("slab")
    shift = edges[0, 0] - slab * TILE
    rows, lanes = nodes.shape[1], nodes.shape[0] * LANES
    node = lax.broadcasted_iota(jnp.int32, (rows, lanes), 0)
    lane = lax.broadcasted_iota(jnp.int32, (rows, lanes), 1)
    column = lane % HELD
    later = column - FIRST
    held = jnp.where(column < FIRST, column + shift, jnp.where(later < shift, later, column))
    plain = lane - 2 * LANES
    from_halo = jnp.where((slab == 0) & (plain < HALO), plain + TILE, plain - HALO + shift)
    grouped = (lane < 3 * HELD) & (column <= TILE)
    held = jnp.where(lane < 2 * LANES, jnp.where(grouped, held, -1), jnp.where(plain < HELD, from_halo, -1))
    chosen = ((held == node) & (node <= TILE)).astype(F32)
    for j in range(lanes // LANES):
        nodes[j] = chosen[:, j * LANES : (j + 1) * LANES]
    cell[...] = jnp.zeros_like(cell)
    cell[:TILE] = widths[...]
    for ref in (low, up, load):
        ref[...] = jnp.zeros_like(ref)
    main[...] = jnp.ones_like(main)
    stored[...] = jnp.zeros_like(stored)
    wide = lambda x: jnp.concatenate([x] * (lanes // LANES), axis=1)
    placed = 0
    pairs = TILE // 2
    for _ in range(LEVELS):
        size = -(-(pairs + 1) // SUB) * SUB
        here = pl.ds(PAD, size)
        inside = lax.broadcasted_iota(jnp.int32, (size, LANES), 0) < pairs
        left = cell[pl.ds(0, size, stride=2)]
        right = cell[pl.ds(1, size, stride=2)]
        total = left + right
        safe = jnp.where(inside, total, 1.0)
        even, odd, after = [
            jnp.concatenate([nodes[j, pl.ds(i, size, stride=2)] for j in range(lanes // LANES)], axis=1)
            for i in range(3)
        ]
        inverse = 1.0 / safe
        detail = odd - (wide(right * inverse) * even + wide(left * inverse) * after)
        detail = jnp.where(wide(inside), detail, 0.0)
        stored[placed : placed + pairs] = detail[:pairs]
        placed += pairs
        load[here] = wide(right / 6.0 + left / 3.0) * detail
        load[pl.ds(PAD - 1, 1)] = jnp.zeros((1, lanes), F32)
        grown = wide(left / 6.0 + right / 3.0) * detail + load[pl.ds(PAD - 1, size)]
        up[here] = total
        before = up[pl.ds(PAD - 1, size)]
        held_rows = lax.broadcasted_iota(jnp.int32, (size, LANES), 0) <= pairs
        diag = jnp.where(held_rows, (before + total) / 3.0, 1.0)
        lower = jnp.where(held_rows, before / 6.0, 0.0)
        upper = total / 6.0
        step = 1
        while step <= pairs:
            low[here] = lower
            up[here] = upper
            main[here] = 1.0 / diag
            load[here] = grown
            back = pl.ds(PAD - step, size)
            fore = pl.ds(PAD + step, size)
            alpha = -lower * main[back]
            gamma = -upper * main[fore]
            diag = diag + alpha * up[back] + gamma * low[fore]
            grown = grown + wide(alpha) * load[back] + wide(gamma) * load[fore]
            lower = alpha * low[back]
            upper = gamma * up[fore]
            step *= 2
        result = even + grown * wide(1.0 / diag)
        result = jnp.where(wide(held_rows), result, 0.0)
        nodes[...] = jnp.zeros_like(nodes)
        for j in range(lanes // LANES):
            nodes[j, :size] = result[:, j * LANES : (j + 1) * LANES]
        cell[...] = jnp.zeros_like(cell)
        cell[:size] = total
        pairs //= 2
    coarse[...] = nodes[2, :SUB]
    coarse_width[...] = cell[:SUB]
    matrix = stored[:, : 2 * LANES]
    lane = lax.broadcasted_iota(jnp.int32, matrix.shape, 1)
    for i in range(3):
        term = matrix.astype(BF16)
        matrix = matrix - term.astype(F32)
        factors[i * TILE : (i + 1) * TILE] = jnp.where(lane < (3 - i) * HELD, term.astype(F32), 0.0).astype(BF16)


def tile_matrix(edges, cell_width):
    widths = jnp.broadcast_to(cell_width[:, None], (TILE, LANES))
    narrow = pltpu.VMEM((PAD + 40 + PAD, LANES), F32)
    broad = pltpu.VMEM((PAD + 40 + PAD, 3 * LANES), F32)
    return call(
        matrix_kernel,
        (
            jax.ShapeDtypeStruct((3 * TILE, 2 * LANES), BF16),
            jax.ShapeDtypeStruct((SUB, LANES), F32),
            jax.ShapeDtypeStruct((SUB, LANES), F32),
        ),
        in_specs=[SMEM_SPEC, VMEM_SPEC],
        out_specs=(VMEM_SPEC,) * 3,
        scratch_shapes=[
            pltpu.VMEM((3, 88, LANES), F32),
            pltpu.VMEM((88, LANES), F32),
            narrow,
            narrow,
            narrow,
            broad,
            pltpu.VMEM((TILE, 3 * LANES), F32),
        ],
    )(edges, widths)


def to_dense(result, turned, sets, sp, species):
    blocks = result.shape[1] // LANES
    per = blocks // 2
    for t in range(blocks):
        turned[t * SUB : (t + 1) * SUB] = result[:, t * LANES : (t + 1) * LANES]
    for half in range(2):
        for k in range(COARSE):
            at = ((half * COARSE + k) * species + sp) * per
            sets[pl.ds(at if isinstance(sp, int) else pl.multiple_of(at, per), per)] = turned[
                pl.ds(half * per * SUB + k, per, stride=SUB)
            ]


def brick_kernel(weights, coarse_width, field, sets, turned):
    sp = pl.program_id(0)
    slab = lax.axis_index("slab")
    own = weights[...]
    result = jnp.dot(own[:, HALO:HELD], field[0, :TILE], precision=HIGHEST, preferred_element_type=F32)
    row = jnp.where(slab == 0, field[0, TILE:HELD], 0.0)
    result += jnp.dot(own[:, :HALO], row, precision=HIGHEST, preferred_element_type=F32)
    to_dense(result, turned, sets, sp, pl.num_programs(0))

    @pl.when(sp == 0)
    def _():
        sets[sets.shape[0] - SUB :] = coarse_width[...]


def brick_part(weights, coarse_width, field):
    species, _, lines = field.shape
    dense = COARSE * species * lines // LANES + SUB
    return call(
        brick_kernel,
        jax.ShapeDtypeStruct((dense, LANES), F32),
        grid=(species,),
        in_specs=[
            pl.BlockSpec((SUB, LANES), lambda i: (0, 0)),
            pl.BlockSpec((SUB, LANES), lambda i: (0, 0)),
            pl.BlockSpec((1, HELD, lines), lambda i: (i, 0, 0)),
        ],
        out_specs=pl.BlockSpec((dense, LANES), lambda i: (0, 0)),
        scratch_shapes=[pltpu.VMEM((lines // LANES * SUB, LANES), F32)],
    )(weights, coarse_width, field)


def halo_kernel(weights, halo, part, own_half, other_half, turned, fresh):
    species = halo.shape[0]
    slab = lax.axis_index("slab")
    own = weights[:, :HALO]
    for sp in range(species):
        result = jnp.dot(own, halo[sp], precision=HIGHEST, preferred_element_type=F32)
        to_dense(result, turned, fresh, sp, species)
    rows = fresh.shape[0] // 2
    for ref, half in ((own_half, slab & 1), (other_half, 1 - (slab & 1))):
        here = pl.ds(pl.multiple_of(half * rows, SUB), rows)
        ref[:rows] = part[here] + jnp.where(slab == 0, 0.0, fresh[here])
        ref[rows:] = part[2 * rows :]


def coarse_sets(weights, halo, part):
    lines = halo.shape[2]
    rows = part.shape[0] - SUB
    half = jax.ShapeDtypeStruct((rows // 2 + SUB, LANES), F32)
    return call(
        halo_kernel,
        (half, half),
        in_specs=[VMEM_SPEC] * 3,
        out_specs=(VMEM_SPEC,) * 2,
        scratch_shapes=[
            pltpu.VMEM((lines // LANES * SUB, LANES), F32),
            pltpu.VMEM((rows, LANES), F32),
        ],
    )(weights, halo, part)


def later_nodes(shift, halo, brick):
    rows = jnp.concatenate([halo, brick], axis=0)
    count = rows.shape[0]
    return pltpu.roll(rows, (count - HALO + shift) % count, 0)


BRICK_END = TILE + SUB


def rest_kernel(edges, halo, field, out):
    species = halo.shape[0]
    shift = edges[0, 0] - lax.axis_index("slab") * TILE
    width = out.shape[1]
    other = pl.ds(pl.multiple_of((1 - lax.axis_index("cross")) * width, LANES), width)
    last = species * SECOND
    out[last:] = jnp.zeros((out.shape[0] - last, width), F32)
    for sp in range(species):
        rows = later_nodes(shift, halo[sp, :, other], field[sp, FIRST:BRICK_END, other])
        out[sp * SECOND : (sp + 1) * SECOND] = rows[:SECOND]
        out[last + sp : last + sp + 1] = rows[SECOND : SECOND + 1]


def rest_away(edges, halo, field, width):
    species = halo.shape[0]
    rows = species * SECOND + -(-species // SUB) * SUB
    return call(
        rest_kernel,
        jax.ShapeDtypeStruct((rows, width), F32),
        in_specs=[SMEM_SPEC, VMEM_SPEC, VMEM_SPEC],
        out_specs=VMEM_SPEC,
        cost=20_000_000,
    )(edges, halo, field)


def detail_kernel(local, edges, factors, first, second, *rest):
    out, wide = rest[-2:]
    species = out.shape[1]
    width = out.shape[2]
    weights = factors[:, : 3 * HELD]
    shift = edges[0, 0] - lax.axis_index("slab") * TILE
    for sp in range(species):
        if local:
            more = later_nodes(shift, first[sp], second[sp, FIRST:BRICK_END])
            pieces = [second[sp, :FIRST], more[: SECOND + HALO]]
        else:
            last = species * SECOND
            end = pltpu.roll(second[last : last + SUB], (SUB - sp) % SUB, 0)
            pieces = [first[sp], second[sp * SECOND : (sp + 1) * SECOND], end, end]
        left = jnp.concatenate(pieces, axis=0)
        terms = []
        for _ in range(3):
            terms.append(left.astype(BF16))
            left = left - terms[-1].astype(F32)
        stack = jnp.concatenate(terms, axis=0)
        result = jnp.dot(weights, stack, preferred_element_type=F32)
        result = result[:TILE] + result[TILE : 2 * TILE] + result[2 * TILE :]
        for t in range(width // LANES):
            wide[t, pl.ds(sp, TILE, stride=species)] = result[:, t * LANES : (t + 1) * LANES]
    for t in range(width // LANES):
        for k in range(DETAILS):
            out[k, :, t * LANES : (t + 1) * LANES] = wide[t, k * species : (k + 1) * species]


def details(local, edges, factors, first, second, width, species, lines, onto=None, part=None):
    chunk = min(width, 512)
    steps = width // chunk
    begin, count = (0, steps) if part is None else (part, 1)

    def here(i):
        i = i + begin
        return i if width == lines else lax.axis_index("cross") * steps + i

    def there(i):
        return (1 - lax.axis_index("cross")) * steps + i + begin

    if local:
        specs = [
            pl.BlockSpec((species, HALO, chunk), lambda i: (0, 0, here(i))),
            pl.BlockSpec((species, HELD, chunk), lambda i: (0, 0, here(i))),
        ]
    else:
        specs = [
            pl.BlockSpec((species, FIRST, chunk), lambda i: (0, 0, i + begin)),
            pl.BlockSpec((second.shape[0], chunk), lambda i: (0, i + begin)),
        ]
    specs = [SMEM_SPEC, pl.BlockSpec((3 * TILE, 2 * LANES), lambda i: (0, 0))] + specs
    operands = [edges, factors, first, second]
    alias = {}
    if onto is not None:
        specs.append(HBM_SPEC)
        operands.append(onto)
        alias = {4: 0}
    return call(
        functools.partial(detail_kernel, local),
        jax.ShapeDtypeStruct((DETAILS, species, lines), F32),
        grid=(count,),
        in_specs=specs,
        out_specs=pl.BlockSpec((DETAILS, species, chunk), lambda i: (0, 0, here(i) if local else there(i))),
        scratch_shapes=[pltpu.VMEM((chunk // LANES, TILE * species, LANES), F32)],
        input_output_aliases=alias,
        cost=20_000_000,
    )(*operands)


def merged(lower, upper):
    lower_values, lower_widths = lower
    upper_values, upper_widths = upper
    shared = 0.5 * (lower_values[-1] + upper_values[0])
    values = lower_values[:-1] + [shared] + upper_values[1:]
    widths = lower_widths + upper_widths
    left, right = widths[0::2], widths[1::2]
    pairs = len(left)
    total = [a + b for a, b in zip(left, right)]
    detail = []
    for i in range(pairs):
        inverse = 1.0 / total[i]
        detail.append(
            values[2 * i + 1] - ((right[i] * inverse) * values[2 * i] + (left[i] * inverse) * values[2 * i + 2])
        )
    loads = []
    for k in range(pairs + 1):
        term = None
        if k < pairs:
            term = (left[k] / 6.0 + right[k] / 3.0) * detail[k]
        if k > 0:
            other = (right[k - 1] / 6.0 + left[k - 1] / 3.0) * detail[k - 1]
            term = other if term is None else term + other
        loads.append(term)
    ratio, solved = [], []
    for k in range(pairs + 1):
        diag = (total[k - 1] if k else 0.0) + (total[k] if k < pairs else 0.0)
        diag = diag / 3.0
        if k:
            off = total[k - 1] / 6.0
            pivot = 1.0 / (diag - off * ratio[-1])
            solved.append((loads[k] - off * solved[-1]) * pivot)
        else:
            pivot = 1.0 / diag
            solved.append(loads[k] * pivot)
        if k < pairs:
            ratio.append(total[k] / 6.0 * pivot)
    for k in range(pairs - 1, -1, -1):
        solved[k] = solved[k] - ratio[k] * solved[k + 1]
    coarse = [values[2 * k] + solved[k] for k in range(pairs + 1)]
    return coarse, detail, total


def values_at(ref, first, rows):
    return [ref[pl.ds(first + k * rows, rows)] for k in range(COARSE)]


def widths_at(ref, first):
    return [ref[pl.ds(first + i, 1)] for i in range(COARSE - 1)]


def put(ref, first, rows, values):
    for k, value in enumerate(values):
        ref[pl.ds(first + k * rows, rows)] = value


def put_widths(ref, first, widths):
    put(ref, first, 1, widths)
    ref[first + COARSE - 1 : first + SUB] = jnp.zeros((SUB - COARSE + 1, LANES), F32)


def in_order(upper_side, mine, theirs):
    def pick(first, second):
        return [jnp.where(upper_side, a, b) for a, b in zip(first, second)]

    lower = (pick(theirs[0], mine[0]), pick(theirs[1], mine[1]))
    upper = (pick(mine[0], theirs[0]), pick(mine[1], theirs[1]))
    return merged(lower, upper)


def merge_kernel(level, depth, rows, swapped, *refs):
    slab = lax.axis_index("slab")
    core = slab & 1
    chip = slab & ~1
    upper_side = (slab >> level) & 1 == 1
    last = level == depth - 1
    set_rows = COARSE * rows + SUB
    detail_rows = (COARSE - 1) * rows
    own, other = refs[0], refs[1]
    outs = refs[-2:]

    def state(ref):
        values = values_at(ref, 0, rows) + widths_at(ref, COARSE * rows)
        if level > 0:
            values += [ref[pl.ds(set_rows + i * rows, rows)] for i in range(COARSE - 1)]
        if level > 1:
            values += [ref[pl.ds(set_rows + detail_rows + i * rows, rows)] for i in range(COARSE - 1)]
        return values

    held = state(own)
    if swapped and last:
        home = core == lax.axis_index("cross")
        held = [jnp.where(home, a, b) for a, b in zip(held, state(refs[2]))]
    mine = (held[:COARSE], held[COARSE : 2 * COARSE - 1])
    odd = held[2 * COARSE - 1 : 3 * COARSE - 2]
    even = held[3 * COARSE - 2 :]
    theirs = (values_at(other, 0, rows), widths_at(other, COARSE * rows))

    def pick(first, second):
        return [jnp.where(upper_side, a, b) for a, b in zip(first, second)]

    lower = (pick(theirs[0], mine[0]), pick(theirs[1], mine[1]))
    upper = (pick(mine[0], theirs[0]), pick(mine[1], theirs[1]))
    coarse, detail, widths = merged(lower, upper)
    if level == 0:
        odd = detail
    else:
        keep = ((chip >> level) & 1 == 1) & (chip & ((1 << level) - 1) == 0)
        if last:
            keep = keep | (chip == 0)
        even = even if level > 1 else [0.0] * (COARSE - 1)
        even = [jnp.where(keep, a, b) for a, b in zip(detail, even)]
    if last:
        here, away = outs
        put(here, 0, rows, coarse)
        put(away, 0, rows, coarse)
        put(here, COARSE * rows, rows, [jnp.where(core == 0, a, b) for a, b in zip(even, odd)])
        put(away, COARSE * rows, rows, [jnp.where(core == 0, b, a) for a, b in zip(even, odd)])
        return
    send, carried = outs
    for ref in (send, carried):
        put(ref, 0, rows, coarse)
        put_widths(ref, COARSE * rows, widths)
    put(carried, set_rows, rows, odd)
    if level > 0:
        put(carried, set_rows + detail_rows, rows, even)


def merge(level, depth, rows, swapped, *operands):
    set_rows = COARSE * rows + SUB
    detail_rows = (COARSE - 1) * rows
    if level == depth - 1:
        sizes = ((2 * COARSE - 1) * rows,) * 2
    else:
        sizes = (set_rows, set_rows + min(level + 1, 2) * detail_rows)
    return call(
        functools.partial(merge_kernel, level, depth, rows, swapped),
        tuple(jax.ShapeDtypeStruct((size, LANES), F32) for size in sizes),
        in_specs=[VMEM_SPEC] * len(operands),
        out_specs=(VMEM_SPEC,) * 2,
    )(*operands)


def finish_kernel(own, other, tree, final, turned):
    core = lax.axis_index("slab") & 1
    species, _, lines = tree.shape
    width = lines // 2
    per = width // LANES
    group = COARSE - 1
    for block, ref in ((core, own), (1 - core, other)):

        def lanes(t):
            return pl.ds(pl.multiple_of(block * width + t * LANES, LANES), LANES)

        for k in range(COARSE):
            for sp in range(species):
                turned[pl.ds(sp, per, stride=species)] = ref[(k * species + sp) * per : (k * species + sp + 1) * per]
            for t in range(per):
                final[k, :, lanes(t)] = turned[t * species : (t + 1) * species]
        for sp in range(species):
            for i in range(group):
                at = ((COARSE + i) * species + sp) * per
                turned[pl.ds(i, per, stride=group)] = ref[at : at + per]
            for t in range(per):
                tree[sp, :, lanes(t)] = turned[t * group : (t + 1) * group]


def finish(own, other, species, lines):
    return call(
        finish_kernel,
        (
            jax.ShapeDtypeStruct((species, COARSE - 1, lines), F32),
            jax.ShapeDtypeStruct((COARSE, species, lines), F32),
        ),
        in_specs=[VMEM_SPEC] * 2,
        out_specs=(VMEM_SPEC,) * 2,
        scratch_shapes=[pltpu.VMEM((lines // 2 // LANES * SUB, LANES), F32)],
    )(own, other)


def from_partner(block, axis, step):
    count = lax.axis_size(axis)
    return lax.ppermute(block, axis, [(i, i ^ step) for i in range(count)])


def shifted(block, axis):
    count = lax.axis_size(axis)
    return lax.ppermute(block, axis, [(i, i + 1) for i in range(count - 1)])


def exchanged(block, axis):
    species, rows, lines = block.shape
    count = lax.axis_size(axis)
    parts = block.reshape(species, rows, count, lines // count)
    return lax.all_to_all(parts, axis, split_axis=2, concat_axis=2, tiled=True).reshape(block.shape)


def last_routes(slabs):
    partner, own = [], []
    for s in range(slabs):
        for c in range(2):
            home = (s & 1) == c
            target = (s, c) if home else (s ^ 1, 1 - c)
            partner.append((s * 2 + c, (target[0] ^ (slabs // 2)) * 2 + target[1]))
            if not home:
                own.append((s * 2 + c, target[0] * 2 + target[1]))
    return partner, own


def on_device(sim_field, brick_edges, cell_width):
    species, _, lines = sim_field.shape
    cross_count = lax.axis_size("cross")
    slabs = lax.axis_size("slab")
    depth = slabs.bit_length() - 1
    width = lines // cross_count
    rows = species * (lines // 2) // LANES
    swapped = cross_count == 2
    both = ("slab", "cross")

    field = sim_field
    halo = shifted(brick_tail(brick_edges, field), "slab")
    if swapped:
        first_in = from_partner(first_rows(field, width), "cross", 1)
    factors, weights, coarse_width = tile_matrix(brick_edges, cell_width)
    part = brick_part(weights, coarse_width, field)
    halo, part, factors = lax.optimization_barrier((halo, part, factors))
    own_half, other_half = coarse_sets(weights, halo, part)
    halo, other_half = lax.optimization_barrier((halo, other_half))
    if swapped:
        rest_in = from_partner(rest_away(brick_edges, halo, field, width), "cross", 1)

    if swapped:
        near = details(True, brick_edges, factors, halo, field, width, species, lines)
    send, carried = other_half, own_half
    for level in range(depth):
        last = level == depth - 1
        if swapped and level == depth - 2:
            send, near = lax.optimization_barrier((send, near))
        if swapped and last:
            partner_route, own_route = last_routes(slabs)
            operands = (carried, lax.ppermute(send, both, partner_route), lax.ppermute(carried, both, own_route))
            tile_detail = details(False, brick_edges, factors, first_in, rest_in, width, species, lines, near)
            operands, tile_detail = lax.optimization_barrier((operands, tile_detail))
        else:
            operands = (carried, from_partner(send, "slab", 1 << level))
        send, carried = merge(level, depth, rows, swapped, *operands)
    here_set, away_set = send, carried
    partner_set = from_partner(away_set, "slab", 1)

    if swapped:
        tree_detail, coarse_final = finish(here_set, partner_set, species, lines)
        coarse_final = coarse_final.transpose(1, 0, 2)
    else:
        core = lax.axis_index("slab") % 2
        first = jnp.where(core == 0, here_set, partner_set)
        second = jnp.where(core == 0, partner_set, here_set)
        ended = jnp.stack([first, second]).reshape(2, 2 * COARSE - 1, species, lines // 2)
        ended = ended.transpose(2, 1, 0, 3).reshape(species, 2 * COARSE - 1, lines)
        ended = exchanged(ended, "cross")
        coarse_final, tree_detail = ended[:, :COARSE], ended[:, COARSE:]
        moved = exchanged(jnp.concatenate([halo, sim_field[:, :HELD]], axis=1), "cross")
        tile_detail = details(True, brick_edges, factors, moved[:, :HALO], moved[:, HALO:], lines, species, lines)
    return (tile_detail.transpose(1, 0, 2), tree_detail, coarse_final)


def solution(mesh):
    placed = (P(None, "slab", "cross"), P("slab", None), P("slab"))
    return jax.shard_map(
        on_device,
        mesh=mesh,
        in_specs=placed,
        out_specs=(P(None, "slab", "cross"), P(None, "slab", "cross"), P(None, None, "cross")),
        check_vma=False,
    )
```

```python
import functools

import jax
import jax.numpy as jnp
from jax import lax
from jax.experimental import pallas as pl
from jax.experimental.pallas import tpu as pltpu
from jax.sharding import PartitionSpec as P

TILE = 64
HALO = 16
LEVELS = 4
COARSE = 5
DETAILS = TILE - COARSE + 1
LANES = 128
SUB = 8
HELD = TILE + HALO
FIRST = 48
SECOND = TILE - FIRST
F32 = jnp.float32
BF16 = jnp.bfloat16
HIGHEST = lax.Precision.HIGHEST


def call(kernel, out_shape, *, vmem=8 << 20, cost=None, **kw):
    params = pltpu.CompilerParams(vmem_limit_bytes=vmem)
    if cost is not None:
        kw["cost_estimate"] = pl.CostEstimate(flops=cost, bytes_accessed=cost // 100, transcendentals=0)
    return pl.pallas_call(kernel, out_shape=out_shape, compiler_params=params, **kw)


VMEM_SPEC = pl.BlockSpec(memory_space=pltpu.VMEM)
SMEM_SPEC = pl.BlockSpec(memory_space=pltpu.SMEM)
HBM_SPEC = pl.BlockSpec(memory_space=pltpu.HBM)


LOW = TILE // 2


def tail_kernel(edges, rows, tail):
    start = edges[0, 1] - edges[0, 0] - HALO - LOW
    rest = start & (SUB - 1)
    whole = pl.multiple_of(start - rest, SUB)
    for sp in range(tail.shape[0]):
        window = rows[sp, pl.ds(whole, HALO + SUB), :]
        tail[sp] = pltpu.roll(window, (HALO + SUB - rest) % (HALO + SUB), 0)[:HALO]


def brick_tail(edges, field):
    species, _, lines = field.shape
    return call(
        tail_kernel,
        jax.ShapeDtypeStruct((species, HALO, lines), F32),
        in_specs=[SMEM_SPEC, VMEM_SPEC],
        out_specs=VMEM_SPEC,
    )(edges, field[:, LOW : LOW + TILE])


def first_kernel(field, away):
    species, _, width = away.shape
    other = pl.ds(pl.multiple_of((1 - lax.axis_index("cross")) * width, LANES), width)
    for sp in range(species):
        away[sp] = field[sp, :FIRST, other]


def first_rows(field, width):
    return call(
        first_kernel,
        jax.ShapeDtypeStruct((field.shape[0], FIRST, width), F32),
        in_specs=[VMEM_SPEC],
        out_specs=VMEM_SPEC,
    )(field)


PAD = 32


def matrix_kernel(edges, widths, factors, coarse, coarse_width, nodes, cell, low, main, up, load, stored):
    slab = lax.axis_index("slab")
    shift = edges[0, 0] - slab * TILE
    rows, lanes = nodes.shape[1], nodes.shape[0] * LANES
    node = lax.broadcasted_iota(jnp.int32, (rows, lanes), 0)
    lane = lax.broadcasted_iota(jnp.int32, (rows, lanes), 1)
    column = lane % HELD
    later = column - FIRST
    held = jnp.where(column < FIRST, column + shift, jnp.where(later < shift, later, column))
    plain = lane - 2 * LANES
    from_halo = jnp.where((slab == 0) & (plain < HALO), plain + TILE, plain - HALO + shift)
    grouped = (lane < 3 * HELD) & (column <= TILE)
    held = jnp.where(lane < 2 * LANES, jnp.where(grouped, held, -1), jnp.where(plain < HELD, from_halo, -1))
    chosen = ((held == node) & (node <= TILE)).astype(F32)
    for j in range(lanes // LANES):
        nodes[j] = chosen[:, j * LANES : (j + 1) * LANES]
    cell[...] = jnp.zeros_like(cell)
    cell[:TILE] = widths[...]
    for ref in (low, up, load):
        ref[...] = jnp.zeros_like(ref)
    main[...] = jnp.ones_like(main)
    stored[...] = jnp.zeros_like(stored)
    wide = lambda x: jnp.concatenate([x] * (lanes // LANES), axis=1)
    placed = 0
    pairs = TILE // 2
    for _ in range(LEVELS):
        size = -(-(pairs + 1) // SUB) * SUB
        here = pl.ds(PAD, size)
        inside = lax.broadcasted_iota(jnp.int32, (size, LANES), 0) < pairs
        left = cell[pl.ds(0, size, stride=2)]
        right = cell[pl.ds(1, size, stride=2)]
        total = left + right
        safe = jnp.where(inside, total, 1.0)
        even, odd, after = [
            jnp.concatenate([nodes[j, pl.ds(i, size, stride=2)] for j in range(lanes // LANES)], axis=1)
            for i in range(3)
        ]
        inverse = 1.0 / safe
        detail = odd - (wide(right * inverse) * even + wide(left * inverse) * after)
        detail = jnp.where(wide(inside), detail, 0.0)
        stored[placed : placed + pairs] = detail[:pairs]
        placed += pairs
        load[here] = wide(right / 6.0 + left / 3.0) * detail
        load[pl.ds(PAD - 1, 1)] = jnp.zeros((1, lanes), F32)
        grown = wide(left / 6.0 + right / 3.0) * detail + load[pl.ds(PAD - 1, size)]
        up[here] = total
        before = up[pl.ds(PAD - 1, size)]
        held_rows = lax.broadcasted_iota(jnp.int32, (size, LANES), 0) <= pairs
        diag = jnp.where(held_rows, (before + total) / 3.0, 1.0)
        lower = jnp.where(held_rows, before / 6.0, 0.0)
        upper = total / 6.0
        step = 1
        while step <= pairs:
            low[here] = lower
            up[here] = upper
            main[here] = 1.0 / diag
            load[here] = grown
            back = pl.ds(PAD - step, size)
            fore = pl.ds(PAD + step, size)
            alpha = -lower * main[back]
            gamma = -upper * main[fore]
            diag = diag + alpha * up[back] + gamma * low[fore]
            grown = grown + wide(alpha) * load[back] + wide(gamma) * load[fore]
            lower = alpha * low[back]
            upper = gamma * up[fore]
            step *= 2
        result = even + grown * wide(1.0 / diag)
        result = jnp.where(wide(held_rows), result, 0.0)
        nodes[...] = jnp.zeros_like(nodes)
        for j in range(lanes // LANES):
            nodes[j, :size] = result[:, j * LANES : (j + 1) * LANES]
        cell[...] = jnp.zeros_like(cell)
        cell[:size] = total
        pairs //= 2
    coarse[...] = nodes[2, :SUB]
    coarse_width[...] = cell[:SUB]
    matrix = stored[:, : 2 * LANES]
    lane = lax.broadcasted_iota(jnp.int32, matrix.shape, 1)
    for i in range(3):
        term = matrix.astype(BF16)
        matrix = matrix - term.astype(F32)
        factors[i * TILE : (i + 1) * TILE] = jnp.where(lane < (3 - i) * HELD, term.astype(F32), 0.0).astype(BF16)


def tile_matrix(edges, cell_width):
    widths = jnp.broadcast_to(cell_width[:, None], (TILE, LANES))
    narrow = pltpu.VMEM((PAD + 40 + PAD, LANES), F32)
    broad = pltpu.VMEM((PAD + 40 + PAD, 3 * LANES), F32)
    return call(
        matrix_kernel,
        (
            jax.ShapeDtypeStruct((3 * TILE, 2 * LANES), BF16),
            jax.ShapeDtypeStruct((SUB, LANES), F32),
            jax.ShapeDtypeStruct((SUB, LANES), F32),
        ),
        in_specs=[SMEM_SPEC, VMEM_SPEC],
        out_specs=(VMEM_SPEC,) * 3,
        scratch_shapes=[
            pltpu.VMEM((3, 88, LANES), F32),
            pltpu.VMEM((88, LANES), F32),
            narrow,
            narrow,
            narrow,
            broad,
            pltpu.VMEM((TILE, 3 * LANES), F32),
        ],
    )(edges, widths)


def to_dense(result, turned, sets, sp, species):
    blocks = result.shape[1] // LANES
    per = blocks // 2
    for t in range(blocks):
        turned[t * SUB : (t + 1) * SUB] = result[:, t * LANES : (t + 1) * LANES]
    for half in range(2):
        for k in range(COARSE):
            at = ((half * COARSE + k) * species + sp) * per
            sets[pl.ds(at if isinstance(sp, int) else pl.multiple_of(at, per), per)] = turned[
                pl.ds(half * per * SUB + k, per, stride=SUB)
            ]


def brick_kernel(weights, coarse_width, field, sets, turned):
    sp = pl.program_id(0)
    slab = lax.axis_index("slab")
    own = weights[...]
    result = jnp.dot(own[:, HALO:HELD], field[0, :TILE], precision=HIGHEST, preferred_element_type=F32)
    row = jnp.where(slab == 0, field[0, TILE:HELD], 0.0)
    result += jnp.dot(own[:, :HALO], row, precision=HIGHEST, preferred_element_type=F32)
    to_dense(result, turned, sets, sp, pl.num_programs(0))

    @pl.when(sp == 0)
    def _():
        sets[sets.shape[0] - SUB :] = coarse_width[...]


def brick_part(weights, coarse_width, field):
    species, _, lines = field.shape
    dense = COARSE * species * lines // LANES + SUB
    return call(
        brick_kernel,
        jax.ShapeDtypeStruct((dense, LANES), F32),
        grid=(species,),
        in_specs=[
            pl.BlockSpec((SUB, LANES), lambda i: (0, 0)),
            pl.BlockSpec((SUB, LANES), lambda i: (0, 0)),
            pl.BlockSpec((1, HELD, lines), lambda i: (i, 0, 0)),
        ],
        out_specs=pl.BlockSpec((dense, LANES), lambda i: (0, 0)),
        scratch_shapes=[pltpu.VMEM((lines // LANES * SUB, LANES), F32)],
    )(weights, coarse_width, field)


def terms_of(value):
    terms = []
    for _ in range(3):
        terms.append(value.astype(BF16))
        value = value - terms[-1].astype(F32)
    return terms


def halo_kernel(weights, halo, part, own_half, other_half, turned, fresh):
    species = halo.shape[0]
    slab = lax.axis_index("slab")
    weight_terms = terms_of(weights[:, :HALO])
    zero = jnp.zeros_like(weights[:, :HALO])
    own = jnp.concatenate(
        [jnp.concatenate([weight_terms[i].astype(F32)] * (3 - i) + [zero] * i, axis=1) for i in range(3)], axis=0
    ).astype(BF16)
    for sp in range(species):
        stack = jnp.concatenate(terms_of(halo[sp]), axis=0)
        result = jnp.dot(own, stack, preferred_element_type=F32)
        result = result[:SUB] + result[SUB : 2 * SUB] + result[2 * SUB :]
        to_dense(result, turned, fresh, sp, species)
    rows = fresh.shape[0] // 2
    for ref, half in ((own_half, slab & 1), (other_half, 1 - (slab & 1))):
        here = pl.ds(pl.multiple_of(half * rows, SUB), rows)
        ref[:rows] = part[here] + jnp.where(slab == 0, 0.0, fresh[here])
        ref[rows:] = part[2 * rows :]


def coarse_sets(weights, halo, part):
    lines = halo.shape[2]
    rows = part.shape[0] - SUB
    half = jax.ShapeDtypeStruct((rows // 2 + SUB, LANES), F32)
    return call(
        halo_kernel,
        (half, half),
        in_specs=[VMEM_SPEC] * 3,
        out_specs=(VMEM_SPEC,) * 2,
        scratch_shapes=[
            pltpu.VMEM((lines // LANES * SUB, LANES), F32),
            pltpu.VMEM((rows, LANES), F32),
        ],
    )(weights, halo, part)


def later_nodes(shift, halo, brick):
    rows = jnp.concatenate([halo, brick], axis=0)
    count = rows.shape[0]
    return pltpu.roll(rows, (count - HALO + shift) % count, 0)


BRICK_END = TILE + SUB


def rest_kernel(edges, halo, field, out):
    species = halo.shape[0]
    shift = edges[0, 0] - lax.axis_index("slab") * TILE
    width = out.shape[1]
    other = pl.ds(pl.multiple_of((1 - lax.axis_index("cross")) * width, LANES), width)
    last = species * SECOND
    out[last:] = jnp.zeros((out.shape[0] - last, width), F32)
    for sp in range(species):
        rows = later_nodes(shift, halo[sp, :, other], field[sp, FIRST:BRICK_END, other])
        out[sp * SECOND : (sp + 1) * SECOND] = rows[:SECOND]
        out[last + sp : last + sp + 1] = rows[SECOND : SECOND + 1]


def rest_away(edges, halo, field, width):
    species = halo.shape[0]
    rows = species * SECOND + -(-species // SUB) * SUB
    return call(
        rest_kernel,
        jax.ShapeDtypeStruct((rows, width), F32),
        in_specs=[SMEM_SPEC, VMEM_SPEC, VMEM_SPEC],
        out_specs=VMEM_SPEC,
        cost=20_000_000,
    )(edges, halo, field)


def detail_kernel(local, edges, factors, first, second, *rest):
    out, wide = rest[-2:]
    species = out.shape[1]
    width = out.shape[2]
    weights = factors[:, : 3 * HELD]
    shift = edges[0, 0] - lax.axis_index("slab") * TILE
    for sp in range(species):
        if local:
            more = later_nodes(shift, first[sp], second[sp, FIRST:BRICK_END])
            pieces = [second[sp, :FIRST], more[: SECOND + HALO]]
        else:
            last = species * SECOND
            end = pltpu.roll(second[last : last + SUB], (SUB - sp) % SUB, 0)
            pieces = [first[sp], second[sp * SECOND : (sp + 1) * SECOND], end, end]
        stack = jnp.concatenate(terms_of(jnp.concatenate(pieces, axis=0)), axis=0)
        result = jnp.dot(weights, stack, preferred_element_type=F32)
        result = result[:TILE] + result[TILE : 2 * TILE] + result[2 * TILE :]
        for t in range(width // LANES):
            wide[t, pl.ds(sp, TILE, stride=species)] = result[:, t * LANES : (t + 1) * LANES]
    for t in range(width // LANES):
        for k in range(DETAILS):
            out[k, :, t * LANES : (t + 1) * LANES] = wide[t, k * species : (k + 1) * species]


def details(local, edges, factors, first, second, width, species, lines, onto=None, part=None):
    chunk = min(width, 512)
    steps = width // chunk
    begin, count = (0, steps) if part is None else (part, 1)

    def here(i):
        i = i + begin
        return i if width == lines else lax.axis_index("cross") * steps + i

    def there(i):
        return (1 - lax.axis_index("cross")) * steps + i + begin

    if local:
        specs = [
            pl.BlockSpec((species, HALO, chunk), lambda i: (0, 0, here(i))),
            pl.BlockSpec((species, HELD, chunk), lambda i: (0, 0, here(i))),
        ]
    else:
        specs = [
            pl.BlockSpec((species, FIRST, chunk), lambda i: (0, 0, i + begin)),
            pl.BlockSpec((second.shape[0], chunk), lambda i: (0, i + begin)),
        ]
    specs = [SMEM_SPEC, pl.BlockSpec((3 * TILE, 2 * LANES), lambda i: (0, 0))] + specs
    operands = [edges, factors, first, second]
    alias = {}
    if onto is not None:
        specs.append(HBM_SPEC)
        operands.append(onto)
        alias = {4: 0}
    return call(
        functools.partial(detail_kernel, local),
        jax.ShapeDtypeStruct((DETAILS, species, lines), F32),
        grid=(count,),
        in_specs=specs,
        out_specs=pl.BlockSpec((DETAILS, species, chunk), lambda i: (0, 0, here(i) if local else there(i))),
        scratch_shapes=[pltpu.VMEM((chunk // LANES, TILE * species, LANES), F32)],
        input_output_aliases=alias,
        cost=20_000_000,
    )(*operands)


def merged(lower, upper):
    lower_values, lower_widths = lower
    upper_values, upper_widths = upper
    shared = 0.5 * (lower_values[-1] + upper_values[0])
    values = lower_values[:-1] + [shared] + upper_values[1:]
    widths = lower_widths + upper_widths
    left, right = widths[0::2], widths[1::2]
    pairs = len(left)
    total = [a + b for a, b in zip(left, right)]
    detail = []
    for i in range(pairs):
        inverse = 1.0 / total[i]
        detail.append(
            values[2 * i + 1] - ((right[i] * inverse) * values[2 * i] + (left[i] * inverse) * values[2 * i + 2])
        )
    loads = []
    for k in range(pairs + 1):
        term = None
        if k < pairs:
            term = (left[k] / 6.0 + right[k] / 3.0) * detail[k]
        if k > 0:
            other = (right[k - 1] / 6.0 + left[k - 1] / 3.0) * detail[k - 1]
            term = other if term is None else term + other
        loads.append(term)
    ratio, solved = [], []
    for k in range(pairs + 1):
        diag = (total[k - 1] if k else 0.0) + (total[k] if k < pairs else 0.0)
        diag = diag / 3.0
        if k:
            off = total[k - 1] / 6.0
            pivot = 1.0 / (diag - off * ratio[-1])
            solved.append((loads[k] - off * solved[-1]) * pivot)
        else:
            pivot = 1.0 / diag
            solved.append(loads[k] * pivot)
        if k < pairs:
            ratio.append(total[k] / 6.0 * pivot)
    for k in range(pairs - 1, -1, -1):
        solved[k] = solved[k] - ratio[k] * solved[k + 1]
    coarse = [values[2 * k] + solved[k] for k in range(pairs + 1)]
    return coarse, detail, total


def values_at(ref, first, rows):
    return [ref[pl.ds(first + k * rows, rows)] for k in range(COARSE)]


def widths_at(ref, first):
    return [ref[pl.ds(first + i, 1)] for i in range(COARSE - 1)]


def put(ref, first, rows, values):
    for k, value in enumerate(values):
        ref[pl.ds(first + k * rows, rows)] = value


def put_widths(ref, first, widths):
    put(ref, first, 1, widths)
    ref[first + COARSE - 1 : first + SUB] = jnp.zeros((SUB - COARSE + 1, LANES), F32)


def in_order(upper_side, mine, theirs):
    def pick(first, second):
        return [jnp.where(upper_side, a, b) for a, b in zip(first, second)]

    lower = (pick(theirs[0], mine[0]), pick(theirs[1], mine[1]))
    upper = (pick(mine[0], theirs[0]), pick(mine[1], theirs[1]))
    return merged(lower, upper)


def merge_kernel(level, depth, rows, swapped, *refs):
    slab = lax.axis_index("slab")
    core = slab & 1
    chip = slab & ~1
    upper_side = (slab >> level) & 1 == 1
    last = level == depth - 1
    set_rows = COARSE * rows + SUB
    detail_rows = (COARSE - 1) * rows
    own, other = refs[0], refs[1]
    outs = refs[-2:]

    def state(ref):
        values = values_at(ref, 0, rows) + widths_at(ref, COARSE * rows)
        if level > 0:
            values += [ref[pl.ds(set_rows + i * rows, rows)] for i in range(COARSE - 1)]
        if level > 1:
            values += [ref[pl.ds(set_rows + detail_rows + i * rows, rows)] for i in range(COARSE - 1)]
        return values

    held = state(own)
    if swapped and last:
        home = core == lax.axis_index("cross")
        held = [jnp.where(home, a, b) for a, b in zip(held, state(refs[2]))]
    mine = (held[:COARSE], held[COARSE : 2 * COARSE - 1])
    odd = held[2 * COARSE - 1 : 3 * COARSE - 2]
    even = held[3 * COARSE - 2 :]
    theirs = (values_at(other, 0, rows), widths_at(other, COARSE * rows))

    def pick(first, second):
        return [jnp.where(upper_side, a, b) for a, b in zip(first, second)]

    lower = (pick(theirs[0], mine[0]), pick(theirs[1], mine[1]))
    upper = (pick(mine[0], theirs[0]), pick(mine[1], theirs[1]))
    coarse, detail, widths = merged(lower, upper)
    if level == 0:
        odd = detail
    else:
        keep = ((chip >> level) & 1 == 1) & (chip & ((1 << level) - 1) == 0)
        if last:
            keep = keep | (chip == 0)
        even = even if level > 1 else [0.0] * (COARSE - 1)
        even = [jnp.where(keep, a, b) for a, b in zip(detail, even)]
    if last:
        here, away = outs
        put(here, 0, rows, coarse)
        put(away, 0, rows, coarse)
        put(here, COARSE * rows, rows, [jnp.where(core == 0, a, b) for a, b in zip(even, odd)])
        put(away, COARSE * rows, rows, [jnp.where(core == 0, b, a) for a, b in zip(even, odd)])
        return
    send, carried = outs
    for ref in (send, carried):
        put(ref, 0, rows, coarse)
        put_widths(ref, COARSE * rows, widths)
    put(carried, set_rows, rows, odd)
    if level > 0:
        put(carried, set_rows + detail_rows, rows, even)


def merge(level, depth, rows, swapped, *operands):
    set_rows = COARSE * rows + SUB
    detail_rows = (COARSE - 1) * rows
    if level == depth - 1:
        sizes = ((2 * COARSE - 1) * rows,) * 2
    else:
        sizes = (set_rows, set_rows + min(level + 1, 2) * detail_rows)
    return call(
        functools.partial(merge_kernel, level, depth, rows, swapped),
        tuple(jax.ShapeDtypeStruct((size, LANES), F32) for size in sizes),
        in_specs=[VMEM_SPEC] * len(operands),
        out_specs=(VMEM_SPEC,) * 2,
    )(*operands)


def finish_kernel(own, other, tree, final, turned):
    core = lax.axis_index("slab") & 1
    species, _, lines = tree.shape
    width = lines // 2
    per = width // LANES
    group = COARSE - 1
    for block, ref in ((core, own), (1 - core, other)):

        def lanes(t):
            return pl.ds(pl.multiple_of(block * width + t * LANES, LANES), LANES)

        for k in range(COARSE):
            for sp in range(species):
                turned[pl.ds(sp, per, stride=species)] = ref[(k * species + sp) * per : (k * species + sp + 1) * per]
            for t in range(per):
                final[k, :, lanes(t)] = turned[t * species : (t + 1) * species]
        for sp in range(species):
            for i in range(group):
                at = ((COARSE + i) * species + sp) * per
                turned[pl.ds(i, per, stride=group)] = ref[at : at + per]
            for t in range(per):
                tree[sp, :, lanes(t)] = turned[t * group : (t + 1) * group]


def finish(own, other, species, lines):
    return call(
        finish_kernel,
        (
            jax.ShapeDtypeStruct((species, COARSE - 1, lines), F32),
            jax.ShapeDtypeStruct((COARSE, species, lines), F32),
        ),
        in_specs=[VMEM_SPEC] * 2,
        out_specs=(VMEM_SPEC,) * 2,
        scratch_shapes=[pltpu.VMEM((lines // 2 // LANES * SUB, LANES), F32)],
    )(own, other)


def from_partner(block, axis, step):
    count = lax.axis_size(axis)
    return lax.ppermute(block, axis, [(i, i ^ step) for i in range(count)])


def shifted(block, axis):
    count = lax.axis_size(axis)
    return lax.ppermute(block, axis, [(i, i + 1) for i in range(count - 1)])


def exchanged(block, axis):
    species, rows, lines = block.shape
    count = lax.axis_size(axis)
    parts = block.reshape(species, rows, count, lines // count)
    return lax.all_to_all(parts, axis, split_axis=2, concat_axis=2, tiled=True).reshape(block.shape)


def last_routes(slabs):
    partner, own = [], []
    for s in range(slabs):
        for c in range(2):
            home = (s & 1) == c
            target = (s, c) if home else (s ^ 1, 1 - c)
            partner.append((s * 2 + c, (target[0] ^ (slabs // 2)) * 2 + target[1]))
            if not home:
                own.append((s * 2 + c, target[0] * 2 + target[1]))
    return partner, own


def on_device(sim_field, brick_edges, cell_width):
    species, _, lines = sim_field.shape
    cross_count = lax.axis_size("cross")
    slabs = lax.axis_size("slab")
    depth = slabs.bit_length() - 1
    width = lines // cross_count
    rows = species * (lines // 2) // LANES
    swapped = cross_count == 2
    both = ("slab", "cross")

    field = sim_field
    halo = shifted(brick_tail(brick_edges, field), "slab")
    if swapped:
        first_in = from_partner(first_rows(field, width), "cross", 1)
    factors, weights, coarse_width = tile_matrix(brick_edges, cell_width)
    part = brick_part(weights, coarse_width, field)
    halo, part, factors = lax.optimization_barrier((halo, part, factors))
    own_half, other_half = coarse_sets(weights, halo, part)
    halo, other_half = lax.optimization_barrier((halo, other_half))
    if swapped:
        rest = rest_away(brick_edges, halo, field, width)
        halo, rest = lax.optimization_barrier((halo, rest))
        rest_in = from_partner(rest, "cross", 1)

    if swapped:
        near = details(True, brick_edges, factors, halo, field, width, species, lines)
    send, carried = other_half, own_half
    for level in range(depth):
        last = level == depth - 1
        if swapped and level == depth - 2:
            send, near = lax.optimization_barrier((send, near))
        if swapped and last:
            partner_route, own_route = last_routes(slabs)
            operands = (carried, lax.ppermute(send, both, partner_route), lax.ppermute(carried, both, own_route))
            tile_detail = details(False, brick_edges, factors, first_in, rest_in, width, species, lines, near)
            operands, tile_detail = lax.optimization_barrier((operands, tile_detail))
        else:
            operands = (carried, from_partner(send, "slab", 1 << level))
        send, carried = merge(level, depth, rows, swapped, *operands)
    here_set, away_set = send, carried
    partner_set = from_partner(away_set, "slab", 1)

    if swapped:
        tree_detail, coarse_final = finish(here_set, partner_set, species, lines)
        coarse_final = coarse_final.transpose(1, 0, 2)
    else:
        core = lax.axis_index("slab") % 2
        first = jnp.where(core == 0, here_set, partner_set)
        second = jnp.where(core == 0, partner_set, here_set)
        ended = jnp.stack([first, second]).reshape(2, 2 * COARSE - 1, species, lines // 2)
        ended = ended.transpose(2, 1, 0, 3).reshape(species, 2 * COARSE - 1, lines)
        ended = exchanged(ended, "cross")
        coarse_final, tree_detail = ended[:, :COARSE], ended[:, COARSE:]
        moved = exchanged(jnp.concatenate([halo, sim_field[:, :HELD]], axis=1), "cross")
        tile_detail = details(True, brick_edges, factors, moved[:, :HALO], moved[:, HALO:], lines, species, lines)
    return (tile_detail.transpose(1, 0, 2), tree_detail, coarse_final)


def solution(mesh):
    placed = (P(None, "slab", "cross"), P("slab", None), P("slab"))
    return jax.shard_map(
        on_device,
        mesh=mesh,
        in_specs=placed,
        out_specs=(P(None, "slab", "cross"), P(None, "slab", "cross"), P(None, None, "cross")),
        check_vma=False,
    )
```

```python
import functools

import jax
import jax.numpy as jnp
from jax import lax
from jax.experimental import pallas as pl
from jax.experimental.pallas import tpu as pltpu
from jax.sharding import PartitionSpec as P

TILE = 64
HALO = 16
LEVELS = 4
COARSE = 5
DETAILS = TILE - COARSE + 1
LANES = 128
SUB = 8
HELD = TILE + HALO
FIRST = 48
SECOND = TILE - FIRST
F32 = jnp.float32
BF16 = jnp.bfloat16
HIGHEST = lax.Precision.HIGHEST


def call(kernel, out_shape, *, vmem=8 << 20, cost=None, **kw):
    params = pltpu.CompilerParams(vmem_limit_bytes=vmem)
    if cost is not None:
        kw["cost_estimate"] = pl.CostEstimate(flops=cost, bytes_accessed=cost // 100, transcendentals=0)
    return pl.pallas_call(kernel, out_shape=out_shape, compiler_params=params, **kw)


VMEM_SPEC = pl.BlockSpec(memory_space=pltpu.VMEM)
SMEM_SPEC = pl.BlockSpec(memory_space=pltpu.SMEM)
HBM_SPEC = pl.BlockSpec(memory_space=pltpu.HBM)


LOW = TILE // 2


def tail_kernel(edges, rows, tail):
    start = edges[0, 1] - edges[0, 0] - HALO - LOW
    rest = start & (SUB - 1)
    whole = pl.multiple_of(start - rest, SUB)
    for sp in range(tail.shape[0]):
        window = rows[sp, pl.ds(whole, HALO + SUB), :]
        tail[sp] = pltpu.roll(window, (HALO + SUB - rest) % (HALO + SUB), 0)[:HALO]


def brick_tail(edges, field):
    species, _, lines = field.shape
    return call(
        tail_kernel,
        jax.ShapeDtypeStruct((species, HALO, lines), F32),
        in_specs=[SMEM_SPEC, VMEM_SPEC],
        out_specs=VMEM_SPEC,
    )(edges, field[:, LOW : LOW + TILE])


def first_kernel(field, away):
    species, _, width = away.shape
    other = pl.ds(pl.multiple_of((1 - lax.axis_index("cross")) * width, LANES), width)
    for sp in range(species):
        away[sp] = field[sp, :FIRST, other]


def first_rows(field, width):
    return call(
        first_kernel,
        jax.ShapeDtypeStruct((field.shape[0], FIRST, width), F32),
        in_specs=[VMEM_SPEC],
        out_specs=VMEM_SPEC,
    )(field)


PAD = 32


def matrix_kernel(edges, widths, factors, coarse, coarse_width, nodes, cell, low, main, up, load, stored):
    slab = lax.axis_index("slab")
    shift = edges[0, 0] - slab * TILE
    rows, lanes = nodes.shape[1], nodes.shape[0] * LANES
    node = lax.broadcasted_iota(jnp.int32, (rows, lanes), 0)
    lane = lax.broadcasted_iota(jnp.int32, (rows, lanes), 1)
    column = lane % HELD
    later = column - FIRST
    held = jnp.where(column < FIRST, column + shift, jnp.where(later < shift, later, column))
    plain = lane - 2 * LANES
    from_halo = jnp.where((slab == 0) & (plain < HALO), plain + TILE, plain - HALO + shift)
    grouped = (lane < 3 * HELD) & (column <= TILE)
    held = jnp.where(lane < 2 * LANES, jnp.where(grouped, held, -1), jnp.where(plain < HELD, from_halo, -1))
    chosen = ((held == node) & (node <= TILE)).astype(F32)
    for j in range(lanes // LANES):
        nodes[j] = chosen[:, j * LANES : (j + 1) * LANES]
    cell[...] = jnp.zeros_like(cell)
    cell[:TILE] = widths[...]
    for ref in (low, up, load):
        ref[...] = jnp.zeros_like(ref)
    main[...] = jnp.ones_like(main)
    stored[...] = jnp.zeros_like(stored)
    wide = lambda x: jnp.concatenate([x] * (lanes // LANES), axis=1)
    placed = 0
    pairs = TILE // 2
    for _ in range(LEVELS):
        size = -(-(pairs + 1) // SUB) * SUB
        here = pl.ds(PAD, size)
        inside = lax.broadcasted_iota(jnp.int32, (size, LANES), 0) < pairs
        left = cell[pl.ds(0, size, stride=2)]
        right = cell[pl.ds(1, size, stride=2)]
        total = left + right
        safe = jnp.where(inside, total, 1.0)
        even, odd, after = [
            jnp.concatenate([nodes[j, pl.ds(i, size, stride=2)] for j in range(lanes // LANES)], axis=1)
            for i in range(3)
        ]
        inverse = 1.0 / safe
        detail = odd - (wide(right * inverse) * even + wide(left * inverse) * after)
        detail = jnp.where(wide(inside), detail, 0.0)
        stored[placed : placed + pairs] = detail[:pairs]
        placed += pairs
        load[here] = wide(right / 6.0 + left / 3.0) * detail
        load[pl.ds(PAD - 1, 1)] = jnp.zeros((1, lanes), F32)
        grown = wide(left / 6.0 + right / 3.0) * detail + load[pl.ds(PAD - 1, size)]
        up[here] = total
        before = up[pl.ds(PAD - 1, size)]
        held_rows = lax.broadcasted_iota(jnp.int32, (size, LANES), 0) <= pairs
        diag = jnp.where(held_rows, (before + total) / 3.0, 1.0)
        lower = jnp.where(held_rows, before / 6.0, 0.0)
        upper = total / 6.0
        step = 1
        while step <= pairs:
            low[here] = lower
            up[here] = upper
            main[here] = 1.0 / diag
            load[here] = grown
            back = pl.ds(PAD - step, size)
            fore = pl.ds(PAD + step, size)
            alpha = -lower * main[back]
            gamma = -upper * main[fore]
            diag = diag + alpha * up[back] + gamma * low[fore]
            grown = grown + wide(alpha) * load[back] + wide(gamma) * load[fore]
            lower = alpha * low[back]
            upper = gamma * up[fore]
            step *= 2
        result = even + grown * wide(1.0 / diag)
        result = jnp.where(wide(held_rows), result, 0.0)
        nodes[...] = jnp.zeros_like(nodes)
        for j in range(lanes // LANES):
            nodes[j, :size] = result[:, j * LANES : (j + 1) * LANES]
        cell[...] = jnp.zeros_like(cell)
        cell[:size] = total
        pairs //= 2
    coarse[...] = nodes[2, :SUB]
    coarse_width[...] = cell[:SUB]
    matrix = stored[:, : 2 * LANES]
    lane = lax.broadcasted_iota(jnp.int32, matrix.shape, 1)
    for i in range(3):
        term = matrix.astype(BF16)
        matrix = matrix - term.astype(F32)
        factors[i * TILE : (i + 1) * TILE] = jnp.where(lane < (3 - i) * HELD, term.astype(F32), 0.0).astype(BF16)


def tile_matrix(edges, cell_width):
    widths = jnp.broadcast_to(cell_width[:, None], (TILE, LANES))
    narrow = pltpu.VMEM((PAD + 40 + PAD, LANES), F32)
    broad = pltpu.VMEM((PAD + 40 + PAD, 3 * LANES), F32)
    return call(
        matrix_kernel,
        (
            jax.ShapeDtypeStruct((3 * TILE, 2 * LANES), BF16),
            jax.ShapeDtypeStruct((SUB, LANES), F32),
            jax.ShapeDtypeStruct((SUB, LANES), F32),
        ),
        in_specs=[SMEM_SPEC, VMEM_SPEC],
        out_specs=(VMEM_SPEC,) * 3,
        scratch_shapes=[
            pltpu.VMEM((3, 88, LANES), F32),
            pltpu.VMEM((88, LANES), F32),
            narrow,
            narrow,
            narrow,
            broad,
            pltpu.VMEM((TILE, 3 * LANES), F32),
        ],
    )(edges, widths)


def to_dense(result, turned, sets, sp, species):
    blocks = result.shape[1] // LANES
    per = blocks // 2
    for t in range(blocks):
        turned[t * SUB : (t + 1) * SUB] = result[:, t * LANES : (t + 1) * LANES]
    for half in range(2):
        for k in range(COARSE):
            at = ((half * COARSE + k) * species + sp) * per
            sets[pl.ds(at if isinstance(sp, int) else pl.multiple_of(at, per), per)] = turned[
                pl.ds(half * per * SUB + k, per, stride=SUB)
            ]


def brick_kernel(weights, coarse_width, field, sets, turned):
    sp = pl.program_id(0)
    slab = lax.axis_index("slab")
    own = weights[...]
    result = jnp.dot(own[:, HALO:HELD], field[0, :TILE], precision=HIGHEST, preferred_element_type=F32)
    row = jnp.where(slab == 0, field[0, TILE:HELD], 0.0)
    result += jnp.dot(own[:, :HALO], row, precision=HIGHEST, preferred_element_type=F32)
    to_dense(result, turned, sets, sp, pl.num_programs(0))

    @pl.when(sp == 0)
    def _():
        sets[sets.shape[0] - SUB :] = coarse_width[...]


def brick_part(weights, coarse_width, field):
    species, _, lines = field.shape
    dense = COARSE * species * lines // LANES + SUB
    return call(
        brick_kernel,
        jax.ShapeDtypeStruct((dense, LANES), F32),
        grid=(species,),
        in_specs=[
            pl.BlockSpec((SUB, LANES), lambda i: (0, 0)),
            pl.BlockSpec((SUB, LANES), lambda i: (0, 0)),
            pl.BlockSpec((1, HELD, lines), lambda i: (i, 0, 0)),
        ],
        out_specs=pl.BlockSpec((dense, LANES), lambda i: (0, 0)),
        scratch_shapes=[pltpu.VMEM((lines // LANES * SUB, LANES), F32)],
    )(weights, coarse_width, field)


def terms_of(value):
    terms = []
    for _ in range(3):
        terms.append(value.astype(BF16))
        value = value - terms[-1].astype(F32)
    return terms


def halo_kernel(weights, halo, part, own_half, other_half, turned, fresh):
    species = halo.shape[0]
    slab = lax.axis_index("slab")
    weight_terms = terms_of(weights[:, :HALO])
    zero = jnp.zeros_like(weights[:, :HALO])
    own = jnp.concatenate(
        [jnp.concatenate([weight_terms[i].astype(F32)] * (3 - i) + [zero] * i, axis=1) for i in range(3)], axis=0
    ).astype(BF16)
    for sp in range(species):
        stack = jnp.concatenate(terms_of(halo[sp]), axis=0)
        result = jnp.dot(own, stack, preferred_element_type=F32)
        result = result[:SUB] + result[SUB : 2 * SUB] + result[2 * SUB :]
        to_dense(result, turned, fresh, sp, species)
    rows = fresh.shape[0] // 2
    for ref, half in ((own_half, slab & 1), (other_half, 1 - (slab & 1))):
        here = pl.ds(pl.multiple_of(half * rows, SUB), rows)
        ref[:rows] = part[here] + jnp.where(slab == 0, 0.0, fresh[here])
        ref[rows:] = part[2 * rows :]


def coarse_sets(weights, halo, part):
    lines = halo.shape[2]
    rows = part.shape[0] - SUB
    half = jax.ShapeDtypeStruct((rows // 2 + SUB, LANES), F32)
    return call(
        halo_kernel,
        (half, half),
        in_specs=[VMEM_SPEC] * 3,
        out_specs=(VMEM_SPEC,) * 2,
        scratch_shapes=[
            pltpu.VMEM((lines // LANES * SUB, LANES), F32),
            pltpu.VMEM((rows, LANES), F32),
        ],
    )(weights, halo, part)


def later_nodes(shift, halo, brick):
    rows = jnp.concatenate([halo, brick], axis=0)
    count = rows.shape[0]
    return pltpu.roll(rows, (count - HALO + shift) % count, 0)


BRICK_END = TILE + SUB


def rest_kernel(edges, halo, field, out):
    species = halo.shape[0]
    shift = edges[0, 0] - lax.axis_index("slab") * TILE
    each = species * (SECOND + 1)
    width = out.shape[0] // each * LANES
    other = pl.ds(pl.multiple_of((1 - lax.axis_index("cross")) * width, LANES), width)
    for sp in range(species):
        rows = later_nodes(shift, halo[sp, :, other], field[sp, FIRST:BRICK_END, other])
        for t in range(width // LANES):
            tile = rows[:, t * LANES : (t + 1) * LANES]
            out[t * each + sp * SECOND : t * each + (sp + 1) * SECOND] = tile[:SECOND]
            last = t * each + species * SECOND + sp
            out[last : last + 1] = tile[SECOND : SECOND + 1]


def rest_away(edges, halo, field, width):
    species = halo.shape[0]
    rows = species * (SECOND + 1) * width // LANES
    return call(
        rest_kernel,
        jax.ShapeDtypeStruct((rows, LANES), F32),
        in_specs=[SMEM_SPEC, VMEM_SPEC, VMEM_SPEC],
        out_specs=VMEM_SPEC,
        cost=20_000_000,
    )(edges, halo, field)


def detail_kernel(local, whole, edges, factors, first, second, *rest):
    out, wide = rest[-2:]
    species = out.shape[1]
    width = out.shape[2]
    weights = factors[:, : 3 * HELD]
    step = pl.program_id(0)
    if local and not whole:
        step += lax.axis_index("cross") * pl.num_programs(0)
    lanes = pl.ds(pl.multiple_of(step * width, LANES), width)
    shift = edges[0, 0] - lax.axis_index("slab") * TILE
    for sp in range(species):
        if local:
            more = later_nodes(shift, first[sp, :, lanes], second[sp, FIRST:BRICK_END, lanes])
            pieces = [second[sp, :FIRST, lanes], more[: SECOND + HALO]]
        else:
            each = species * (SECOND + 1)
            base = step * (width // LANES * each)

            def rows_of(at, count):
                return jnp.concatenate(
                    [second[pl.ds(base + t * each + at, count)] for t in range(width // LANES)], axis=1
                )

            end = rows_of(species * SECOND + sp, 1)
            end = jnp.concatenate([end, jnp.zeros((HALO - 1, width), F32)], axis=0)
            pieces = [first[sp, :, lanes], rows_of(sp * SECOND, SECOND), end]
        stack = jnp.concatenate(terms_of(jnp.concatenate(pieces, axis=0)), axis=0)
        result = jnp.dot(weights, stack, preferred_element_type=F32)
        result = result[:TILE] + result[TILE : 2 * TILE] + result[2 * TILE :]
        for t in range(width // LANES):
            wide[t, pl.ds(sp, TILE, stride=species)] = result[:, t * LANES : (t + 1) * LANES]
    for t in range(width // LANES):
        for k in range(DETAILS):
            out[k, :, t * LANES : (t + 1) * LANES] = wide[t, k * species : (k + 1) * species]


def details(local, edges, factors, first, second, width, species, lines, onto=None):
    chunk = min(width, 512)
    steps = width // chunk

    def here(i):
        return i if width == lines else lax.axis_index("cross") * steps + i

    def there(i):
        return (1 - lax.axis_index("cross")) * steps + i

    specs = [SMEM_SPEC] + [VMEM_SPEC] * 3
    operands = [edges, factors, first, second]
    alias = {}
    if onto is not None:
        specs.append(HBM_SPEC)
        operands.append(onto)
        alias = {4: 0}
    return call(
        functools.partial(detail_kernel, local, width == lines),
        jax.ShapeDtypeStruct((DETAILS, species, lines), F32),
        grid=(steps,),
        in_specs=specs,
        out_specs=pl.BlockSpec((DETAILS, species, chunk), lambda i: (0, 0, here(i) if local else there(i))),
        scratch_shapes=[pltpu.VMEM((chunk // LANES, TILE * species, LANES), F32)],
        input_output_aliases=alias,
        cost=20_000_000,
    )(*operands)


def merged(lower, upper):
    lower_values, lower_widths = lower
    upper_values, upper_widths = upper
    shared = 0.5 * (lower_values[-1] + upper_values[0])
    values = lower_values[:-1] + [shared] + upper_values[1:]
    widths = lower_widths + upper_widths
    left, right = widths[0::2], widths[1::2]
    pairs = len(left)
    total = [a + b for a, b in zip(left, right)]
    detail = []
    for i in range(pairs):
        inverse = 1.0 / total[i]
        detail.append(
            values[2 * i + 1] - ((right[i] * inverse) * values[2 * i] + (left[i] * inverse) * values[2 * i + 2])
        )
    loads = []
    for k in range(pairs + 1):
        term = None
        if k < pairs:
            term = (left[k] / 6.0 + right[k] / 3.0) * detail[k]
        if k > 0:
            other = (right[k - 1] / 6.0 + left[k - 1] / 3.0) * detail[k - 1]
            term = other if term is None else term + other
        loads.append(term)
    ratio, solved = [], []
    for k in range(pairs + 1):
        diag = (total[k - 1] if k else 0.0) + (total[k] if k < pairs else 0.0)
        diag = diag / 3.0
        if k:
            off = total[k - 1] / 6.0
            pivot = 1.0 / (diag - off * ratio[-1])
            solved.append((loads[k] - off * solved[-1]) * pivot)
        else:
            pivot = 1.0 / diag
            solved.append(loads[k] * pivot)
        if k < pairs:
            ratio.append(total[k] / 6.0 * pivot)
    for k in range(pairs - 1, -1, -1):
        solved[k] = solved[k] - ratio[k] * solved[k + 1]
    coarse = [values[2 * k] + solved[k] for k in range(pairs + 1)]
    return coarse, detail, total


def values_at(ref, first, rows):
    return [ref[pl.ds(first + k * rows, rows)] for k in range(COARSE)]


def widths_at(ref, first):
    return [ref[pl.ds(first + i, 1)] for i in range(COARSE - 1)]


def put(ref, first, rows, values):
    for k, value in enumerate(values):
        ref[pl.ds(first + k * rows, rows)] = value


def put_widths(ref, first, widths):
    put(ref, first, 1, widths)
    ref[first + COARSE - 1 : first + SUB] = jnp.zeros((SUB - COARSE + 1, LANES), F32)


def in_order(upper_side, mine, theirs):
    def pick(first, second):
        return [jnp.where(upper_side, a, b) for a, b in zip(first, second)]

    lower = (pick(theirs[0], mine[0]), pick(theirs[1], mine[1]))
    upper = (pick(mine[0], theirs[0]), pick(mine[1], theirs[1]))
    return merged(lower, upper)


def merge_kernel(level, depth, rows, swapped, *refs):
    slab = lax.axis_index("slab")
    core = slab & 1
    chip = slab & ~1
    upper_side = (slab >> level) & 1 == 1
    last = level == depth - 1
    set_rows = COARSE * rows + SUB
    detail_rows = (COARSE - 1) * rows
    own, other = refs[0], refs[1]
    outs = refs[-2:]

    def state(ref):
        values = values_at(ref, 0, rows) + widths_at(ref, COARSE * rows)
        if level > 0:
            values += [ref[pl.ds(set_rows + i * rows, rows)] for i in range(COARSE - 1)]
        if level > 1:
            values += [ref[pl.ds(set_rows + detail_rows + i * rows, rows)] for i in range(COARSE - 1)]
        return values

    held = state(own)
    if swapped and last:
        home = core == lax.axis_index("cross")
        held = [jnp.where(home, a, b) for a, b in zip(held, state(refs[2]))]
    mine = (held[:COARSE], held[COARSE : 2 * COARSE - 1])
    odd = held[2 * COARSE - 1 : 3 * COARSE - 2]
    even = held[3 * COARSE - 2 :]
    theirs = (values_at(other, 0, rows), widths_at(other, COARSE * rows))

    def pick(first, second):
        return [jnp.where(upper_side, a, b) for a, b in zip(first, second)]

    lower = (pick(theirs[0], mine[0]), pick(theirs[1], mine[1]))
    upper = (pick(mine[0], theirs[0]), pick(mine[1], theirs[1]))
    coarse, detail, widths = merged(lower, upper)
    if level == 0:
        odd = detail
    else:
        keep = ((chip >> level) & 1 == 1) & (chip & ((1 << level) - 1) == 0)
        if last:
            keep = keep | (chip == 0)
        even = even if level > 1 else [0.0] * (COARSE - 1)
        even = [jnp.where(keep, a, b) for a, b in zip(detail, even)]
    if last:
        here, away = outs
        put(here, 0, rows, coarse)
        put(away, 0, rows, coarse)
        put(here, COARSE * rows, rows, [jnp.where(core == 0, a, b) for a, b in zip(even, odd)])
        put(away, COARSE * rows, rows, [jnp.where(core == 0, b, a) for a, b in zip(even, odd)])
        return
    send, carried = outs
    for ref in (send, carried):
        put(ref, 0, rows, coarse)
        put_widths(ref, COARSE * rows, widths)
    put(carried, set_rows, rows, odd)
    if level > 0:
        put(carried, set_rows + detail_rows, rows, even)


def merge(level, depth, rows, swapped, *operands):
    set_rows = COARSE * rows + SUB
    detail_rows = (COARSE - 1) * rows
    if level == depth - 1:
        sizes = ((2 * COARSE - 1) * rows,) * 2
    else:
        sizes = (set_rows, set_rows + min(level + 1, 2) * detail_rows)
    return call(
        functools.partial(merge_kernel, level, depth, rows, swapped),
        tuple(jax.ShapeDtypeStruct((size, LANES), F32) for size in sizes),
        in_specs=[VMEM_SPEC] * len(operands),
        out_specs=(VMEM_SPEC,) * 2,
    )(*operands)


def in_outputs_order(part, tree, final, turned):
    species, group, width = tree.shape
    per = width // LANES
    for k in range(COARSE):
        for sp in range(species):
            turned[pl.ds(sp, per, stride=species)] = part[(k * species + sp) * per : (k * species + sp + 1) * per]
        for t in range(per):
            final[k, :, t * LANES : (t + 1) * LANES] = turned[t * species : (t + 1) * species]
    for sp in range(species):
        for i in range(group):
            at = ((COARSE + i) * species + sp) * per
            turned[pl.ds(i, per, stride=group)] = part[at : at + per]
        for t in range(per):
            tree[sp, :, t * LANES : (t + 1) * LANES] = turned[t * group : (t + 1) * group]


def finish_kernel(own_tree, own_final, other, tree, final, other_tree, other_final, turned, sems):
    core = lax.axis_index("slab") & 1
    width = own_tree.shape[2]

    def to(ref, source, block, sem):
        lanes = pl.ds(pl.multiple_of(block * width, LANES), width)
        copy = pltpu.make_async_copy(source, ref.at[:, :, lanes], sem)
        copy.start()
        return copy

    copies = [to(tree, own_tree, core, sems.at[0]), to(final, own_final, core, sems.at[1])]
    in_outputs_order(other, other_tree, other_final, turned)
    copies += [to(tree, other_tree, 1 - core, sems.at[2]), to(final, other_final, 1 - core, sems.at[3])]
    for copy in copies:
        copy.wait()


def finish(own, other, species, lines):
    half = lines // 2
    shapes = ((species, COARSE - 1, half), (COARSE, species, half))
    turned = pltpu.VMEM((half // LANES * SUB, LANES), F32)
    placed = call(
        in_outputs_order,
        tuple(jax.ShapeDtypeStruct(shape, F32) for shape in shapes),
        in_specs=[VMEM_SPEC],
        out_specs=(VMEM_SPEC,) * 2,
        scratch_shapes=[turned],
    )(own)
    return call(
        finish_kernel,
        tuple(jax.ShapeDtypeStruct(shape[:2] + (lines,), F32) for shape in shapes),
        in_specs=[VMEM_SPEC] * 3,
        out_specs=(HBM_SPEC,) * 2,
        scratch_shapes=[pltpu.VMEM(shape, F32) for shape in shapes] + [turned, pltpu.SemaphoreType.DMA((4,))],
    )(*placed, other)


def from_partner(block, axis, step):
    count = lax.axis_size(axis)
    return lax.ppermute(block, axis, [(i, i ^ step) for i in range(count)])


def shifted(block, axis):
    count = lax.axis_size(axis)
    return lax.ppermute(block, axis, [(i, i + 1) for i in range(count - 1)])


def exchanged(block, axis):
    species, rows, lines = block.shape
    count = lax.axis_size(axis)
    parts = block.reshape(species, rows, count, lines // count)
    return lax.all_to_all(parts, axis, split_axis=2, concat_axis=2, tiled=True).reshape(block.shape)


def last_routes(slabs):
    partner, own = [], []
    for s in range(slabs):
        for c in range(2):
            home = (s & 1) == c
            target = (s, c) if home else (s ^ 1, 1 - c)
            partner.append((s * 2 + c, (target[0] ^ (slabs // 2)) * 2 + target[1]))
            if not home:
                own.append((s * 2 + c, target[0] * 2 + target[1]))
    return partner, own


def on_device(sim_field, brick_edges, cell_width):
    species, _, lines = sim_field.shape
    cross_count = lax.axis_size("cross")
    slabs = lax.axis_size("slab")
    depth = slabs.bit_length() - 1
    width = lines // cross_count
    rows = species * (lines // 2) // LANES
    swapped = cross_count == 2
    both = ("slab", "cross")

    field = sim_field
    halo = shifted(brick_tail(brick_edges, field), "slab")
    if swapped:
        first_in = from_partner(first_rows(field, width), "cross", 1)
    factors, weights, coarse_width = tile_matrix(brick_edges, cell_width)
    part = brick_part(weights, coarse_width, field)
    halo, part, factors = lax.optimization_barrier((halo, part, factors))
    own_half, other_half = coarse_sets(weights, halo, part)
    halo, other_half = lax.optimization_barrier((halo, other_half))
    if swapped:
        rest = rest_away(brick_edges, halo, field, width)
        halo, rest = lax.optimization_barrier((halo, rest))
        rest_in = from_partner(rest, "cross", 1)

    if swapped:
        near = details(True, brick_edges, factors, halo, field, width, species, lines)
    send, carried = other_half, own_half
    for level in range(depth):
        last = level == depth - 1
        if swapped and level == depth - 2:
            send, near = lax.optimization_barrier((send, near))
        if swapped and last:
            partner_route, own_route = last_routes(slabs)
            operands = (carried, lax.ppermute(send, both, partner_route), lax.ppermute(carried, both, own_route))
            tile_detail = details(False, brick_edges, factors, first_in, rest_in, width, species, lines, near)
            operands, tile_detail = lax.optimization_barrier((operands, tile_detail))
        else:
            operands = (carried, from_partner(send, "slab", 1 << level))
        send, carried = merge(level, depth, rows, swapped, *operands)
    here_set, away_set = send, carried
    partner_set = from_partner(away_set, "slab", 1)

    if swapped:
        tree_detail, coarse_final = finish(here_set, partner_set, species, lines)
        coarse_final = coarse_final.transpose(1, 0, 2)
    else:
        core = lax.axis_index("slab") % 2
        first = jnp.where(core == 0, here_set, partner_set)
        second = jnp.where(core == 0, partner_set, here_set)
        ended = jnp.stack([first, second]).reshape(2, 2 * COARSE - 1, species, lines // 2)
        ended = ended.transpose(2, 1, 0, 3).reshape(species, 2 * COARSE - 1, lines)
        ended = exchanged(ended, "cross")
        coarse_final, tree_detail = ended[:, :COARSE], ended[:, COARSE:]
        moved = exchanged(jnp.concatenate([halo, sim_field[:, :HELD]], axis=1), "cross")
        tile_detail = details(True, brick_edges, factors, moved[:, :HALO], moved[:, HALO:], lines, species, lines)
    return (tile_detail.transpose(1, 0, 2), tree_detail, coarse_final)


def solution(mesh):
    placed = (P(None, "slab", "cross"), P("slab", None), P("slab"))
    return jax.shard_map(
        on_device,
        mesh=mesh,
        in_specs=placed,
        out_specs=(P(None, "slab", "cross"), P(None, "slab", "cross"), P(None, None, "cross")),
        check_vma=False,
    )
```

```python
import functools

import jax
import jax.numpy as jnp
from jax import lax
from jax.experimental import pallas as pl
from jax.experimental.pallas import tpu as pltpu
from jax.sharding import PartitionSpec as P

TILE = 64
HALO = 16
LEVELS = 4
COARSE = 5
DETAILS = TILE - COARSE + 1
LANES = 128
SUB = 8
HELD = TILE + HALO
FIRST = 48
SECOND = TILE - FIRST
F32 = jnp.float32
BF16 = jnp.bfloat16
HIGHEST = lax.Precision.HIGHEST


def call(kernel, out_shape, *, vmem=8 << 20, cost=None, **kw):
    params = pltpu.CompilerParams(vmem_limit_bytes=vmem)
    if cost is not None:
        kw["cost_estimate"] = pl.CostEstimate(flops=cost, bytes_accessed=cost // 100, transcendentals=0)
    return pl.pallas_call(kernel, out_shape=out_shape, compiler_params=params, **kw)


VMEM_SPEC = pl.BlockSpec(memory_space=pltpu.VMEM)
SMEM_SPEC = pl.BlockSpec(memory_space=pltpu.SMEM)
HBM_SPEC = pl.BlockSpec(memory_space=pltpu.HBM)


LOW = TILE // 2


def tail_kernel(edges, rows, tail):
    start = edges[0, 1] - edges[0, 0] - HALO - LOW
    rest = start & (SUB - 1)
    whole = pl.multiple_of(start - rest, SUB)
    for sp in range(tail.shape[0]):
        window = rows[sp, pl.ds(whole, HALO + SUB), :]
        tail[sp] = pltpu.roll(window, (HALO + SUB - rest) % (HALO + SUB), 0)[:HALO]


def brick_tail(edges, field):
    species, _, lines = field.shape
    return call(
        tail_kernel,
        jax.ShapeDtypeStruct((species, HALO, lines), F32),
        in_specs=[SMEM_SPEC, VMEM_SPEC],
        out_specs=VMEM_SPEC,
    )(edges, field[:, LOW : LOW + TILE - SUB])


def first_kernel(field, away):
    species, _, width = away.shape
    other = pl.ds(pl.multiple_of((1 - lax.axis_index("cross")) * width, LANES), width)
    for sp in range(species):
        away[sp] = field[sp, :FIRST, other]


def first_rows(field, width):
    return call(
        first_kernel,
        jax.ShapeDtypeStruct((field.shape[0], FIRST, width), F32),
        in_specs=[VMEM_SPEC],
        out_specs=VMEM_SPEC,
    )(field)


PAD = 32


def matrix_kernel(edges, widths, factors, coarse, coarse_width, nodes, cell, low, main, up, load, stored):
    slab = lax.axis_index("slab")
    shift = edges[0, 0] - slab * TILE
    rows, lanes = nodes.shape[1], nodes.shape[0] * LANES
    node = lax.broadcasted_iota(jnp.int32, (rows, lanes), 0)
    lane = lax.broadcasted_iota(jnp.int32, (rows, lanes), 1)
    column = lane % HELD
    later = column - FIRST
    held = jnp.where(column < FIRST, column + shift, jnp.where(later < shift, later, column))
    plain = lane - 2 * LANES
    from_halo = jnp.where((slab == 0) & (plain < HALO), plain + TILE, plain - HALO + shift)
    grouped = (lane < 3 * HELD) & (column <= TILE)
    held = jnp.where(lane < 2 * LANES, jnp.where(grouped, held, -1), jnp.where(plain < HELD, from_halo, -1))
    chosen = ((held == node) & (node <= TILE)).astype(F32)
    for j in range(lanes // LANES):
        nodes[j] = chosen[:, j * LANES : (j + 1) * LANES]
    cell[...] = jnp.zeros_like(cell)
    cell[:TILE] = widths[...]
    for ref in (low, up, load):
        ref[...] = jnp.zeros_like(ref)
    main[...] = jnp.ones_like(main)
    stored[...] = jnp.zeros_like(stored)
    wide = lambda x: jnp.concatenate([x] * (lanes // LANES), axis=1)
    placed = 0
    pairs = TILE // 2
    for _ in range(LEVELS):
        size = -(-(pairs + 1) // SUB) * SUB
        here = pl.ds(PAD, size)
        inside = lax.broadcasted_iota(jnp.int32, (size, LANES), 0) < pairs
        left = cell[pl.ds(0, size, stride=2)]
        right = cell[pl.ds(1, size, stride=2)]
        total = left + right
        safe = jnp.where(inside, total, 1.0)
        even, odd, after = [
            jnp.concatenate([nodes[j, pl.ds(i, size, stride=2)] for j in range(lanes // LANES)], axis=1)
            for i in range(3)
        ]
        inverse = 1.0 / safe
        detail = odd - (wide(right * inverse) * even + wide(left * inverse) * after)
        detail = jnp.where(wide(inside), detail, 0.0)
        stored[placed : placed + pairs] = detail[:pairs]
        placed += pairs
        load[here] = wide(right / 6.0 + left / 3.0) * detail
        load[pl.ds(PAD - 1, 1)] = jnp.zeros((1, lanes), F32)
        grown = wide(left / 6.0 + right / 3.0) * detail + load[pl.ds(PAD - 1, size)]
        up[here] = total
        before = up[pl.ds(PAD - 1, size)]
        held_rows = lax.broadcasted_iota(jnp.int32, (size, LANES), 0) <= pairs
        diag = jnp.where(held_rows, (before + total) / 3.0, 1.0)
        lower = jnp.where(held_rows, before / 6.0, 0.0)
        upper = total / 6.0
        step = 1
        while step <= pairs:
            low[here] = lower
            up[here] = upper
            main[here] = 1.0 / diag
            load[here] = grown
            back = pl.ds(PAD - step, size)
            fore = pl.ds(PAD + step, size)
            alpha = -lower * main[back]
            gamma = -upper * main[fore]
            diag = diag + alpha * up[back] + gamma * low[fore]
            grown = grown + wide(alpha) * load[back] + wide(gamma) * load[fore]
            lower = alpha * low[back]
            upper = gamma * up[fore]
            step *= 2
        result = even + grown * wide(1.0 / diag)
        result = jnp.where(wide(held_rows), result, 0.0)
        nodes[...] = jnp.zeros_like(nodes)
        for j in range(lanes // LANES):
            nodes[j, :size] = result[:, j * LANES : (j + 1) * LANES]
        cell[...] = jnp.zeros_like(cell)
        cell[:size] = total
        pairs //= 2
    coarse[...] = nodes[2, :SUB]
    coarse_width[...] = cell[:SUB]
    matrix = stored[:, : 2 * LANES]
    lane = lax.broadcasted_iota(jnp.int32, matrix.shape, 1)
    for i in range(3):
        term = matrix.astype(BF16)
        matrix = matrix - term.astype(F32)
        factors[i * TILE : (i + 1) * TILE] = jnp.where(lane < (3 - i) * HELD, term.astype(F32), 0.0).astype(BF16)


def tile_matrix(edges, cell_width):
    widths = jnp.broadcast_to(cell_width[:, None], (TILE, LANES))
    narrow = pltpu.VMEM((PAD + 40 + PAD, LANES), F32)
    broad = pltpu.VMEM((PAD + 40 + PAD, 3 * LANES), F32)
    return call(
        matrix_kernel,
        (
            jax.ShapeDtypeStruct((3 * TILE, 2 * LANES), BF16),
            jax.ShapeDtypeStruct((SUB, LANES), F32),
            jax.ShapeDtypeStruct((SUB, LANES), F32),
        ),
        in_specs=[SMEM_SPEC, VMEM_SPEC],
        out_specs=(VMEM_SPEC,) * 3,
        scratch_shapes=[
            pltpu.VMEM((3, 88, LANES), F32),
            pltpu.VMEM((88, LANES), F32),
            narrow,
            narrow,
            narrow,
            broad,
            pltpu.VMEM((TILE, 3 * LANES), F32),
        ],
    )(edges, widths)


def to_dense(result, turned, sets, sp, species):
    blocks = result.shape[1] // LANES
    per = blocks // 2
    for t in range(blocks):
        turned[t * SUB : (t + 1) * SUB] = result[:, t * LANES : (t + 1) * LANES]
    for half in range(2):
        for k in range(COARSE):
            at = ((half * COARSE + k) * species + sp) * per
            sets[pl.ds(at if isinstance(sp, int) else pl.multiple_of(at, per), per)] = turned[
                pl.ds(half * per * SUB + k, per, stride=SUB)
            ]


def brick_kernel(weights, coarse_width, field, sets, turned):
    sp = pl.program_id(0)
    slab = lax.axis_index("slab")
    own = weights[...]
    result = jnp.dot(own[:, HALO:HELD], field[0, :TILE], precision=HIGHEST, preferred_element_type=F32)
    row = jnp.where(slab == 0, field[0, TILE:HELD], 0.0)
    result += jnp.dot(own[:, :HALO], row, precision=HIGHEST, preferred_element_type=F32)
    to_dense(result, turned, sets, sp, pl.num_programs(0))

    @pl.when(sp == 0)
    def _():
        sets[sets.shape[0] - SUB :] = coarse_width[...]


def brick_part(weights, coarse_width, field):
    species, _, lines = field.shape
    dense = COARSE * species * lines // LANES + SUB
    return call(
        brick_kernel,
        jax.ShapeDtypeStruct((dense, LANES), F32),
        grid=(species,),
        in_specs=[
            pl.BlockSpec((SUB, LANES), lambda i: (0, 0)),
            pl.BlockSpec((SUB, LANES), lambda i: (0, 0)),
            pl.BlockSpec((1, HELD, lines), lambda i: (i, 0, 0)),
        ],
        out_specs=pl.BlockSpec((dense, LANES), lambda i: (0, 0)),
        scratch_shapes=[pltpu.VMEM((lines // LANES * SUB, LANES), F32)],
    )(weights, coarse_width, field)


def terms_of(value):
    terms = []
    for _ in range(3):
        terms.append(value.astype(BF16))
        value = value - terms[-1].astype(F32)
    return terms


def halo_kernel(weights, halo, part, own_half, other_half, turned, fresh):
    species = halo.shape[0]
    slab = lax.axis_index("slab")
    weight_terms = terms_of(weights[:, :HALO])
    zero = jnp.zeros_like(weights[:, :HALO])
    own = jnp.concatenate(
        [jnp.concatenate([weight_terms[i].astype(F32)] * (3 - i) + [zero] * i, axis=1) for i in range(3)], axis=0
    ).astype(BF16)
    for sp in range(species):
        stack = jnp.concatenate(terms_of(halo[sp]), axis=0)
        result = jnp.dot(own, stack, preferred_element_type=F32)
        result = result[:SUB] + result[SUB : 2 * SUB] + result[2 * SUB :]
        to_dense(result, turned, fresh, sp, species)
    rows = fresh.shape[0] // 2
    for ref, half in ((own_half, slab & 1), (other_half, 1 - (slab & 1))):
        here = pl.ds(pl.multiple_of(half * rows, SUB), rows)
        ref[:rows] = part[here] + jnp.where(slab == 0, 0.0, fresh[here])
        ref[rows:] = part[2 * rows :]


def coarse_sets(weights, halo, part):
    lines = halo.shape[2]
    rows = part.shape[0] - SUB
    half = jax.ShapeDtypeStruct((rows // 2 + SUB, LANES), F32)
    return call(
        halo_kernel,
        (half, half),
        in_specs=[VMEM_SPEC] * 3,
        out_specs=(VMEM_SPEC,) * 2,
        scratch_shapes=[
            pltpu.VMEM((lines // LANES * SUB, LANES), F32),
            pltpu.VMEM((rows, LANES), F32),
        ],
    )(weights, halo, part)


def later_nodes(shift, halo, brick):
    rows = jnp.concatenate([halo, brick], axis=0)
    count = rows.shape[0]
    return pltpu.roll(rows, (count - HALO + shift) % count, 0)


BRICK_END = TILE + SUB


def rest_kernel(edges, halo, field, out):
    species = halo.shape[0]
    shift = edges[0, 0] - lax.axis_index("slab") * TILE
    each = species * (SECOND + 1)
    width = out.shape[0] // each * LANES
    other = pl.ds(pl.multiple_of((1 - lax.axis_index("cross")) * width, LANES), width)
    for sp in range(species):
        rows = later_nodes(shift, halo[sp, :, other], field[sp, FIRST:BRICK_END, other])
        for t in range(width // LANES):
            tile = rows[:, t * LANES : (t + 1) * LANES]
            out[t * each + sp * SECOND : t * each + (sp + 1) * SECOND] = tile[:SECOND]
            last = t * each + species * SECOND + sp
            out[last : last + 1] = tile[SECOND : SECOND + 1]


def rest_away(edges, halo, field, width):
    species = halo.shape[0]
    rows = species * (SECOND + 1) * width // LANES
    return call(
        rest_kernel,
        jax.ShapeDtypeStruct((rows, LANES), F32),
        in_specs=[SMEM_SPEC, VMEM_SPEC, VMEM_SPEC],
        out_specs=VMEM_SPEC,
        cost=20_000_000,
    )(edges, halo, field)


def detail_kernel(local, whole, edges, factors, first, second, *rest):
    out, wide = rest[-2:]
    species = out.shape[1]
    width = out.shape[2]
    weights = factors[:, : 3 * HELD]
    step = pl.program_id(0)
    if local and not whole:
        step += lax.axis_index("cross") * pl.num_programs(0)
    lanes = pl.ds(pl.multiple_of(step * width, LANES), width)
    shift = edges[0, 0] - lax.axis_index("slab") * TILE
    for sp in range(species):
        if local:
            more = later_nodes(shift, first[sp, :, lanes], second[sp, FIRST:BRICK_END, lanes])
            pieces = [second[sp, :FIRST, lanes], more[: SECOND + HALO]]
        else:
            each = species * (SECOND + 1)
            base = step * (width // LANES * each)

            def rows_of(at, count):
                return jnp.concatenate(
                    [second[pl.ds(base + t * each + at, count)] for t in range(width // LANES)], axis=1
                )

            end = rows_of(species * SECOND + sp, 1)
            end = jnp.concatenate([end, jnp.zeros((HALO - 1, width), F32)], axis=0)
            pieces = [first[sp, :, lanes], rows_of(sp * SECOND, SECOND), end]
        stack = jnp.concatenate(terms_of(jnp.concatenate(pieces, axis=0)), axis=0)
        result = jnp.dot(weights, stack, preferred_element_type=F32)
        result = result[:TILE] + result[TILE : 2 * TILE] + result[2 * TILE :]
        for t in range(width // LANES):
            wide[t, pl.ds(sp, TILE, stride=species)] = result[:, t * LANES : (t + 1) * LANES]
    for t in range(width // LANES):
        for k in range(DETAILS):
            out[k, :, t * LANES : (t + 1) * LANES] = wide[t, k * species : (k + 1) * species]


def details(local, edges, factors, first, second, width, species, lines, onto=None):
    chunk = min(width, 512)
    steps = width // chunk

    def here(i):
        return i if width == lines else lax.axis_index("cross") * steps + i

    def there(i):
        return (1 - lax.axis_index("cross")) * steps + i

    specs = [SMEM_SPEC] + [VMEM_SPEC] * 3
    operands = [edges, factors, first, second]
    alias = {}
    if onto is not None:
        specs.append(HBM_SPEC)
        operands.append(onto)
        alias = {4: 0}
    return call(
        functools.partial(detail_kernel, local, width == lines),
        jax.ShapeDtypeStruct((DETAILS, species, lines), F32),
        grid=(steps,),
        in_specs=specs,
        out_specs=pl.BlockSpec((DETAILS, species, chunk), lambda i: (0, 0, here(i) if local else there(i))),
        scratch_shapes=[pltpu.VMEM((chunk // LANES, TILE * species, LANES), F32)],
        input_output_aliases=alias,
        cost=20_000_000,
    )(*operands)


def merged(lower, upper):
    lower_values, lower_widths = lower
    upper_values, upper_widths = upper
    shared = 0.5 * (lower_values[-1] + upper_values[0])
    values = lower_values[:-1] + [shared] + upper_values[1:]
    widths = lower_widths + upper_widths
    left, right = widths[0::2], widths[1::2]
    pairs = len(left)
    total = [a + b for a, b in zip(left, right)]
    detail = []
    for i in range(pairs):
        inverse = 1.0 / total[i]
        detail.append(
            values[2 * i + 1] - ((right[i] * inverse) * values[2 * i] + (left[i] * inverse) * values[2 * i + 2])
        )
    loads = []
    for k in range(pairs + 1):
        term = None
        if k < pairs:
            term = (left[k] / 6.0 + right[k] / 3.0) * detail[k]
        if k > 0:
            other = (right[k - 1] / 6.0 + left[k - 1] / 3.0) * detail[k - 1]
            term = other if term is None else term + other
        loads.append(term)
    ratio, solved = [], []
    for k in range(pairs + 1):
        diag = (total[k - 1] if k else 0.0) + (total[k] if k < pairs else 0.0)
        diag = diag / 3.0
        if k:
            off = total[k - 1] / 6.0
            pivot = 1.0 / (diag - off * ratio[-1])
            solved.append((loads[k] - off * solved[-1]) * pivot)
        else:
            pivot = 1.0 / diag
            solved.append(loads[k] * pivot)
        if k < pairs:
            ratio.append(total[k] / 6.0 * pivot)
    for k in range(pairs - 1, -1, -1):
        solved[k] = solved[k] - ratio[k] * solved[k + 1]
    coarse = [values[2 * k] + solved[k] for k in range(pairs + 1)]
    return coarse, detail, total


def values_at(ref, first, rows):
    return [ref[pl.ds(first + k * rows, rows)] for k in range(COARSE)]


def widths_at(ref, first):
    return [ref[pl.ds(first + i, 1)] for i in range(COARSE - 1)]


def put(ref, first, rows, values):
    for k, value in enumerate(values):
        ref[pl.ds(first + k * rows, rows)] = value


def put_widths(ref, first, widths):
    put(ref, first, 1, widths)
    ref[first + COARSE - 1 : first + SUB] = jnp.zeros((SUB - COARSE + 1, LANES), F32)


def in_order(upper_side, mine, theirs):
    def pick(first, second):
        return [jnp.where(upper_side, a, b) for a, b in zip(first, second)]

    lower = (pick(theirs[0], mine[0]), pick(theirs[1], mine[1]))
    upper = (pick(mine[0], theirs[0]), pick(mine[1], theirs[1]))
    return merged(lower, upper)


def merge_kernel(level, depth, rows, swapped, *refs):
    slab = lax.axis_index("slab")
    core = slab & 1
    chip = slab & ~1
    upper_side = (slab >> level) & 1 == 1
    last = level == depth - 1
    set_rows = COARSE * rows + SUB
    detail_rows = (COARSE - 1) * rows
    own, other = refs[0], refs[1]
    outs = refs[-2:]

    def state(ref):
        values = values_at(ref, 0, rows) + widths_at(ref, COARSE * rows)
        if level > 0:
            values += [ref[pl.ds(set_rows + i * rows, rows)] for i in range(COARSE - 1)]
        if level > 1:
            values += [ref[pl.ds(set_rows + detail_rows + i * rows, rows)] for i in range(COARSE - 1)]
        return values

    held = state(own)
    if swapped and last:
        home = core == lax.axis_index("cross")
        held = [jnp.where(home, a, b) for a, b in zip(held, state(refs[2]))]
    mine = (held[:COARSE], held[COARSE : 2 * COARSE - 1])
    odd = held[2 * COARSE - 1 : 3 * COARSE - 2]
    even = held[3 * COARSE - 2 :]
    theirs = (values_at(other, 0, rows), widths_at(other, COARSE * rows))

    def pick(first, second):
        return [jnp.where(upper_side, a, b) for a, b in zip(first, second)]

    lower = (pick(theirs[0], mine[0]), pick(theirs[1], mine[1]))
    upper = (pick(mine[0], theirs[0]), pick(mine[1], theirs[1]))
    coarse, detail, widths = merged(lower, upper)
    if level == 0:
        odd = detail
    else:
        keep = ((chip >> level) & 1 == 1) & (chip & ((1 << level) - 1) == 0)
        if last:
            keep = keep | (chip == 0)
        even = even if level > 1 else [0.0] * (COARSE - 1)
        even = [jnp.where(keep, a, b) for a, b in zip(detail, even)]
    if last:
        here, away = outs
        put(here, 0, rows, coarse)
        put(away, 0, rows, coarse)
        put(here, COARSE * rows, rows, [jnp.where(core == 0, a, b) for a, b in zip(even, odd)])
        put(away, COARSE * rows, rows, [jnp.where(core == 0, b, a) for a, b in zip(even, odd)])
        return
    send, carried = outs
    for ref in (send, carried):
        put(ref, 0, rows, coarse)
        put_widths(ref, COARSE * rows, widths)
    put(carried, set_rows, rows, odd)
    if level > 0:
        put(carried, set_rows + detail_rows, rows, even)


def merge(level, depth, rows, swapped, *operands):
    set_rows = COARSE * rows + SUB
    detail_rows = (COARSE - 1) * rows
    if level == depth - 1:
        sizes = ((2 * COARSE - 1) * rows,) * 2
    else:
        sizes = (set_rows, set_rows + min(level + 1, 2) * detail_rows)
    return call(
        functools.partial(merge_kernel, level, depth, rows, swapped),
        tuple(jax.ShapeDtypeStruct((size, LANES), F32) for size in sizes),
        in_specs=[VMEM_SPEC] * len(operands),
        out_specs=(VMEM_SPEC,) * 2,
    )(*operands)


def in_outputs_order(part, tree, final, turned):
    species, group, width = tree.shape
    per = width // LANES
    for k in range(COARSE):
        for sp in range(species):
            turned[pl.ds(sp, per, stride=species)] = part[(k * species + sp) * per : (k * species + sp + 1) * per]
        for t in range(per):
            final[k, :, t * LANES : (t + 1) * LANES] = turned[t * species : (t + 1) * species]
    for sp in range(species):
        for i in range(group):
            at = ((COARSE + i) * species + sp) * per
            turned[pl.ds(i, per, stride=group)] = part[at : at + per]
        for t in range(per):
            tree[sp, :, t * LANES : (t + 1) * LANES] = turned[t * group : (t + 1) * group]


def finish_kernel(own_tree, own_final, other, tree, final, other_tree, other_final, turned, sems):
    core = lax.axis_index("slab") & 1
    width = own_tree.shape[2]

    def to(ref, source, block, sem):
        lanes = pl.ds(pl.multiple_of(block * width, LANES), width)
        copy = pltpu.make_async_copy(source, ref.at[:, :, lanes], sem)
        copy.start()
        return copy

    copies = [to(tree, own_tree, core, sems.at[0]), to(final, own_final, core, sems.at[1])]
    in_outputs_order(other, other_tree, other_final, turned)
    copies += [to(tree, other_tree, 1 - core, sems.at[2]), to(final, other_final, 1 - core, sems.at[3])]
    for copy in copies:
        copy.wait()


def finish(own, other, species, lines):
    half = lines // 2
    shapes = ((species, COARSE - 1, half), (COARSE, species, half))
    turned = pltpu.VMEM((half // LANES * SUB, LANES), F32)
    placed = call(
        in_outputs_order,
        tuple(jax.ShapeDtypeStruct(shape, F32) for shape in shapes),
        in_specs=[VMEM_SPEC],
        out_specs=(VMEM_SPEC,) * 2,
        scratch_shapes=[turned],
    )(own)
    return call(
        finish_kernel,
        tuple(jax.ShapeDtypeStruct(shape[:2] + (lines,), F32) for shape in shapes),
        in_specs=[VMEM_SPEC] * 3,
        out_specs=(HBM_SPEC,) * 2,
        scratch_shapes=[pltpu.VMEM(shape, F32) for shape in shapes] + [turned, pltpu.SemaphoreType.DMA((4,))],
    )(*placed, other)


def from_partner(block, axis, step):
    count = lax.axis_size(axis)
    return lax.ppermute(block, axis, [(i, i ^ step) for i in range(count)])


def shifted(block, axis):
    count = lax.axis_size(axis)
    return lax.ppermute(block, axis, [(i, i + 1) for i in range(count - 1)])


def exchanged(block, axis):
    species, rows, lines = block.shape
    count = lax.axis_size(axis)
    parts = block.reshape(species, rows, count, lines // count)
    return lax.all_to_all(parts, axis, split_axis=2, concat_axis=2, tiled=True).reshape(block.shape)


def last_routes(slabs):
    partner, own = [], []
    for s in range(slabs):
        for c in range(2):
            home = (s & 1) == c
            target = (s, c) if home else (s ^ 1, 1 - c)
            partner.append((s * 2 + c, (target[0] ^ (slabs // 2)) * 2 + target[1]))
            if not home:
                own.append((s * 2 + c, target[0] * 2 + target[1]))
    return partner, own


def on_device(sim_field, brick_edges, cell_width):
    species, _, lines = sim_field.shape
    cross_count = lax.axis_size("cross")
    slabs = lax.axis_size("slab")
    depth = slabs.bit_length() - 1
    width = lines // cross_count
    rows = species * (lines // 2) // LANES
    swapped = cross_count == 2
    both = ("slab", "cross")

    field = sim_field
    halo = shifted(brick_tail(brick_edges, field), "slab")
    if swapped:
        first_in = from_partner(first_rows(field, width), "cross", 1)
    factors, weights, coarse_width = tile_matrix(brick_edges, cell_width)
    part = brick_part(weights, coarse_width, field)
    halo, part, factors = lax.optimization_barrier((halo, part, factors))
    own_half, other_half = coarse_sets(weights, halo, part)
    halo, other_half = lax.optimization_barrier((halo, other_half))
    if swapped:
        rest = rest_away(brick_edges, halo, field, width)
        halo, rest = lax.optimization_barrier((halo, rest))
        rest_in = from_partner(rest, "cross", 1)

    if swapped:
        near = details(True, brick_edges, factors, halo, field, width, species, lines)
    send, carried = other_half, own_half
    for level in range(depth):
        last = level == depth - 1
        if swapped and level == depth - 2:
            send, near = lax.optimization_barrier((send, near))
        if swapped and last:
            partner_route, own_route = last_routes(slabs)
            operands = (carried, lax.ppermute(send, both, partner_route), lax.ppermute(carried, both, own_route))
            tile_detail = details(False, brick_edges, factors, first_in, rest_in, width, species, lines, near)
            operands, tile_detail = lax.optimization_barrier((operands, tile_detail))
        else:
            operands = (carried, from_partner(send, "slab", 1 << level))
        send, carried = merge(level, depth, rows, swapped, *operands)
    here_set, away_set = send, carried
    partner_set = from_partner(away_set, "slab", 1)

    if swapped:
        tree_detail, coarse_final = finish(here_set, partner_set, species, lines)
        coarse_final = coarse_final.transpose(1, 0, 2)
    else:
        core = lax.axis_index("slab") % 2
        first = jnp.where(core == 0, here_set, partner_set)
        second = jnp.where(core == 0, partner_set, here_set)
        ended = jnp.stack([first, second]).reshape(2, 2 * COARSE - 1, species, lines // 2)
        ended = ended.transpose(2, 1, 0, 3).reshape(species, 2 * COARSE - 1, lines)
        ended = exchanged(ended, "cross")
        coarse_final, tree_detail = ended[:, :COARSE], ended[:, COARSE:]
        moved = exchanged(jnp.concatenate([halo, sim_field[:, :HELD]], axis=1), "cross")
        tile_detail = details(True, brick_edges, factors, moved[:, :HALO], moved[:, HALO:], lines, species, lines)
    return (tile_detail.transpose(1, 0, 2), tree_detail, coarse_final)


def solution(mesh):
    placed = (P(None, "slab", "cross"), P("slab", None), P("slab"))
    return jax.shard_map(
        on_device,
        mesh=mesh,
        in_specs=placed,
        out_specs=(P(None, "slab", "cross"), P(None, "slab", "cross"), P(None, None, "cross")),
        check_vma=False,
    )
```

```python
import functools

import jax
import jax.numpy as jnp
from jax import lax
from jax.experimental import pallas as pl
from jax.experimental.pallas import tpu as pltpu
from jax.sharding import PartitionSpec as P

TILE = 64
HALO = 16
LEVELS = 4
COARSE = 5
DETAILS = TILE - COARSE + 1
LANES = 128
SUB = 8
HELD = TILE + HALO
FIRST = 48
SECOND = TILE - FIRST
F32 = jnp.float32
BF16 = jnp.bfloat16
HIGHEST = lax.Precision.HIGHEST


def call(kernel, out_shape, *, vmem=8 << 20, cost=None, **kw):
    params = pltpu.CompilerParams(vmem_limit_bytes=vmem)
    if cost is not None:
        kw["cost_estimate"] = pl.CostEstimate(flops=cost, bytes_accessed=cost // 100, transcendentals=0)
    return pl.pallas_call(kernel, out_shape=out_shape, compiler_params=params, **kw)


VMEM_SPEC = pl.BlockSpec(memory_space=pltpu.VMEM)
SMEM_SPEC = pl.BlockSpec(memory_space=pltpu.SMEM)
HBM_SPEC = pl.BlockSpec(memory_space=pltpu.HBM)


LOW = TILE // 2


def tail_kernel(edges, rows, tail):
    start = edges[0, 1] - edges[0, 0] - HALO - LOW
    rest = start & (SUB - 1)
    whole = pl.multiple_of(start - rest, SUB)
    for sp in range(tail.shape[0]):
        window = rows[sp, pl.ds(whole, HALO + SUB), :]
        tail[sp] = pltpu.roll(window, (HALO + SUB - rest) % (HALO + SUB), 0)[:HALO]


def brick_tail(edges, field):
    species, _, lines = field.shape
    return call(
        tail_kernel,
        jax.ShapeDtypeStruct((species, HALO, lines), F32),
        in_specs=[SMEM_SPEC, VMEM_SPEC],
        out_specs=VMEM_SPEC,
    )(edges, field[:, LOW : LOW + TILE - SUB])


def first_kernel(field, away):
    species, _, width = away.shape
    other = pl.ds(pl.multiple_of((1 - lax.axis_index("cross")) * width, LANES), width)
    for sp in range(species):
        away[sp] = field[sp, :FIRST, other]


def first_rows(field, width):
    return call(
        first_kernel,
        jax.ShapeDtypeStruct((field.shape[0], FIRST, width), F32),
        in_specs=[VMEM_SPEC],
        out_specs=VMEM_SPEC,
    )(field)


PAD = 32


def matrix_kernel(edges, widths, factors, coarse, coarse_width, nodes, cell, low, main, up, load, stored):
    slab = lax.axis_index("slab")
    shift = edges[0, 0] - slab * TILE
    rows, lanes = nodes.shape[1], nodes.shape[0] * LANES
    node = lax.broadcasted_iota(jnp.int32, (rows, lanes), 0)
    lane = lax.broadcasted_iota(jnp.int32, (rows, lanes), 1)
    column = lane % HELD
    later = column - FIRST
    held = jnp.where(column < FIRST, column + shift, jnp.where(later < shift, later, column))
    plain = lane - 2 * LANES
    from_halo = jnp.where((slab == 0) & (plain < HALO), plain + TILE, plain - HALO + shift)
    grouped = (lane < 3 * HELD) & (column <= TILE)
    held = jnp.where(lane < 2 * LANES, jnp.where(grouped, held, -1), jnp.where(plain < HELD, from_halo, -1))
    chosen = ((held == node) & (node <= TILE)).astype(F32)
    for j in range(lanes // LANES):
        nodes[j] = chosen[:, j * LANES : (j + 1) * LANES]
    cell[...] = jnp.zeros_like(cell)
    cell[:TILE] = widths[...]
    for ref in (low, up, load):
        ref[...] = jnp.zeros_like(ref)
    main[...] = jnp.ones_like(main)
    stored[...] = jnp.zeros_like(stored)
    wide = lambda x: jnp.concatenate([x] * (lanes // LANES), axis=1)
    placed = 0
    pairs = TILE // 2
    for _ in range(LEVELS):
        size = -(-(pairs + 1) // SUB) * SUB
        here = pl.ds(PAD, size)
        inside = lax.broadcasted_iota(jnp.int32, (size, LANES), 0) < pairs
        left = cell[pl.ds(0, size, stride=2)]
        right = cell[pl.ds(1, size, stride=2)]
        total = left + right
        safe = jnp.where(inside, total, 1.0)
        even, odd, after = [
            jnp.concatenate([nodes[j, pl.ds(i, size, stride=2)] for j in range(lanes // LANES)], axis=1)
            for i in range(3)
        ]
        inverse = 1.0 / safe
        detail = odd - (wide(right * inverse) * even + wide(left * inverse) * after)
        detail = jnp.where(wide(inside), detail, 0.0)
        stored[placed : placed + pairs] = detail[:pairs]
        placed += pairs
        load[here] = wide(right / 6.0 + left / 3.0) * detail
        load[pl.ds(PAD - 1, 1)] = jnp.zeros((1, lanes), F32)
        grown = wide(left / 6.0 + right / 3.0) * detail + load[pl.ds(PAD - 1, size)]
        up[here] = total
        before = up[pl.ds(PAD - 1, size)]
        held_rows = lax.broadcasted_iota(jnp.int32, (size, LANES), 0) <= pairs
        diag = jnp.where(held_rows, (before + total) / 3.0, 1.0)
        lower = jnp.where(held_rows, before / 6.0, 0.0)
        upper = total / 6.0
        step = 1
        while step <= pairs:
            low[here] = lower
            up[here] = upper
            main[here] = 1.0 / diag
            load[here] = grown
            back = pl.ds(PAD - step, size)
            fore = pl.ds(PAD + step, size)
            alpha = -lower * main[back]
            gamma = -upper * main[fore]
            diag = diag + alpha * up[back] + gamma * low[fore]
            grown = grown + wide(alpha) * load[back] + wide(gamma) * load[fore]
            lower = alpha * low[back]
            upper = gamma * up[fore]
            step *= 2
        result = even + grown * wide(1.0 / diag)
        result = jnp.where(wide(held_rows), result, 0.0)
        nodes[...] = jnp.zeros_like(nodes)
        for j in range(lanes // LANES):
            nodes[j, :size] = result[:, j * LANES : (j + 1) * LANES]
        cell[...] = jnp.zeros_like(cell)
        cell[:size] = total
        pairs //= 2
    coarse[...] = nodes[2, :SUB]
    coarse_width[...] = cell[:SUB]
    matrix = stored[:, : 2 * LANES]
    lane = lax.broadcasted_iota(jnp.int32, matrix.shape, 1)
    for i in range(3):
        term = matrix.astype(BF16)
        matrix = matrix - term.astype(F32)
        factors[i * TILE : (i + 1) * TILE] = jnp.where(lane < (3 - i) * HELD, term.astype(F32), 0.0).astype(BF16)


def tile_matrix(edges, cell_width):
    widths = jnp.broadcast_to(cell_width[:, None], (TILE, LANES))
    narrow = pltpu.VMEM((PAD + 40 + PAD, LANES), F32)
    broad = pltpu.VMEM((PAD + 40 + PAD, 3 * LANES), F32)
    return call(
        matrix_kernel,
        (
            jax.ShapeDtypeStruct((3 * TILE, 2 * LANES), BF16),
            jax.ShapeDtypeStruct((SUB, LANES), F32),
            jax.ShapeDtypeStruct((SUB, LANES), F32),
        ),
        in_specs=[SMEM_SPEC, VMEM_SPEC],
        out_specs=(VMEM_SPEC,) * 3,
        scratch_shapes=[
            pltpu.VMEM((3, 88, LANES), F32),
            pltpu.VMEM((88, LANES), F32),
            narrow,
            narrow,
            narrow,
            broad,
            pltpu.VMEM((TILE, 3 * LANES), F32),
        ],
    )(edges, widths)


def to_dense(result, turned, sets, sp, species):
    blocks = result.shape[1] // LANES
    per = blocks // 2
    for t in range(blocks):
        turned[t * SUB : (t + 1) * SUB] = result[:, t * LANES : (t + 1) * LANES]
    for half in range(2):
        for k in range(COARSE):
            at = ((half * COARSE + k) * species + sp) * per
            sets[pl.ds(at if isinstance(sp, int) else pl.multiple_of(at, per), per)] = turned[
                pl.ds(half * per * SUB + k, per, stride=SUB)
            ]


def brick_kernel(weights, coarse_width, field, sets, turned):
    sp = pl.program_id(0)
    slab = lax.axis_index("slab")
    own = weights[...]
    result = jnp.dot(own[:, HALO:HELD], field[0, :TILE], precision=HIGHEST, preferred_element_type=F32)
    row = jnp.where(slab == 0, field[0, TILE:HELD], 0.0)
    result += jnp.dot(own[:, :HALO], row, precision=HIGHEST, preferred_element_type=F32)
    to_dense(result, turned, sets, sp, pl.num_programs(0))

    @pl.when(sp == 0)
    def _():
        sets[sets.shape[0] - SUB :] = coarse_width[...]


def brick_part(weights, coarse_width, field):
    species, _, lines = field.shape
    dense = COARSE * species * lines // LANES + SUB
    return call(
        brick_kernel,
        jax.ShapeDtypeStruct((dense, LANES), F32),
        grid=(species,),
        in_specs=[
            pl.BlockSpec((SUB, LANES), lambda i: (0, 0)),
            pl.BlockSpec((SUB, LANES), lambda i: (0, 0)),
            pl.BlockSpec((1, HELD, lines), lambda i: (i, 0, 0)),
        ],
        out_specs=pl.BlockSpec((dense, LANES), lambda i: (0, 0)),
        scratch_shapes=[pltpu.VMEM((lines // LANES * SUB, LANES), F32)],
    )(weights, coarse_width, field)


def terms_of(value):
    terms = []
    for _ in range(3):
        terms.append(value.astype(BF16))
        value = value - terms[-1].astype(F32)
    return terms


def halo_kernel(weights, halo, part, own_half, other_half, turned, fresh):
    species = halo.shape[0]
    slab = lax.axis_index("slab")
    weight_terms = terms_of(weights[:, :HALO])
    zero = jnp.zeros_like(weights[:, :HALO])
    own = jnp.concatenate(
        [jnp.concatenate([weight_terms[i].astype(F32)] * (3 - i) + [zero] * i, axis=1) for i in range(3)], axis=0
    ).astype(BF16)
    for sp in range(species):
        stack = jnp.concatenate(terms_of(halo[sp]), axis=0)
        result = jnp.dot(own, stack, preferred_element_type=F32)
        result = result[:SUB] + result[SUB : 2 * SUB] + result[2 * SUB :]
        to_dense(result, turned, fresh, sp, species)
    rows = fresh.shape[0] // 2
    for ref, half in ((own_half, slab & 1), (other_half, 1 - (slab & 1))):
        here = pl.ds(pl.multiple_of(half * rows, SUB), rows)
        ref[:rows] = part[here] + jnp.where(slab == 0, 0.0, fresh[here])
        ref[rows:] = part[2 * rows :]


def coarse_sets(weights, halo, part):
    lines = halo.shape[2]
    rows = part.shape[0] - SUB
    half = jax.ShapeDtypeStruct((rows // 2 + SUB, LANES), F32)
    return call(
        halo_kernel,
        (half, half),
        in_specs=[VMEM_SPEC] * 3,
        out_specs=(VMEM_SPEC,) * 2,
        scratch_shapes=[
            pltpu.VMEM((lines // LANES * SUB, LANES), F32),
            pltpu.VMEM((rows, LANES), F32),
        ],
    )(weights, halo, part)


def later_nodes(shift, halo, brick):
    rows = jnp.concatenate([halo, brick], axis=0)
    count = rows.shape[0]
    return pltpu.roll(rows, (count - HALO + shift) % count, 0)


BRICK_END = TILE + SUB


def rest_kernel(edges, halo, field, out):
    species = halo.shape[0]
    shift = edges[0, 0] - lax.axis_index("slab") * TILE
    each = species * (SECOND + 1)
    width = out.shape[0] // each * LANES
    other = pl.ds(pl.multiple_of((1 - lax.axis_index("cross")) * width, LANES), width)
    for sp in range(species):
        rows = later_nodes(shift, halo[sp, :, other], field[sp, FIRST:BRICK_END, other])
        for t in range(width // LANES):
            tile = rows[:, t * LANES : (t + 1) * LANES]
            out[t * each + sp * SECOND : t * each + (sp + 1) * SECOND] = tile[:SECOND]
            last = t * each + species * SECOND + sp
            out[last : last + 1] = tile[SECOND : SECOND + 1]


def rest_away(edges, halo, field, width):
    species = halo.shape[0]
    rows = species * (SECOND + 1) * width // LANES
    return call(
        rest_kernel,
        jax.ShapeDtypeStruct((rows, LANES), F32),
        in_specs=[SMEM_SPEC, VMEM_SPEC, VMEM_SPEC],
        out_specs=VMEM_SPEC,
        cost=20_000_000,
    )(edges, halo, field)


def detail_kernel(local, whole, edges, factors, first, second, *rest):
    out, wide = rest[-2:]
    species = out.shape[1]
    width = out.shape[2]
    weights = factors[:, : 3 * HELD]
    step = pl.program_id(0)
    if local and not whole:
        step += lax.axis_index("cross") * pl.num_programs(0)
    lanes = pl.ds(pl.multiple_of(step * width, LANES), width)
    shift = edges[0, 0] - lax.axis_index("slab") * TILE
    for sp in range(species):
        if local:
            more = later_nodes(shift, first[sp, :, lanes], second[sp, FIRST:BRICK_END, lanes])
            pieces = [second[sp, :FIRST, lanes], more[: SECOND + HALO]]
        else:
            each = species * (SECOND + 1)
            base = step * (width // LANES * each)

            def rows_of(at, count):
                return jnp.concatenate(
                    [second[pl.ds(base + t * each + at, count)] for t in range(width // LANES)], axis=1
                )

            end = rows_of(species * SECOND + sp, 1)
            end = jnp.concatenate([end, jnp.zeros((HALO - 1, width), F32)], axis=0)
            pieces = [first[sp, :, lanes], rows_of(sp * SECOND, SECOND), end]
        stack = jnp.concatenate(terms_of(jnp.concatenate(pieces, axis=0)), axis=0)
        result = jnp.dot(weights, stack, preferred_element_type=F32)
        result = result[:TILE] + result[TILE : 2 * TILE] + result[2 * TILE :]
        for t in range(width // LANES):
            wide[t, pl.ds(sp, TILE, stride=species)] = result[:, t * LANES : (t + 1) * LANES]
    for t in range(width // LANES):
        for k in range(DETAILS):
            out[k, :, t * LANES : (t + 1) * LANES] = wide[t, k * species : (k + 1) * species]


def details(local, edges, factors, first, second, width, species, lines, onto=None):
    chunk = min(width, 512)
    steps = width // chunk

    def here(i):
        return i if width == lines else lax.axis_index("cross") * steps + i

    def there(i):
        return (1 - lax.axis_index("cross")) * steps + i

    specs = [SMEM_SPEC] + [VMEM_SPEC] * 3
    operands = [edges, factors, first, second]
    alias = {}
    if onto is not None:
        specs.append(HBM_SPEC)
        operands.append(onto)
        alias = {4: 0}
    return call(
        functools.partial(detail_kernel, local, width == lines),
        jax.ShapeDtypeStruct((DETAILS, species, lines), F32),
        grid=(steps,),
        in_specs=specs,
        out_specs=pl.BlockSpec((DETAILS, species, chunk), lambda i: (0, 0, here(i) if local else there(i))),
        scratch_shapes=[pltpu.VMEM((chunk // LANES, TILE * species, LANES), F32)],
        input_output_aliases=alias,
        cost=20_000_000,
    )(*operands)


def merged(lower, upper):
    lower_values, lower_widths = lower
    upper_values, upper_widths = upper
    shared = 0.5 * (lower_values[-1] + upper_values[0])
    values = lower_values[:-1] + [shared] + upper_values[1:]
    widths = lower_widths + upper_widths
    left, right = widths[0::2], widths[1::2]
    pairs = len(left)
    total = [a + b for a, b in zip(left, right)]
    detail = []
    for i in range(pairs):
        inverse = 1.0 / total[i]
        detail.append(
            values[2 * i + 1] - ((right[i] * inverse) * values[2 * i] + (left[i] * inverse) * values[2 * i + 2])
        )
    loads = []
    for k in range(pairs + 1):
        term = None
        if k < pairs:
            term = (left[k] / 6.0 + right[k] / 3.0) * detail[k]
        if k > 0:
            other = (right[k - 1] / 6.0 + left[k - 1] / 3.0) * detail[k - 1]
            term = other if term is None else term + other
        loads.append(term)
    ratio, solved = [], []
    for k in range(pairs + 1):
        diag = (total[k - 1] if k else 0.0) + (total[k] if k < pairs else 0.0)
        diag = diag / 3.0
        if k:
            off = total[k - 1] / 6.0
            pivot = 1.0 / (diag - off * ratio[-1])
            solved.append((loads[k] - off * solved[-1]) * pivot)
        else:
            pivot = 1.0 / diag
            solved.append(loads[k] * pivot)
        if k < pairs:
            ratio.append(total[k] / 6.0 * pivot)
    for k in range(pairs - 1, -1, -1):
        solved[k] = solved[k] - ratio[k] * solved[k + 1]
    coarse = [values[2 * k] + solved[k] for k in range(pairs + 1)]
    return coarse, detail, total


def values_at(ref, first, rows):
    return [ref[pl.ds(first + k * rows, rows)] for k in range(COARSE)]


def widths_at(ref, first):
    return [ref[pl.ds(first + i, 1)] for i in range(COARSE - 1)]


def put(ref, first, rows, values):
    for k, value in enumerate(values):
        ref[pl.ds(first + k * rows, rows)] = value


def put_widths(ref, first, widths):
    put(ref, first, 1, widths)
    ref[first + COARSE - 1 : first + SUB] = jnp.zeros((SUB - COARSE + 1, LANES), F32)


def in_order(upper_side, mine, theirs):
    def pick(first, second):
        return [jnp.where(upper_side, a, b) for a, b in zip(first, second)]

    lower = (pick(theirs[0], mine[0]), pick(theirs[1], mine[1]))
    upper = (pick(mine[0], theirs[0]), pick(mine[1], theirs[1]))
    return merged(lower, upper)


def merge_kernel(level, depth, rows, swapped, *refs):
    slab = lax.axis_index("slab")
    core = slab & 1
    chip = slab & ~1
    upper_side = (slab >> level) & 1 == 1
    last = level == depth - 1
    set_rows = COARSE * rows + SUB
    detail_rows = (COARSE - 1) * rows
    own, other = refs[0], refs[1]
    outs = refs[-2:]

    def state(ref):
        values = values_at(ref, 0, rows) + widths_at(ref, COARSE * rows)
        if level > 0:
            values += [ref[pl.ds(set_rows + i * rows, rows)] for i in range(COARSE - 1)]
        if level > 1:
            values += [ref[pl.ds(set_rows + detail_rows + i * rows, rows)] for i in range(COARSE - 1)]
        return values

    held = state(own)
    if swapped and last:
        home = core == lax.axis_index("cross")
        held = [jnp.where(home, a, b) for a, b in zip(held, state(refs[2]))]
    mine = (held[:COARSE], held[COARSE : 2 * COARSE - 1])
    odd = held[2 * COARSE - 1 : 3 * COARSE - 2]
    even = held[3 * COARSE - 2 :]
    theirs = (values_at(other, 0, rows), widths_at(other, COARSE * rows))

    def pick(first, second):
        return [jnp.where(upper_side, a, b) for a, b in zip(first, second)]

    lower = (pick(theirs[0], mine[0]), pick(theirs[1], mine[1]))
    upper = (pick(mine[0], theirs[0]), pick(mine[1], theirs[1]))
    coarse, detail, widths = merged(lower, upper)
    if level == 0:
        odd = detail
    else:
        keep = ((chip >> level) & 1 == 1) & (chip & ((1 << level) - 1) == 0)
        if last:
            keep = keep | (chip == 0)
        even = even if level > 1 else [0.0] * (COARSE - 1)
        even = [jnp.where(keep, a, b) for a, b in zip(detail, even)]
    if last:
        here, away = outs
        put(here, 0, rows, coarse)
        put(away, 0, rows, coarse)
        put(here, COARSE * rows, rows, [jnp.where(core == 0, a, b) for a, b in zip(even, odd)])
        put(away, COARSE * rows, rows, [jnp.where(core == 0, b, a) for a, b in zip(even, odd)])
        return
    send, carried = outs
    for ref in (send, carried):
        put(ref, 0, rows, coarse)
        put_widths(ref, COARSE * rows, widths)
    put(carried, set_rows, rows, odd)
    if level > 0:
        put(carried, set_rows + detail_rows, rows, even)


def merge(level, depth, rows, swapped, *operands):
    set_rows = COARSE * rows + SUB
    detail_rows = (COARSE - 1) * rows
    if level == depth - 1:
        sizes = ((2 * COARSE - 1) * rows,) * 2
    else:
        sizes = (set_rows, set_rows + min(level + 1, 2) * detail_rows)
    return call(
        functools.partial(merge_kernel, level, depth, rows, swapped),
        tuple(jax.ShapeDtypeStruct((size, LANES), F32) for size in sizes),
        in_specs=[VMEM_SPEC] * len(operands),
        out_specs=(VMEM_SPEC,) * 2,
    )(*operands)


def in_outputs_order(part, tree, final, turned):
    species, group, width = tree.shape
    per = width // LANES
    for k in range(COARSE):
        for sp in range(species):
            turned[pl.ds(sp, per, stride=species)] = part[(k * species + sp) * per : (k * species + sp + 1) * per]
        for t in range(per):
            final[k, :, t * LANES : (t + 1) * LANES] = turned[t * species : (t + 1) * species]
    for sp in range(species):
        for i in range(group):
            at = ((COARSE + i) * species + sp) * per
            turned[pl.ds(i, per, stride=group)] = part[at : at + per]
        for t in range(per):
            tree[sp, :, t * LANES : (t + 1) * LANES] = turned[t * group : (t + 1) * group]


def finish_kernel(own_tree, own_final, other, tree, final, other_tree, other_final, turned, sems):
    core = lax.axis_index("slab") & 1
    width = own_tree.shape[2]

    def to(ref, source, block, sem):
        lanes = pl.ds(pl.multiple_of(block * width, LANES), width)
        copy = pltpu.make_async_copy(source, ref.at[:, :, lanes], sem)
        copy.start()
        return copy

    copies = [to(tree, own_tree, core, sems.at[0]), to(final, own_final, core, sems.at[1])]
    in_outputs_order(other, other_tree, other_final, turned)
    copies += [to(tree, other_tree, 1 - core, sems.at[2]), to(final, other_final, 1 - core, sems.at[3])]
    for copy in copies:
        copy.wait()


def finish(own, other, species, lines):
    half = lines // 2
    shapes = ((species, COARSE - 1, half), (COARSE, species, half))
    turned = pltpu.VMEM((half // LANES * SUB, LANES), F32)
    placed = call(
        in_outputs_order,
        tuple(jax.ShapeDtypeStruct(shape, F32) for shape in shapes),
        in_specs=[VMEM_SPEC],
        out_specs=(VMEM_SPEC,) * 2,
        scratch_shapes=[turned],
    )(own)
    return call(
        finish_kernel,
        tuple(jax.ShapeDtypeStruct(shape[:2] + (lines,), F32) for shape in shapes),
        in_specs=[VMEM_SPEC] * 3,
        out_specs=(HBM_SPEC,) * 2,
        scratch_shapes=[pltpu.VMEM(shape, F32) for shape in shapes] + [turned, pltpu.SemaphoreType.DMA((4,))],
    )(*placed, other)


def from_partner(block, axis, step):
    count = lax.axis_size(axis)
    return lax.ppermute(block, axis, [(i, i ^ step) for i in range(count)])


def shifted(block, axis):
    count = lax.axis_size(axis)
    return lax.ppermute(block, axis, [(i, i + 1) for i in range(count - 1)])


def exchanged(block, axis):
    species, rows, lines = block.shape
    count = lax.axis_size(axis)
    parts = block.reshape(species, rows, count, lines // count)
    return lax.all_to_all(parts, axis, split_axis=2, concat_axis=2, tiled=True).reshape(block.shape)


def last_routes(slabs):
    partner, own = [], []
    for s in range(slabs):
        for c in range(2):
            home = (s & 1) == c
            target = (s, c) if home else (s ^ 1, 1 - c)
            partner.append((s * 2 + c, (target[0] ^ (slabs // 2)) * 2 + target[1]))
            if not home:
                own.append((s * 2 + c, target[0] * 2 + target[1]))
    return partner, own


def on_device(sim_field, brick_edges, cell_width):
    species, _, lines = sim_field.shape
    cross_count = lax.axis_size("cross")
    slabs = lax.axis_size("slab")
    depth = slabs.bit_length() - 1
    width = lines // cross_count
    rows = species * (lines // 2) // LANES
    swapped = cross_count == 2
    both = ("slab", "cross")

    field = sim_field
    halo = shifted(brick_tail(brick_edges, field), "slab")
    if swapped:
        first_in = from_partner(first_rows(field, width), "cross", 1)
    factors, weights, coarse_width = tile_matrix(brick_edges, cell_width)
    part = brick_part(weights, coarse_width, field)
    halo, part, factors = lax.optimization_barrier((halo, part, factors))
    own_half, other_half = coarse_sets(weights, halo, part)
    halo, other_half = lax.optimization_barrier((halo, other_half))
    if swapped:
        rest = rest_away(brick_edges, halo, field, width)
        first_other = from_partner(other_half, "slab", 1)
        first_other, halo, rest = lax.optimization_barrier((first_other, halo, rest))
        rest_in = from_partner(rest, "cross", 1)

    if swapped:
        near = details(True, brick_edges, factors, halo, field, width, species, lines)
    send, carried = other_half, own_half
    for level in range(depth):
        last = level == depth - 1
        if swapped and level == depth - 2:
            send, near = lax.optimization_barrier((send, near))
        if swapped and last:
            partner_route, own_route = last_routes(slabs)
            operands = (carried, lax.ppermute(send, both, partner_route), lax.ppermute(carried, both, own_route))
            tile_detail = details(False, brick_edges, factors, first_in, rest_in, width, species, lines, near)
            operands, tile_detail = lax.optimization_barrier((operands, tile_detail))
        else:
            other = first_other if swapped and level == 0 else from_partner(send, "slab", 1 << level)
            operands = (carried, other)
        send, carried = merge(level, depth, rows, swapped, *operands)
    here_set, away_set = send, carried
    partner_set = from_partner(away_set, "slab", 1)

    if swapped:
        tree_detail, coarse_final = finish(here_set, partner_set, species, lines)
        coarse_final = coarse_final.transpose(1, 0, 2)
    else:
        core = lax.axis_index("slab") % 2
        first = jnp.where(core == 0, here_set, partner_set)
        second = jnp.where(core == 0, partner_set, here_set)
        ended = jnp.stack([first, second]).reshape(2, 2 * COARSE - 1, species, lines // 2)
        ended = ended.transpose(2, 1, 0, 3).reshape(species, 2 * COARSE - 1, lines)
        ended = exchanged(ended, "cross")
        coarse_final, tree_detail = ended[:, :COARSE], ended[:, COARSE:]
        moved = exchanged(jnp.concatenate([halo, sim_field[:, :HELD]], axis=1), "cross")
        tile_detail = details(True, brick_edges, factors, moved[:, :HALO], moved[:, HALO:], lines, species, lines)
    return (tile_detail.transpose(1, 0, 2), tree_detail, coarse_final)


def solution(mesh):
    placed = (P(None, "slab", "cross"), P("slab", None), P("slab"))
    return jax.shard_map(
        on_device,
        mesh=mesh,
        in_specs=placed,
        out_specs=(P(None, "slab", "cross"), P(None, "slab", "cross"), P(None, None, "cross")),
        check_vma=False,
    )
```
